256 devices in a mesh: bucket: 2 (over core), fsdp: 8 (over z), sp: 16 (over x, y).
Axes of the slice: x: 4, y: 4, z: 8, core: 2. Of those that a mesh axis runs over, the one named last changes fastest.
Arguments:
- hidden_states: bfloat16 [2, 8, 2048, 4096], P('bucket', 'fsdp', 'sp'), may hold values from -60 to 60
- norm_gain: float32 [4096], replicated, may hold values from 0.1 to 1.9
- w_query: bfloat16 [4096, 2048], P(('bucket', 'fsdp'), 'sp'), may hold values from -1 to 1
- w_key: bfloat16 [4096, 512], P(('bucket', 'fsdp'), 'sp'), may hold values from -2 to 2
- w_value: bfloat16 [4096, 512], P(('bucket', 'fsdp'), 'sp'), may hold values from -0.09375 to 0.09375
- out_grad: bfloat16 [2, 8, 2048, 2048], P('bucket', 'fsdp', None, 'sp'), may hold values from -6 to 6
- short_docs: int32 [8, 2048], P('fsdp'), may hold values from 0 to 127, never falling along the last dimension, each value on 1 to 128 neighbouring positions
Outputs:
- attended: bfloat16 [2, 8, 2048, 2048], P('bucket', 'fsdp', None, 'sp')
- grad_query: float32 [4096, 2048], P(('bucket', 'fsdp'), 'sp')
- grad_key: float32 [4096, 512], P(('bucket', 'fsdp'), 'sp')
- grad_value: float32 [4096, 512], P(('bucket', 'fsdp'), 'sp')
The draws below stay inside these ranges and needn't reach their ends.
All inputs are finite; a program needn't handle non-finite values.
Results may differ from the reference program's by a relative error of at most 0.029.
The reference program's roundings to bfloat16 on the way count: a program that leaves them out, or rounds other values in their place, can miss the bound.
Values may be sent and summed in bfloat16 or wider, within the bound.
A program may use at most 128 MiB of HBM per device.

```python
import math
import jax
import jax.numpy as jnp
import numpy as np
from jax import lax

D = 4096
HQ = 16
KVH = 4
DH = 128
SEQ_LEN = 2048
SEQS = 8


def draw_hidden_states(key, part):
    base_key, row_key, col_key = jax.random.split(key, 3)
    shape_all = (2, SEQS, SEQ_LEN, D)
    row_scales = jnp.exp(jax.random.uniform(row_key, (2, SEQS, SEQ_LEN, 1), jnp.float32, 0.0, math.log(10.0)))
    col_scales = jnp.exp(jax.random.uniform(col_key, (1, 1, 1, D), jnp.float32, 0.0, math.log(10.0)))
    base = jax.random.normal(base_key, shape_all, jnp.float32) * col_scales
    return jnp.clip(base * row_scales, -60.0, 60.0).astype(jnp.bfloat16)


def query_columns(key):
    normal_vals = jax.random.normal(jax.random.fold_in(key, 11), (D, HQ * DH), jnp.float32)
    return jnp.clip(normal_vals * D ** (-0.5), -1.0, 1.0)


def draw_w_query(key, part):
    return query_columns(key).astype(jnp.bfloat16)


def draw_w_key(key, part):
    noise_vals = jax.random.normal(jax.random.fold_in(key, 12), (D, KVH * DH), jnp.float32) * D ** (-0.5)
    return jnp.clip(noise_vals, -2.0, 2.0).astype(jnp.bfloat16)


def shard_levels(stream_key, dims, pieces, low, top_value):
    level = 1.0
    for dim, shards_of in pieces:
        heights = jax.random.uniform(jax.random.fold_in(jax.random.fold_in(stream_key, 6), dim), (shards_of,), jnp.float32, low / len(pieces), top_value / len(pieces))
        level = level * jnp.repeat(jnp.exp(heights), dims[dim] // shards_of).reshape((-1,) + (1,) * (len(dims) - 1 - dim))
    return level


def profile(count, total, bound, lean):
    loads = [(1 << 20) // math.isqrt(rank ** lean) + 1 for rank in range(2, count + 1)]
    surplus, counts = total - bound - (count - 1), [1] * (count - 1)
    while surplus > 0:
        candidates = [i for i in range(count - 1) if counts[i] < bound]
        pool, budget = sum([loads[i] for i in candidates]), surplus
        for i in candidates:
            more = min(bound - counts[i], max(1, budget * loads[i] // pool), surplus)
            counts[i] = counts[i] + more
            surplus = surplus - more
    return np.array([bound] + counts)


def uneven_parts(rng, amount, total, limit, skew):
    if amount == 2:
        one = jax.random.randint(rng, (), max(1, total - limit), min(limit, total - 1) + 1)
        return jnp.stack([one, total - one])
    lengths = jnp.asarray(profile(amount, total, limit, skew), jnp.int32)
    couples = (amount - 1) // 2
    source_of, taker = lengths[1:1 + 2 * couples:2], lengths[2:2 + 2 * couples:2]
    margin = jnp.minimum(source_of - 1, limit - taker)
    passed = jax.random.randint(jax.random.fold_in(rng, 1), (couples,), 0, 1 << 20) % (margin + 1)
    lengths = lengths.at[1:1 + 2 * couples:2].set(source_of - passed).at[2:2 + 2 * couples:2].set(taker + passed)
    return lengths[jax.random.permutation(jax.random.fold_in(rng, 2), amount)]


def scatter_about(stream_key, shape, scale, reach, pieces=(), kind=jnp.bfloat16):
    entries = scale * jax.random.normal(stream_key, shape, jnp.float32)
    if pieces:
        entries = entries * shard_levels(stream_key, shape, pieces, -0.22, 0.18)
    return jnp.clip(entries, -reach, reach).astype(kind)


def setup_inputs(seed: int = 0) -> dict:
    splits = jax.random.split(jax.random.key(seed), 8)
    return {
        "hidden_states": draw_hidden_states(jax.random.fold_in(splits[7], 71), 0),
        "norm_gain": jnp.clip(1.0 + 0.18 * jax.random.normal(splits[1], (D,), jnp.float32), 0.1, 1.9),
        "w_query": draw_w_query(jax.random.fold_in(splits[7], 71), 0),
        "w_key": draw_w_key(jax.random.fold_in(splits[7], 71), 0),
        "w_value": scatter_about(splits[4], (D, KVH * DH), D ** -0.5, 0.09375, ((0, 16), (1, 16))),
        "out_grad": scatter_about(splits[5], (2, SEQS, SEQ_LEN, HQ * DH), 1.0, 6.0, ((0, 2), (1, 8), (3, 16))),
        "short_docs": jax.vmap(lambda own: jnp.searchsorted(jnp.cumsum(uneven_parts(own, SEQ_LEN // 16, SEQ_LEN, min(128, SEQ_LEN // 4), 2)), jnp.arange(SEQ_LEN), side="right"))(jax.random.split(splits[6], SEQS)).reshape((SEQS, SEQ_LEN)).astype(jnp.int32),
    }


norm_eps = 1e-05
rope_base = 500000.0

def rotate_heads(values, sign_factor):
    length = values.shape[0]
    half_index = jnp.arange(DH // 2, dtype=jnp.float32)
    frequencies = rope_base ** (-2.0 * half_index / DH)
    angles = jnp.arange(length, dtype=jnp.float32)[:, None] * frequencies[None, :]
    cosine = jnp.cos(angles)[:, None, :]
    sine_vals = (sign_factor * jnp.sin(angles))[:, None, :]
    paired = values.reshape(values.shape[:-1] + (DH // 2, 2))
    even_part = paired[..., 0]
    odd_part = paired[..., 1]
    turned = jnp.stack([even_part * cosine - odd_part * sine_vals, even_part * sine_vals + odd_part * cosine], axis=-1)
    return turned.reshape(values.shape)

def row_pass(hidden_row, doc_row, grad_row, norm_gain, w_query, w_key, w_value):
    rows_wide = hidden_row.astype(jnp.float32)
    inv_rms = lax.rsqrt(lax.optimization_barrier(jnp.mean(rows_wide * rows_wide, axis=1, keepdims=True)) + norm_eps)
    normed = (rows_wide * inv_rms * norm_gain).astype(jnp.bfloat16)
    seq_len = normed.shape[0]
    queries = jnp.dot(normed, w_query, preferred_element_type=jnp.float32).reshape(seq_len, HQ, DH)
    keys_raw = jnp.dot(normed, w_key, preferred_element_type=jnp.float32).reshape(seq_len, KVH, DH)
    values_all = jnp.dot(normed, w_value, preferred_element_type=jnp.float32).astype(jnp.bfloat16).reshape(seq_len, KVH, DH)
    query_rot = rotate_heads(queries, 1.0).astype(jnp.bfloat16)
    key_rot = rotate_heads(keys_raw, 1.0).astype(jnp.bfloat16)
    grad_heads = grad_row.reshape(seq_len, HQ, DH)
    positions = jnp.arange(seq_len, dtype=jnp.int32)
    allowed = (positions[None, :] <= positions[:, None]) & (doc_row[:, None] == doc_row[None, :])
    score_scale = 1.0 / math.sqrt(DH)
    group_q = HQ // KVH

    def head_pass(head):
        kv_head = head // group_q
        q_head = lax.dynamic_index_in_dim(query_rot, head, 1, keepdims=False)
        k_head = lax.dynamic_index_in_dim(key_rot, kv_head, 1, keepdims=False)
        v_head = lax.dynamic_index_in_dim(values_all, kv_head, 1, keepdims=False)
        g_head = lax.dynamic_index_in_dim(grad_heads, head, 1, keepdims=False)
        scores = jnp.dot(q_head, k_head.T, preferred_element_type=jnp.float32) * score_scale
        scores = jnp.where(allowed, scores, -jnp.inf)
        row_max = lax.optimization_barrier(jnp.max(scores, axis=1, keepdims=True))
        exp_scores = jnp.exp(scores - row_max)
        probs = (exp_scores / lax.optimization_barrier(jnp.sum(exp_scores, axis=1, keepdims=True))).astype(jnp.bfloat16)
        out_head = jnp.dot(probs, v_head, preferred_element_type=jnp.float32).astype(jnp.bfloat16)
        dprobs = jnp.dot(g_head, v_head.T, preferred_element_type=jnp.float32)
        probs_wide = probs.astype(jnp.float32)
        row_dot = lax.optimization_barrier(jnp.sum(probs_wide * dprobs, axis=1, keepdims=True))
        dscores = (probs_wide * (dprobs - row_dot) * score_scale).astype(jnp.bfloat16)
        dq_head = jnp.dot(dscores, k_head, preferred_element_type=jnp.float32)
        dk_head = jnp.dot(dscores.T, q_head, preferred_element_type=jnp.float32)
        dv_head = jnp.dot(probs.T, g_head, preferred_element_type=jnp.float32)
        return (out_head, dq_head, dk_head, dv_head)
    out_heads, dq_heads, dk_heads, dv_heads = lax.map(head_pass, jnp.arange(HQ, dtype=jnp.int32))
    attended = jnp.transpose(out_heads, (1, 0, 2)).reshape(seq_len, HQ * DH)
    dquery = rotate_heads(jnp.transpose(dq_heads, (1, 0, 2)), -1.0).astype(jnp.bfloat16).reshape(seq_len, HQ * DH)
    dkey_sum = lax.optimization_barrier(jnp.sum(dk_heads.reshape(KVH, group_q, seq_len, DH), axis=1))
    dkey = rotate_heads(jnp.transpose(dkey_sum, (1, 0, 2)), -1.0).astype(jnp.bfloat16).reshape(seq_len, KVH * DH)
    dvalue_sum = lax.optimization_barrier(jnp.sum(dv_heads.reshape(KVH, group_q, seq_len, DH), axis=1))
    dvalue = jnp.transpose(dvalue_sum, (1, 0, 2)).astype(jnp.bfloat16).reshape(seq_len, KVH * DH)
    part_query = jnp.dot(normed.T, dquery, preferred_element_type=jnp.float32).astype(jnp.bfloat16)
    part_key = jnp.dot(normed.T, dkey, preferred_element_type=jnp.float32).astype(jnp.bfloat16)
    part_value = jnp.dot(normed.T, dvalue, preferred_element_type=jnp.float32).astype(jnp.bfloat16)
    return (attended, part_query, part_key, part_value)

def reference(hidden_states, norm_gain, w_query, w_key, w_value, out_grad, short_docs):
    row_total = 2 * SEQS
    hidden_rows = hidden_states.reshape(row_total, SEQ_LEN, D)
    grad_rows = out_grad.reshape(row_total, SEQ_LEN, HQ * DH)
    doc_rows = jnp.concatenate([jnp.zeros_like(short_docs), short_docs], axis=0)

    def scan_step(totals, inputs):
        hidden_row, doc_row, grad_row = inputs
        attended, part_query, part_key, part_value = row_pass(hidden_row, doc_row, grad_row, norm_gain, w_query, w_key, w_value)
        new_totals = (totals[0] + part_query.astype(jnp.float32), totals[1] + part_key.astype(jnp.float32), totals[2] + part_value.astype(jnp.float32))
        return (new_totals, attended)
    start_totals = (jnp.zeros((D, HQ * DH), jnp.float32), jnp.zeros((D, KVH * DH), jnp.float32), jnp.zeros((D, KVH * DH), jnp.float32))
    totals, attended_rows = lax.scan(scan_step, start_totals, (hidden_rows, doc_rows, grad_rows))
    return (attended_rows.reshape(2, SEQS, SEQ_LEN, HQ * DH), totals[0], totals[1], totals[2])
```

```python
import math
import functools
import numpy as np
import jax
import jax.numpy as jnp
from jax import lax
from jax.experimental import pallas as pl
from jax.experimental.pallas import tpu as pltpu
from jax.sharding import PartitionSpec as P

DH = 128
SEQ = 2048
QB = 256
KB = 256
NEG = -1e30
SCALE = 1.0 / math.sqrt(DH)
EXP_C = SCALE * math.log2(math.e)


def rope_tables():
    freq = np.float32(500000.0) ** (-2.0 * np.arange(64, dtype=np.float32) / DH)
    freq = np.repeat(freq.astype(np.float64), 2)[None, :]
    sign = np.where(np.arange(DH) % 2 == 0, -1.0, 1.0)[None, :]
    fine = np.arange(128)[:, None] * freq
    coarse = 128 * np.arange(16)[:, None] * freq
    f = np.stack([np.cos(fine), np.sin(fine) * sign]).astype(np.float32)
    c = np.stack([np.cos(coarse), np.sin(coarse) * sign]).astype(np.float32)
    return f, c


def rope_block(fine_ref, coarse_ref, block):
    cf, sf = fine_ref[0], fine_ref[1]
    cc = coarse_ref[0, pl.ds(block, 1), :]
    sc = coarse_ref[1, pl.ds(block, 1), :]
    return cf * cc - sf * sc, sf * cc + cf * sc


def swap_pairs(x):
    lane = lax.broadcasted_iota(jnp.int32, x.shape, 1)
    return jnp.where(lane % 2 == 0, pltpu.roll(x, DH - 1, 1), pltpu.roll(x, 1, 1))


def nn(a, b):
    return jnp.dot(a, b, preferred_element_type=jnp.float32)


def nt(a, b):
    return lax.dot_general(a, b, (((1,), (1,)), ((), ())), preferred_element_type=jnp.float32)


def attention_kernel(q_ref, k_ref, v_ref, g_ref, docs_row, docs_col, fine_ref, coarse_ref,
                     att_ref, dq_ref, dk_ref, dv_ref,
                     kt, vt, s_scr, p_scr, acc, dk_acc, dv_acc):
    bucket = lax.axis_index("bucket")

    @pl.loop(0, SEQ // KB)
    def _(j):
        rows = pl.ds(pl.multiple_of(j * KB, KB), KB)
        kt[j] = k_ref[rows, :].T
        vt[j] = v_ref[rows, :].T

    dk_acc[...] = jnp.zeros_like(dk_acc)
    dv_acc[...] = jnp.zeros_like(dv_acc)

    def finish_query(i, dqt):
        dq = dqt.T * SCALE
        for half in range(QB // 128):
            block = i * (QB // 128) + half
            cos, sin = rope_block(fine_ref, coarse_ref, block)
            x = dq[half * 128:(half + 1) * 128]
            dq_ref[pl.ds(pl.multiple_of(block * 128, 128), 128), :] = (
                x * cos - swap_pairs(x) * sin).astype(jnp.bfloat16)

    @pl.when(bucket == 0)
    def _():
        @pl.loop(0, SEQ // QB)
        def _(i):
            qrows = pl.ds(pl.multiple_of(i * QB, QB), QB)
            q = q_ref[qrows, :]
            g = g_ref[qrows, :]

            def scores(j):
                return nt(k_ref[pl.ds(pl.multiple_of(j * KB, KB), KB), :], q)

            def pass1(j, m):
                s = scores(j)
                s_scr[j] = s
                return jnp.maximum(m, jnp.max(s.reshape(KB // 8, 8, QB), axis=0))

            m8 = lax.fori_loop(0, i, pass1, jnp.full((8, QB), NEG, jnp.float32))
            s = scores(i)
            key = lax.broadcasted_iota(jnp.int32, (KB, QB), 0)
            qry = lax.broadcasted_iota(jnp.int32, (KB, QB), 1)
            s = jnp.where(key <= qry, s, NEG)
            s_scr[i] = s
            m8 = jnp.maximum(m8, jnp.max(s.reshape(KB // 8, 8, QB), axis=0))
            m = jnp.max(m8, axis=0, keepdims=True)
            acc[...] = jnp.zeros_like(acc)

            def pass2(j, l8):
                p = jnp.exp2((s_scr[j] - m) * EXP_C)
                pb = p.astype(jnp.bfloat16)
                p_scr[j] = pb
                acc[...] += nn(vt[j], pb)
                return l8 + jnp.sum(p.reshape(KB // 8, 8, QB), axis=0)

            l8 = lax.fori_loop(0, i + 1, pass2, jnp.zeros((8, QB), jnp.float32))
            rl = 1.0 / jnp.sum(l8, axis=0, keepdims=True)
            ot = acc[...] * rl
            att_ref[qrows, :] = ot.T.astype(jnp.bfloat16)
            gt = (g.astype(jnp.float32).T * rl).astype(jnp.bfloat16)
            gs = gt.T
            d = jnp.sum(ot * gt.astype(jnp.float32), axis=0, keepdims=True)
            acc[...] = jnp.zeros_like(acc)

            @pl.loop(0, i + 1)
            def _(j):
                krows = pl.ds(pl.multiple_of(j * KB, KB), KB)
                pb = p_scr[j]
                dp = nn(v_ref[krows, :], gt)
                ds = (pb.astype(jnp.float32) * (dp - d)).astype(jnp.bfloat16)
                acc[...] += nn(kt[j], ds)
                dk_acc[krows, :] += nn(ds, q)
                dv_acc[krows, :] += nn(pb, gs)

            finish_query(i, acc[...])

    @pl.when(bucket == 1)
    def _():
        span = QB + 128

        @pl.loop(0, SEQ // QB)
        def _(i):
            qrows = pl.ds(pl.multiple_of(i * QB, QB), QB)
            first = pl.multiple_of(jnp.maximum(i * QB - 128, 0), 128)
            krows = pl.ds(first, span)
            q = q_ref[qrows, :]
            g = g_ref[qrows, :]
            k = k_ref[krows, :]
            v = v_ref[krows, :]
            key = lax.broadcasted_iota(jnp.int32, (span, QB), 0) + first
            qry = lax.broadcasted_iota(jnp.int32, (span, QB), 1) + i * QB
            same = docs_col[krows, :] == docs_row[i]
            s = jnp.where((key <= qry) & same, nt(k, q), NEG)
            m = jnp.max(s, axis=0, keepdims=True)
            p = jnp.exp2((s - m) * EXP_C)
            rl = 1.0 / jnp.sum(p, axis=0, keepdims=True)
            pb = p.astype(jnp.bfloat16)
            ot = nn(v.T, pb) * rl
            att_ref[qrows, :] = ot.T.astype(jnp.bfloat16)
            gt = (g.astype(jnp.float32).T * rl).astype(jnp.bfloat16)
            gs = gt.T
            d = jnp.sum(ot * gt.astype(jnp.float32), axis=0, keepdims=True)
            dp = nn(v, gt)
            ds = (pb.astype(jnp.float32) * (dp - d)).astype(jnp.bfloat16)
            finish_query(i, nn(k.T, ds))
            dk_acc[krows, :] += nn(ds, q)
            dv_acc[krows, :] += nn(pb, gs)

    dk_ref[...] = (dk_acc[...] * SCALE).astype(jnp.bfloat16)
    dv_ref[...] = dv_acc[...].astype(jnp.bfloat16)


def attention(q, k, v, g, docs):
    fine, coarse = rope_tables()
    nb = SEQ // KB
    vmem = pl.BlockSpec(memory_space=pltpu.VMEM)
    out = jax.ShapeDtypeStruct((SEQ, DH), jnp.bfloat16)
    return pl.pallas_call(
        attention_kernel,
        out_shape=(out, out, out, out),
        in_specs=[vmem] * 8,
        out_specs=(vmem,) * 4,
        scratch_shapes=[
            pltpu.VMEM((nb, DH, KB), jnp.bfloat16),
            pltpu.VMEM((nb, DH, KB), jnp.bfloat16),
            pltpu.VMEM((nb, KB, QB), jnp.float32),
            pltpu.VMEM((nb, KB, QB), jnp.bfloat16),
            pltpu.VMEM((DH, QB), jnp.float32),
            pltpu.VMEM((SEQ, DH), jnp.float32),
            pltpu.VMEM((SEQ, DH), jnp.float32),
        ],
        compiler_params=pltpu.CompilerParams(vmem_limit_bytes=40 << 20),
        name="attention",
    )(q, k, v, g, docs.reshape(SEQ // QB, 1, QB), docs.reshape(SEQ, 1), jnp.asarray(fine), jnp.asarray(coarse))


HQ = 16
KVH = 4


norm_eps = 1e-05
rope_base = 500000.0


def swapped(value, axis, stride):
    mask = 2**stride
    pairs = [(source, source ^ mask) for source in range(lax.axis_size(axis))]
    return lax.ppermute(value, axis, pairs)


def pair_rotate(values, first_col, sign_factor):
    length, column_total = values.shape
    pair_index = (first_col + 2 * jnp.arange(column_total // 2, dtype=jnp.int32)) % DH // 2
    frequencies = rope_base ** (-2.0 * pair_index.astype(jnp.float32) / DH)
    angles = jnp.arange(length, dtype=jnp.float32)[:, None] * frequencies[None, :]
    cosine = jnp.cos(angles)
    sine_vals = sign_factor * jnp.sin(angles)
    paired = values.reshape(length, column_total // 2, 2)
    even_part = paired[:, :, 0]
    odd_part = paired[:, :, 1]
    turned = jnp.stack(
        [even_part * cosine - odd_part * sine_vals, even_part * sine_vals + odd_part * cosine],
        axis=2,
    )
    return turned.reshape(length, column_total)


def local(hidden_states, norm_gain, w_query, w_key, w_value, out_grad, short_docs):
    tok_rows = hidden_states.shape[2]
    features = hidden_states.shape[3]
    sp_count = lax.axis_size("sp")
    sp_index = lax.axis_index("sp")
    bucket_index = lax.axis_index("bucket")
    local_rows = hidden_states.reshape(tok_rows, features).astype(jnp.float32)
    inv_rms = lax.rsqrt(jnp.mean(local_rows * local_rows, axis=1, keepdims=True) + norm_eps)
    normed_local = (local_rows * inv_rms * norm_gain).astype(jnp.bfloat16)
    normed = lax.all_gather(normed_local, "sp", axis=0, tiled=True)
    seq_len = normed.shape[0]
    q_cols = w_query.shape[1]
    kv_cols = w_key.shape[1]
    pieces = (
        lax.all_gather(w_query, ("bucket", "fsdp"), axis=0, tiled=True),
        lax.all_gather(w_key, ("bucket", "fsdp"), axis=0, tiled=True),
        lax.all_gather(w_value, ("bucket", "fsdp"), axis=0, tiled=True),
    )
    columns = normed
    queries, key_part, value_part = tuple(
        (jnp.dot(columns, piece, preferred_element_type=jnp.float32) for piece in pieces)
    )
    kv_first = sp_index * kv_cols
    query_rot = pair_rotate(queries, 0, 1.0).astype(jnp.bfloat16)
    key_rot = pair_rotate(key_part, kv_first, 1.0).astype(jnp.bfloat16)
    value_own = value_part.astype(jnp.bfloat16)
    heads_dev = q_cols // DH
    group_q = HQ // KVH
    kv_heads_dev = max(1, heads_dev // group_q)
    spread = max(1, sp_count // KVH)
    bit_levels = spread.bit_length() - 1
    key_use = key_rot
    value_use = value_own
    for bit_level in range(bit_levels):
        other_key, other_value = swapped((key_use, value_use), "sp", bit_level)
        upper_half = sp_index // 2**bit_level % 2 == 1
        key_use = jnp.where(
            upper_half,
            jnp.concatenate([other_key, key_use], 1),
            jnp.concatenate([key_use, other_key], 1),
        )
        value_use = jnp.where(
            upper_half,
            jnp.concatenate([other_value, value_use], 1),
            jnp.concatenate([value_use, other_value], 1),
        )
    doc_ids = jnp.where(bucket_index == 0, 0, short_docs[0])
    attended, dquery, dkey_sum, dvalue_sum = attention(query_rot, key_use, value_use, out_grad.reshape(seq_len, q_cols), doc_ids)
    attended = attended.reshape(1, 1, seq_len, q_cols)
    dkey_sum = dkey_sum.astype(jnp.float32)
    dvalue_sum = dvalue_sum.astype(jnp.float32)
    dkey_full = dkey_sum
    dvalue_full = dvalue_sum
    for bit_level in range(bit_levels):
        got_key, got_value = (
            swapped(dkey_full.astype(jnp.bfloat16), "sp", bit_level).astype(dkey_full.dtype),
            swapped(dvalue_full.astype(jnp.bfloat16), "sp", bit_level).astype(dvalue_full.dtype),
        )
        dkey_full = dkey_full + got_key
        dvalue_full = dvalue_full + got_value
    own_start = sp_index % spread * kv_cols
    dkey_cur = lax.dynamic_slice_in_dim(dkey_full, own_start, kv_cols, 1)
    dvalue_cur = lax.dynamic_slice_in_dim(dvalue_full, own_start, kv_cols, 1)
    dkey = pair_rotate(dkey_cur, kv_first, -1.0).astype(jnp.bfloat16)
    dvalue = dvalue_cur.astype(jnp.bfloat16)
    grads_joined = jnp.concatenate([dquery, dkey, dvalue], axis=1)
    columns = normed
    summed = lax.psum_scatter(
        jnp.einsum("tc,tg->cg", columns, grads_joined, preferred_element_type=jnp.float32).astype(
            jnp.bfloat16
        ),
        ("bucket", "fsdp"),
        scatter_dimension=0,
        tiled=True,
    ).astype(jnp.float32)
    return (
        attended,
        summed[:, :q_cols],
        summed[:, q_cols : q_cols + kv_cols],
        summed[:, q_cols + kv_cols :],
    )


def solution(mesh):
    return jax.shard_map(
        local,
        mesh=mesh,
        in_specs=(
            P("bucket", "fsdp", "sp", None),
            P(),
            P(("bucket", "fsdp"), "sp"),
            P(("bucket", "fsdp"), "sp"),
            P(("bucket", "fsdp"), "sp"),
            P("bucket", "fsdp", None, "sp"),
            P("fsdp", None),
        ),
        out_specs=(
            P("bucket", "fsdp", None, "sp"),
            P(("bucket", "fsdp"), "sp"),
            P(("bucket", "fsdp"), "sp"),
            P(("bucket", "fsdp"), "sp"),
        ),
        check_vma=False,
    )
```

```python
import math
import functools
import numpy as np
import jax
import jax.numpy as jnp
from jax import lax
from jax.experimental import pallas as pl
from jax.experimental.pallas import tpu as pltpu
from jax.sharding import PartitionSpec as P

MESH = pl.DeviceIdType.MESH

DH = 128
SEQ = 2048
QB = 256
KB = 256
NEG = -1e30
SCALE = 1.0 / math.sqrt(DH)
EXP_C = SCALE * math.log2(math.e)


def rope_tables():
    freq = np.float32(500000.0) ** (-2.0 * np.arange(64, dtype=np.float32) / DH)
    freq = np.repeat(freq.astype(np.float64), 2)[None, :]
    sign = np.where(np.arange(DH) % 2 == 0, -1.0, 1.0)[None, :]
    fine = np.arange(128)[:, None] * freq
    coarse = 128 * np.arange(16)[:, None] * freq
    f = np.stack([np.cos(fine), np.sin(fine) * sign]).astype(np.float32)
    c = np.stack([np.cos(coarse), np.sin(coarse) * sign]).astype(np.float32)
    return f, c


def rope_block(fine_ref, coarse_ref, block):
    cf, sf = fine_ref[0], fine_ref[1]
    cc = coarse_ref[0, pl.ds(block, 1), :]
    sc = coarse_ref[1, pl.ds(block, 1), :]
    return cf * cc - sf * sc, sf * cc + cf * sc


def swap_pairs(x):
    lane = lax.broadcasted_iota(jnp.int32, x.shape, 1)
    return jnp.where(lane % 2 == 0, pltpu.roll(x, DH - 1, 1), pltpu.roll(x, 1, 1))


def nn(a, b):
    return jnp.dot(a, b, preferred_element_type=jnp.float32)


def nt(a, b):
    return lax.dot_general(a, b, (((1,), (1,)), ((), ())), preferred_element_type=jnp.float32)


def attention_kernel(qkv_ref, g_ref, docs_row, docs_col, fine_ref, coarse_ref,
                     att_ref, d_ref,
                     kt, vt, s_scr, p_scr, acc, dk_acc, dv_acc):
    bucket = lax.axis_index("bucket")
    q_ref, k_ref, v_ref = (qkv_ref.at[:, pl.ds(part * DH, DH)] for part in range(3))
    dq_ref, dk_ref, dv_ref = (d_ref.at[:, pl.ds(part * DH, DH)] for part in range(3))

    @pl.loop(0, SEQ // KB)
    def _(j):
        rows = pl.ds(pl.multiple_of(j * KB, KB), KB)
        kt[j] = k_ref[rows, :].T
        vt[j] = v_ref[rows, :].T

    dk_acc[...] = jnp.zeros_like(dk_acc)
    dv_acc[...] = jnp.zeros_like(dv_acc)

    def finish_query(i, dqt):
        dq = dqt.T * SCALE
        for half in range(QB // 128):
            block = i * (QB // 128) + half
            cos, sin = rope_block(fine_ref, coarse_ref, block)
            x = dq[half * 128:(half + 1) * 128]
            dq_ref[pl.ds(pl.multiple_of(block * 128, 128), 128), :] = (
                x * cos - swap_pairs(x) * sin).astype(jnp.bfloat16)

    @pl.when(bucket == 0)
    def _():
        @pl.loop(0, SEQ // QB)
        def _(i):
            qrows = pl.ds(pl.multiple_of(i * QB, QB), QB)
            q = q_ref[qrows, :]
            g = g_ref[qrows, :]

            def scores(j):
                return nt(k_ref[pl.ds(pl.multiple_of(j * KB, KB), KB), :], q)

            def pass1(j, m):
                s = scores(j)
                s_scr[j] = s
                return jnp.maximum(m, jnp.max(s.reshape(KB // 8, 8, QB), axis=0))

            m8 = lax.fori_loop(0, i, pass1, jnp.full((8, QB), NEG, jnp.float32))
            s = scores(i)
            key = lax.broadcasted_iota(jnp.int32, (KB, QB), 0)
            qry = lax.broadcasted_iota(jnp.int32, (KB, QB), 1)
            s = jnp.where(key <= qry, s, NEG)
            s_scr[i] = s
            m8 = jnp.maximum(m8, jnp.max(s.reshape(KB // 8, 8, QB), axis=0))
            m = jnp.max(m8, axis=0, keepdims=True)
            acc[...] = jnp.zeros_like(acc)

            def pass2(j, l8):
                p = jnp.exp2((s_scr[j] - m) * EXP_C)
                pb = p.astype(jnp.bfloat16)
                p_scr[j] = pb
                acc[...] += nn(vt[j], pb)
                return l8 + jnp.sum(p.reshape(KB // 8, 8, QB), axis=0)

            l8 = lax.fori_loop(0, i + 1, pass2, jnp.zeros((8, QB), jnp.float32))
            rl = 1.0 / jnp.sum(l8, axis=0, keepdims=True)
            ot = acc[...] * rl
            att_ref[qrows, :] = ot.T.astype(jnp.bfloat16)
            gt = (g.astype(jnp.float32).T * rl).astype(jnp.bfloat16)
            gs = gt.T
            d = jnp.sum(ot * gt.astype(jnp.float32), axis=0, keepdims=True)
            acc[...] = jnp.zeros_like(acc)

            @pl.loop(0, i + 1)
            def _(j):
                krows = pl.ds(pl.multiple_of(j * KB, KB), KB)
                pb = p_scr[j]
                dp = nn(v_ref[krows, :], gt)
                ds = (pb.astype(jnp.float32) * (dp - d)).astype(jnp.bfloat16)
                acc[...] += nn(kt[j], ds)
                dk_acc[krows, :] += nn(ds, q)
                dv_acc[krows, :] += nn(pb, gs)

            finish_query(i, acc[...])

    @pl.when(bucket == 1)
    def _():
        span = QB + 128

        @pl.loop(0, SEQ // QB)
        def _(i):
            qrows = pl.ds(pl.multiple_of(i * QB, QB), QB)
            first = pl.multiple_of(jnp.maximum(i * QB - 128, 0), 128)
            krows = pl.ds(first, span)
            q = q_ref[qrows, :]
            g = g_ref[qrows, :]
            k = k_ref[krows, :]
            v = v_ref[krows, :]
            key = lax.broadcasted_iota(jnp.int32, (span, QB), 0) + first
            qry = lax.broadcasted_iota(jnp.int32, (span, QB), 1) + i * QB
            same = docs_col[krows, :] == docs_row[i]
            s = jnp.where((key <= qry) & same, nt(k, q), NEG)
            m = jnp.max(s, axis=0, keepdims=True)
            p = jnp.exp2((s - m) * EXP_C)
            rl = 1.0 / jnp.sum(p, axis=0, keepdims=True)
            pb = p.astype(jnp.bfloat16)
            ot = nn(v.T, pb) * rl
            att_ref[qrows, :] = ot.T.astype(jnp.bfloat16)
            gt = (g.astype(jnp.float32).T * rl).astype(jnp.bfloat16)
            gs = gt.T
            d = jnp.sum(ot * gt.astype(jnp.float32), axis=0, keepdims=True)
            dp = nn(v, gt)
            ds = (pb.astype(jnp.float32) * (dp - d)).astype(jnp.bfloat16)
            finish_query(i, nn(k.T, ds))
            dk_acc[krows, :] += nn(ds, q)
            dv_acc[krows, :] += nn(pb, gs)

    dk_ref[...] = (dk_acc[...] * SCALE).astype(jnp.bfloat16)
    dv_ref[...] = dv_acc[...].astype(jnp.bfloat16)


def attention(qkv, g, docs, fine, coarse):
    nb = SEQ // KB
    vmem = pl.BlockSpec(memory_space=pltpu.VMEM)
    return pl.pallas_call(
        attention_kernel,
        out_shape=(jax.ShapeDtypeStruct((SEQ, DH), jnp.bfloat16), jax.ShapeDtypeStruct((SEQ, 3 * DH), jnp.bfloat16)),
        in_specs=[vmem] * 6,
        out_specs=(vmem,) * 2,
        scratch_shapes=[
            pltpu.VMEM((nb, DH, KB), jnp.bfloat16),
            pltpu.VMEM((nb, DH, KB), jnp.bfloat16),
            pltpu.VMEM((nb, KB, QB), jnp.float32),
            pltpu.VMEM((nb, KB, QB), jnp.bfloat16),
            pltpu.VMEM((DH, QB), jnp.float32),
            pltpu.VMEM((SEQ, DH), jnp.float32),
            pltpu.VMEM((SEQ, DH), jnp.float32),
        ],
        compiler_params=pltpu.CompilerParams(vmem_limit_bytes=40 << 20),
        name="attention",
    )(qkv, g, docs.reshape(SEQ // QB, 1, QB), docs.reshape(SEQ, 1), fine, coarse)


D = 4096
TB = 128
WR = 192
WF = 256
EPS = 1e-5


class Copies:
    def __init__(self, send, recv):
        self.send, self.recv, self.ids, self.live = send, recv, {}, []

    def make(self, key, src, dst, dev):
        i = self.ids.setdefault(key, len(self.ids))
        return pltpu.make_async_remote_copy(src_ref=src, dst_ref=dst, send_sem=self.send.at[i], recv_sem=self.recv.at[i],
                                            device_id=dev, device_id_type=MESH)

    def start(self, key, src, dst, dev):
        copy = self.make(key, src, dst, dev)
        copy.start()
        self.live.append(copy)

    def arrive(self, key, dst, dev):
        self.make(key, dst, dst, dev).wait_recv()

    def drain(self):
        for copy in self.live:
            copy.wait_send()


def place():
    c, z, sp = lax.axis_index("bucket"), lax.axis_index("fsdp"), lax.axis_index("sp")
    return c, z, sp // 4, sp % 4


def greet(devs):
    barrier = pltpu.get_barrier_semaphore()
    for dev in devs:
        pl.semaphore_signal(barrier, inc=1, device_id=dev, device_id_type=MESH)
    return lambda: pl.semaphore_wait(barrier, len(devs))


FRONT_SEMS = 7 + 32 + 32 + 12 + 12


def front_kernel(h_ref, gain_ref, w_ref, fine_ref, coarse_ref, n_ref, qkv_ref, wbuf, acc, stage, ssem, rsem):
    c, z, x, y = place()
    xdev = lambda d: {"sp": (x + d) % 4 * 4 + y}
    ydev = lambda d: {"sp": x * 4 + (y + d) % 4}
    zdev = lambda d: {"fsdp": (z + d) % 8}
    other = {"bucket": 1 - c}
    wait_all = greet([xdev(1), xdev(3), ydev(1), ydev(2), ydev(3), zdev(1), zdev(7), other])

    def wslot(core, zz, yy, lo=0, size=WR):
        col = pl.multiple_of((core * 8 + zz % 8) * WF, WF)
        return wbuf.at[yy % 4, pl.ds(lo, size), pl.ds(col, WF)]

    for r in range(0, TB, 32):
        rows = h_ref[r:r + 32, :].astype(jnp.float32)
        inv = lax.rsqrt(jnp.mean(rows * rows, axis=1, keepdims=True) + EPS)
        n_ref[x, r:r + 32, :] = (rows * inv * gain_ref[...]).astype(jnp.bfloat16)
    wslot(c, z, y)[...] = w_ref[...]
    wait_all()

    cp = Copies(ssem, rsem)
    zoff = [0, -1, -2, -3, -4, 1, 2, 3]

    def spread(zi):
        src = w_ref if zi == 0 else wslot(c, z + zoff[zi], y)
        dst = wslot(c, z + zoff[zi], y)
        cp.start(("yr", zi), src, dst, ydev(1))
        cp.start(("yl", zi), src, dst, ydev(3))
        cp.start(("c", zi, 0), src, dst, other)

    def serve(zi):
        zz = z + zoff[zi]
        cp.arrive(("yr", zi), wslot(c, zz, y + 3), ydev(1))
        half = wslot(c, zz, y + 3, 0, WR // 2)
        cp.start(("ya", zi), half, half, ydev(1))
        cp.start(("c", zi, 1), wslot(c, zz, y + 3), wslot(c, zz, y + 3), other)
        cp.arrive(("yl", zi), wslot(c, zz, y + 1), ydev(3))
        half = wslot(c, zz, y + 1, WR // 2, WR // 2)
        cp.start(("yb", zi), half, half, ydev(3))
        cp.start(("c", zi, 2), wslot(c, zz, y + 1), wslot(c, zz, y + 1), other)

    def last(zi):
        zz = z + zoff[zi]
        cp.arrive(("ya", zi), wslot(c, zz, y + 2, 0, WR // 2), ydev(1))
        cp.arrive(("yb", zi), wslot(c, zz, y + 2, WR // 2, WR // 2), ydev(3))
        cp.start(("c", zi, 3), wslot(c, zz, y + 2), wslot(c, zz, y + 2), other)

    def npiece(xx, p):
        return n_ref.at[xx % 4, pl.ds(p * 32, 32), :]

    cp.start(("zr", 1), w_ref, wslot(c, z, y), zdev(1))
    cp.start(("zl", 1), w_ref, wslot(c, z, y), zdev(7))
    spread(0)
    for p in range(4):
        cp.start(("xr", p), npiece(x, p), npiece(x, p), xdev(1))
        cp.start(("xl", 3 - p), npiece(x, 3 - p), npiece(x, 3 - p), xdev(3))

    def relay_x(p):
        cp.arrive(("xr", p), npiece(x + 3, p), xdev(1))
        cp.start(("xa", p), npiece(x + 3, p), npiece(x + 3, p), xdev(1))
        cp.arrive(("xl", 3 - p), npiece(x + 1, 3 - p), xdev(3))
        cp.start(("xb", 3 - p), npiece(x + 1, 3 - p), npiece(x + 1, 3 - p), xdev(3))

    done, waiting = [0], []
    for step in range(1, 5):
        src = wslot(c, z - step, y)
        cp.arrive(("zr", step), src, zdev(1))
        if step < 4:
            cp.start(("zr", step + 1), src, src, zdev(1))
        spread(step)
        fresh = [step]
        if step < 4:
            src = wslot(c, z + step, y)
            cp.arrive(("zl", step), src, zdev(7))
            if step < 3:
                cp.start(("zl", step + 1), src, src, zdev(7))
            spread(4 + step)
            fresh.append(4 + step)
        for zi in done:
            serve(zi)
        for zi in waiting:
            last(zi)
        waiting, done = done, fresh
        if step == 3:
            relay_x(0)
            relay_x(1)
    for zi in done:
        serve(zi)
    for zi in waiting + done:
        last(zi)
    for zi in range(8):
        for yk, dy in enumerate((0, 3, 1, 2)):
            cp.arrive(("c", zi, yk), wslot(1 - c, z + zoff[zi], y + dy), other)
    for p in (2, 3):
        cp.arrive(("xr", p), npiece(x + 3, p), xdev(1))
        cp.arrive(("xl", 3 - p), npiece(x + 1, 3 - p), xdev(3))

    lane = lax.broadcasted_iota(jnp.int32, (TB, DH), 1)

    def project(offsets, first):
        rows = len(offsets) * TB
        acc[0:rows, :] = jnp.zeros((rows, 6 * DH), jnp.float32)

        @pl.loop(0, D // 512)
        def _(f):
            cols = pl.ds(pl.multiple_of(f * 512, 512), 512)
            lhs = jnp.concatenate([n_ref[(x + d) % 4, :, cols] for d in offsets], axis=0)
            rhs = jnp.concatenate([wbuf[yy, 0:DH, cols] for yy in range(4)] + [wbuf[yy, DH:WR, cols] for yy in range(4)], axis=0)
            acc[0:rows, :] += nt(lhs, rhs)

        for n, d in enumerate(offsets):
            i = first + n
            xx = (x + d) % 4
            r = pl.ds(n * TB, TB)
            cos, sin = rope_block(fine_ref, coarse_ref, 4 * xx + y)
            turn = lambda t: (t * cos + swap_pairs(t) * sin).astype(jnp.bfloat16)
            a, b = acc[r, 4 * DH:5 * DH], acc[r, 5 * DH:6 * DH]
            pick = lambda p0, p1, p2, p3: jnp.where(lane < 32, p0, jnp.where(lane < 64, p1, jnp.where(lane < 96, p2, p3)))
            key = turn(pick(a, pltpu.roll(a, 96, 1), pltpu.roll(b, 64, 1), pltpu.roll(b, 32, 1)))
            val = pick(pltpu.roll(a, 96, 1), pltpu.roll(a, 64, 1), pltpu.roll(b, 32, 1), b).astype(jnp.bfloat16)
            for dy in range(4):
                q = turn(acc[r, pl.ds(pl.multiple_of((y + dy) % 4 * DH, DH), DH)])
                dst = qkv_ref.at[xx, y] if dy == 0 else stage.at[i, dy - 1]
                dst[:, 0:DH] = q
                dst[:, DH:2 * DH] = key
                dst[:, 2 * DH:3 * DH] = val
            for dy in (2, 1, 3):
                cp.start(("q", i, dy), stage.at[i, dy - 1], qkv_ref.at[xx, y], ydev(dy))

    project((0, 3, 1), 0)
    for p in (0, 1):
        cp.arrive(("xa", p), npiece(x + 2, p), xdev(1))
        cp.arrive(("xb", 3 - p), npiece(x + 2, 3 - p), xdev(3))
    project((2,), 3)
    for i, d in enumerate((0, 3, 1, 2)):
        for dy in range(1, 4):
            cp.arrive(("q", i, dy), qkv_ref.at[(x + d) % 4, (y - dy) % 4], ydev(dy))
    cp.drain()


def front(h, gain, w, fine, coarse):
    vmem = pl.BlockSpec(memory_space=pltpu.VMEM)
    return pl.pallas_call(
        front_kernel,
        out_shape=(jax.ShapeDtypeStruct((4, TB, D), jnp.bfloat16), jax.ShapeDtypeStruct((4, 4, TB, 3 * DH), jnp.bfloat16)),
        in_specs=[vmem] * 5,
        out_specs=(vmem,) * 2,
        scratch_shapes=[
            pltpu.VMEM((4, WR, D), jnp.bfloat16),
            pltpu.VMEM((3 * TB, 6 * DH), jnp.float32),
            pltpu.VMEM((4, 3, TB, 3 * DH), jnp.bfloat16),
            pltpu.SemaphoreType.DMA((FRONT_SEMS,)),
            pltpu.SemaphoreType.DMA((FRONT_SEMS,)),
        ],
        compiler_params=pltpu.CompilerParams(vmem_limit_bytes=40 << 20, collective_id=0, has_side_effects=True),
        name="front",
    )(h, gain, w, fine, coarse)


BACK_SEMS = 3 + 8 + 32 + 8


def back_kernel(n_ref, d_ref, fine_ref, coarse_ref, gq_ref, gk_ref, gv_ref,
                rbuf, dt, own, cstage, cbuf, hstage, hbuf, fstage, fbuf, zstage, zbuf, ssem, rsem):
    c, z, x, y = place()
    ydev = lambda d: {"sp": x * 4 + (y + d) % 4}
    zdev = lambda d: {"fsdp": (z + d) % 8}
    other = {"bucket": 1 - c}
    greet([ydev(1), ydev(2), ydev(3), other] + [zdev(d) for d in range(1, 8)])()
    cp = Copies(ssem, rsem)
    for dy in (2, 1, 3):
        cp.start(("d", dy), d_ref.at[:, (y + dy) % 4], rbuf.at[dy - 1], ydev(dy))
    for dy in range(1, 4):
        cp.arrive(("d", dy), rbuf.at[dy - 1], ydev(dy))

    for i in range(4):
        cols = pl.ds(i * TB, TB)
        part = [d_ref[i, y, :, :]] + [rbuf[dy - 1, i] for dy in range(1, 4)]
        for dy in range(4):
            dt[(y - dy) % 4, 0:DH, cols] = part[dy][:, 0:DH].T
        key, val = (sum(p[:, s * DH:(s + 1) * DH].astype(jnp.float32) for p in part) for s in (1, 2))
        cos, sin = rope_block(fine_ref, coarse_ref, 4 * i + y)
        key = (key * cos - swap_pairs(key) * sin).astype(jnp.bfloat16).T
        val = val.astype(jnp.bfloat16).T
        for yy in range(4):
            dt[yy, DH:DH + 32, cols] = key[yy * 32:(yy + 1) * 32]
            dt[yy, DH + 32:WR, cols] = val[yy * 32:(yy + 1) * 32]

    order = (4, 3, 5, 2, 6, 1, 7, 0)
    half = WR // 2

    def product(core, dz):
        col = pl.multiple_of((core * 8 + (z + dz) % 8) * WF, WF)
        rhs = n_ref[:, :, pl.ds(col, WF)].reshape(4 * TB, WF)
        return nn(dt[...].reshape(4 * WR, 4 * TB), rhs).reshape(4, WR, WF)

    def compute(t):
        cstage[t] = product(1 - c, order[t]).astype(jnp.bfloat16)
        cp.start(("c", t), cstage.at[t], cbuf.at[t], other)
        own[t] = product(c, order[t])

    def meet(t):
        cp.arrive(("c", t), cbuf.at[t], other)
        own[t] += cbuf[t].astype(jnp.float32)
        hstage[t, 0] = own[t, (y + 2) % 4, 0:half].astype(jnp.bfloat16)
        hstage[t, 1] = own[t, (y + 2) % 4, half:WR].astype(jnp.bfloat16)
        cp.start(("a", t), hstage.at[t, 0], hbuf.at[t, 0], ydev(1))
        cp.start(("b", t), hstage.at[t, 1], hbuf.at[t, 1], ydev(3))

    def pass_on(t):
        cp.arrive(("a", t), hbuf.at[t, 0], ydev(1))
        fstage[t, 0, 0:half] = (own[t, (y + 1) % 4, 0:half] + hbuf[t, 0].astype(jnp.float32)).astype(jnp.bfloat16)
        fstage[t, 0, half:WR] = own[t, (y + 1) % 4, half:WR].astype(jnp.bfloat16)
        cp.start(("r", t), fstage.at[t, 0], fbuf.at[t, 0], ydev(1))
        cp.arrive(("b", t), hbuf.at[t, 1], ydev(3))
        fstage[t, 1, 0:half] = own[t, (y + 3) % 4, 0:half].astype(jnp.bfloat16)
        fstage[t, 1, half:WR] = (own[t, (y + 3) % 4, half:WR] + hbuf[t, 1].astype(jnp.float32)).astype(jnp.bfloat16)
        cp.start(("l", t), fstage.at[t, 1], fbuf.at[t, 1], ydev(3))

    def home(t):
        cp.arrive(("r", t), fbuf.at[t, 0], ydev(1))
        cp.arrive(("l", t), fbuf.at[t, 1], ydev(3))
        total = own[t, y] + fbuf[t, 0].astype(jnp.float32) + fbuf[t, 1].astype(jnp.float32)
        if order[t] == 0:
            own[t, 0] = total
        else:
            zstage[t] = total.astype(jnp.bfloat16)
            cp.start(("z", t), zstage.at[t], zbuf.at[t], zdev(order[t]))

    for t in range(8 + 3):
        for delay, stage in ((0, compute), (1, meet), (2, pass_on), (3, home)):
            if 0 <= t - delay < 8:
                stage(t - delay)

    total = own[7, 0]
    for t in range(7):
        cp.arrive(("z", t), zbuf.at[t], zdev(order[t]))
        total = total + zbuf[t].astype(jnp.float32)
    gq_ref[...] = total[0:DH].T
    gk_ref[...] = total[DH:DH + 32].T
    gv_ref[...] = total[DH + 32:WR].T
    cp.drain()


def back(n, d, fine, coarse):
    vmem = pl.BlockSpec(memory_space=pltpu.VMEM)
    bf = jnp.bfloat16
    return pl.pallas_call(
        back_kernel,
        out_shape=tuple(jax.ShapeDtypeStruct((WF, w), jnp.float32) for w in (DH, 32, 32)),
        in_specs=[vmem] * 4,
        out_specs=(vmem,) * 3,
        scratch_shapes=[
            pltpu.VMEM((3, 4, TB, 3 * DH), bf),
            pltpu.VMEM((4, WR, 4 * TB), bf),
            pltpu.VMEM((8, 4, WR, WF), jnp.float32),
            pltpu.VMEM((8, 4, WR, WF), bf),
            pltpu.VMEM((8, 4, WR, WF), bf),
            pltpu.VMEM((8, 2, WR // 2, WF), bf),
            pltpu.VMEM((8, 2, WR // 2, WF), bf),
            pltpu.VMEM((8, 2, WR, WF), bf),
            pltpu.VMEM((8, 2, WR, WF), bf),
            pltpu.VMEM((7, WR, WF), bf),
            pltpu.VMEM((7, WR, WF), bf),
            pltpu.SemaphoreType.DMA((BACK_SEMS,)),
            pltpu.SemaphoreType.DMA((BACK_SEMS,)),
        ],
        compiler_params=pltpu.CompilerParams(vmem_limit_bytes=48 << 20, collective_id=1, has_side_effects=True),
        name="back",
    )(n, d, fine, coarse)


def local(hidden_states, norm_gain, w_query, w_key, w_value, out_grad, short_docs):
    fine, coarse = (jnp.asarray(t) for t in rope_tables())
    w = jnp.concatenate([w_query.T, w_key.T, w_value.T], axis=0)
    n, qkv = front(hidden_states.reshape(TB, D), norm_gain.reshape(1, D), w, fine, coarse)
    docs = jnp.where(lax.axis_index("bucket") == 0, 0, short_docs[0])
    att, d = attention(qkv.reshape(SEQ, 3 * DH), out_grad.reshape(SEQ, DH), docs, fine, coarse)
    gq, gk, gv = back(n, d.reshape(4, 4, TB, 3 * DH), fine, coarse)
    return att.reshape(1, 1, SEQ, DH), gq, gk, gv


def solution(mesh):
    both = ("bucket", "fsdp")
    return jax.shard_map(
        local,
        mesh=mesh,
        in_specs=(P("bucket", "fsdp", "sp", None), P(), P(both, "sp"), P(both, "sp"), P(both, "sp"),
                  P("bucket", "fsdp", None, "sp"), P("fsdp", None)),
        out_specs=(P("bucket", "fsdp", None, "sp"), P(both, "sp"), P(both, "sp"), P(both, "sp")),
        check_vma=False,
    )
```

```python
import math
import functools
import numpy as np
import jax
import jax.numpy as jnp
from jax import lax
from jax.experimental import pallas as pl
from jax.experimental.pallas import tpu as pltpu
from jax.sharding import PartitionSpec as P

MESH = pl.DeviceIdType.MESH

DH = 128
SEQ = 2048
QB = 512
KB = 512
NEG = -1e30
SCALE = 1.0 / math.sqrt(DH)
EXP_C = SCALE * math.log2(math.e)


def rope_tables():
    freq = np.float32(500000.0) ** (-2.0 * np.arange(64, dtype=np.float32) / DH)
    freq = np.repeat(freq.astype(np.float64), 2)[None, :]
    sign = np.where(np.arange(DH) % 2 == 0, -1.0, 1.0)[None, :]
    fine = np.arange(128)[:, None] * freq
    coarse = 128 * np.arange(16)[:, None] * freq
    f = np.stack([np.cos(fine), np.sin(fine) * sign]).astype(np.float32)
    c = np.stack([np.cos(coarse), np.sin(coarse) * sign]).astype(np.float32)
    return f, c


def rope_block(fine_ref, coarse_ref, block):
    cf, sf = fine_ref[0], fine_ref[1]
    cc = coarse_ref[0, pl.ds(block, 1), :]
    sc = coarse_ref[1, pl.ds(block, 1), :]
    return cf * cc - sf * sc, sf * cc + cf * sc


def swap_pairs(x):
    lane = lax.broadcasted_iota(jnp.int32, x.shape, 1)
    return jnp.where(lane % 2 == 0, pltpu.roll(x, DH - 1, 1), pltpu.roll(x, 1, 1))


def nn(a, b):
    return jnp.dot(a, b, preferred_element_type=jnp.float32)


def nt(a, b):
    return lax.dot_general(a, b, (((1,), (1,)), ((), ())), preferred_element_type=jnp.float32)


D = 4096
TB = 128
WR = 192
WF = 256
EPS = 1e-5
RA, HA, HB = 112, 48, 32


class Copies:
    def __init__(self, send, recv):
        self.send, self.recv, self.ids, self.live = send, recv, {}, []

    def make(self, key, src, dst, dev):
        i = self.ids.setdefault(key, len(self.ids))
        return pltpu.make_async_remote_copy(src_ref=src, dst_ref=dst, send_sem=self.send.at[i], recv_sem=self.recv.at[i],
                                            device_id=dev, device_id_type=MESH)

    def start(self, key, src, dst, dev):
        copy = self.make(key, src, dst, dev)
        copy.start()
        self.live.append(copy)

    def arrive(self, key, dst, dev):
        self.make(key, dst, dst, dev).wait_recv()

    def drain(self):
        for copy in self.live:
            copy.wait_send()


def place():
    c, z, sp = lax.axis_index("bucket"), lax.axis_index("fsdp"), lax.axis_index("sp")
    return c, z, sp // 4, sp % 4


def greet(devs):
    barrier = pltpu.get_barrier_semaphore()
    for dev in devs:
        pl.semaphore_signal(barrier, inc=1, device_id=dev, device_id_type=MESH)
    return lambda: pl.semaphore_wait(barrier, len(devs))


FRONT_SEMS = 7 + 32 + 4 + 28 + 16 + 12 + 12


def front_kernel(h_ref, gain_ref, w_ref, fine_ref, coarse_ref, n_ref, qkv_ref, wbuf, acc, stage, ssem, rsem):
    c, z, x, y = place()
    xdev = lambda d: {"sp": (x + d) % 4 * 4 + y}
    ydev = lambda d: {"sp": x * 4 + (y + d) % 4}
    zdev = lambda d: {"fsdp": (z + d) % 8}
    other = {"bucket": 1 - c}
    wait_all = greet([xdev(1), xdev(3), ydev(1), ydev(2), ydev(3), zdev(1), zdev(7), other])

    def wslot(core, zz, yy, lo=0, size=WR):
        col = pl.multiple_of((core * 8 + zz % 8) * WF, WF)
        return wbuf.at[yy % 4, pl.ds(lo, size), pl.ds(col, WF)]

    for r in range(0, TB, 32):
        rows = h_ref[r:r + 32, :].astype(jnp.float32)
        inv = lax.rsqrt(jnp.mean(rows * rows, axis=1, keepdims=True) + EPS)
        n_ref[x, r:r + 32, :] = (rows * inv * gain_ref[...]).astype(jnp.bfloat16)
    wslot(c, z, y)[...] = w_ref[...]
    wait_all()

    cp = Copies(ssem, rsem)
    zoff = [0, -1, -2, -3, -4, 1, 2, 3]
    yoff = [0, 3, 1, 2]

    def spread(zi):
        src = w_ref.at[pl.ds(0, RA), :] if zi == 0 else wslot(c, z + zoff[zi], y, 0, RA)
        dst = wslot(c, z + zoff[zi], y, 0, RA)
        cp.start(("yr", zi), src, dst, ydev(1))
        cp.start(("yl", zi), src, dst, ydev(3))

    def serve(zi):
        zz = z + zoff[zi]
        cp.arrive(("yr", zi), wslot(c, zz, y + 3, 0, RA), ydev(1))
        part = wslot(c, zz, y + 3, 0, HA)
        cp.start(("ya", zi), part, part, ydev(1))
        cp.arrive(("yl", zi), wslot(c, zz, y + 1, 0, RA), ydev(3))
        part = wslot(c, zz, y + 1, HA, RA - HA)
        cp.start(("yb", zi), part, part, ydev(3))

    def wall(core, zz, lo, size):
        col = pl.multiple_of((core * 8 + zz % 8) * WF, WF)
        return wbuf.at[:, pl.ds(lo, size), pl.ds(col, WF)]

    def last(zi):
        zz = z + zoff[zi]
        cp.arrive(("ya", zi), wslot(c, zz, y + 2, 0, HA), ydev(1))
        cp.arrive(("yb", zi), wslot(c, zz, y + 2, HA, RA - HA), ydev(3))
        cp.start(("ca", zi), wall(c, zz, 0, RA), wall(c, zz, 0, RA), other)

    def chain(yk, step, right):
        n = 4 if right == (yk < 2) else 3
        if step > n:
            return
        zz = z - step if right else z + step
        name = "br" if right else "bl"
        part = wslot(c, zz, y + yoff[yk], RA, WR - RA)
        if step > 0:
            cp.arrive((name, yk, step), part, zdev(1 if right else 7))
        if step < n:
            src = w_ref.at[pl.ds(RA, WR - RA), :] if yk == 0 and step == 0 else part
            cp.start((name, yk, step + 1), src, part, zdev(1 if right else 7))

    def npiece(xx, p):
        return n_ref.at[xx % 4, pl.ds(p * 32, 32), :]

    own_a, own_b = w_ref.at[pl.ds(0, RA), :], w_ref.at[pl.ds(RA, WR - RA), :]
    cp.start(("zr", 1), own_a, wslot(c, z, y, 0, RA), zdev(1))
    cp.start(("zl", 1), own_a, wslot(c, z, y, 0, RA), zdev(7))
    cp.start(("er", 0), own_b, wslot(c, z, y, RA, WR - RA), ydev(1))
    cp.start(("el", 0), own_b, wslot(c, z, y, RA, WR - RA), ydev(3))
    spread(0)
    chain(0, 0, True)
    chain(0, 0, False)
    for p in range(4):
        cp.start(("xr", p), npiece(x, p), npiece(x, p), xdev(1))
        cp.start(("xl", 3 - p), npiece(x, 3 - p), npiece(x, 3 - p), xdev(3))
    cp.arrive(("er", 0), wslot(c, z, y + 3, RA, WR - RA), ydev(1))
    part = wslot(c, z, y + 3, RA, HB)
    cp.start(("ea", 0), part, part, ydev(1))
    chain(1, 0, True)
    chain(1, 0, False)
    cp.arrive(("el", 0), wslot(c, z, y + 1, RA, WR - RA), ydev(3))
    part = wslot(c, z, y + 1, RA + HB, WR - RA - HB)
    cp.start(("eb", 0), part, part, ydev(3))
    chain(2, 0, True)
    chain(2, 0, False)

    def relay_x(p):
        cp.arrive(("xr", p), npiece(x + 3, p), xdev(1))
        cp.start(("xa", p), npiece(x + 3, p), npiece(x + 3, p), xdev(1))
        cp.arrive(("xl", 3 - p), npiece(x + 1, 3 - p), xdev(3))
        cp.start(("xb", 3 - p), npiece(x + 1, 3 - p), npiece(x + 1, 3 - p), xdev(3))

    def core_b(zi):
        zz = z + zoff[zi]
        cp.start(("cb", zi), wall(c, zz, RA, WR - RA), wall(c, zz, RA, WR - RA), other)

    done, waiting = [0], []
    for step in range(1, 5):
        src = wslot(c, z - step, y, 0, RA)
        cp.arrive(("zr", step), src, zdev(1))
        if step < 4:
            cp.start(("zr", step + 1), src, src, zdev(1))
        spread(step)
        fresh = [step]
        if step < 4:
            src = wslot(c, z + step, y, 0, RA)
            cp.arrive(("zl", step), src, zdev(7))
            if step < 3:
                cp.start(("zl", step + 1), src, src, zdev(7))
            spread(4 + step)
            fresh.append(4 + step)
        if step == 1:
            cp.arrive(("ea", 0), wslot(c, z, y + 2, RA, HB), ydev(1))
            cp.arrive(("eb", 0), wslot(c, z, y + 2, RA + HB, WR - RA - HB), ydev(3))
            chain(3, 0, True)
            chain(3, 0, False)
            core_b(0)
        for zi in done:
            serve(zi)
        for yk in range(4):
            chain(yk, step, True)
            chain(yk, step, False)
        core_b(step)
        if step < 4:
            core_b(4 + step)
        for zi in waiting:
            last(zi)
        waiting, done = done, fresh
        if step == 3:
            relay_x(0)
            relay_x(1)
    for zi in done:
        serve(zi)
    for zi in waiting + done:
        last(zi)
    for zi in range(8):
        cp.arrive(("ca", zi), wall(1 - c, z + zoff[zi], 0, RA), other)
        cp.arrive(("cb", zi), wall(1 - c, z + zoff[zi], RA, WR - RA), other)

    lane = lax.broadcasted_iota(jnp.int32, (TB, DH), 1)

    def project(offsets, first):
        rows = len(offsets) * TB
        acc[0:rows, :] = jnp.zeros((rows, 6 * DH), jnp.float32)

        @pl.loop(0, D // 512)
        def _(f):
            cols = pl.ds(pl.multiple_of(f * 512, 512), 512)
            lhs = jnp.concatenate([n_ref[(x + d) % 4, :, cols] for d in offsets], axis=0)
            rhs = jnp.concatenate([wbuf[yy, 0:DH, cols] for yy in range(4)] + [wbuf[yy, DH:WR, cols] for yy in range(4)], axis=0)
            acc[0:rows, :] += nt(lhs, rhs)

        for n, d in enumerate(offsets):
            i = first + n
            xx = (x + d) % 4
            r = pl.ds(n * TB, TB)
            cos, sin = rope_block(fine_ref, coarse_ref, 4 * xx + y)
            turn = lambda t: (t * cos + swap_pairs(t) * sin).astype(jnp.bfloat16)
            a, b = acc[r, 4 * DH:5 * DH], acc[r, 5 * DH:6 * DH]
            pick = lambda p0, p1, p2, p3: jnp.where(lane < 32, p0, jnp.where(lane < 64, p1, jnp.where(lane < 96, p2, p3)))
            key = turn(pick(a, pltpu.roll(a, 96, 1), pltpu.roll(b, 64, 1), pltpu.roll(b, 32, 1)))
            val = pick(pltpu.roll(a, 96, 1), pltpu.roll(a, 64, 1), pltpu.roll(b, 32, 1), b).astype(jnp.bfloat16)
            for dy in range(4):
                q = turn(acc[r, pl.ds(pl.multiple_of((y + dy) % 4 * DH, DH), DH)])
                dst = qkv_ref.at[xx, y] if dy == 0 else stage.at[i, dy - 1]
                dst[:, 0:DH] = q
                dst[:, DH:2 * DH] = key
                dst[:, 2 * DH:3 * DH] = val
            for dy in (2, 1, 3):
                cp.start(("q", i, dy), stage.at[i, dy - 1], qkv_ref.at[xx, y], ydev(dy))

    project((0,), 0)
    for p in (2, 3):
        cp.arrive(("xr", p), npiece(x + 3, p), xdev(1))
        cp.arrive(("xl", 3 - p), npiece(x + 1, 3 - p), xdev(3))
    project((3, 1), 1)
    for p in (0, 1):
        cp.arrive(("xa", p), npiece(x + 2, p), xdev(1))
        cp.arrive(("xb", 3 - p), npiece(x + 2, 3 - p), xdev(3))
    project((2,), 3)
    for i, d in enumerate((0, 3, 1, 2)):
        for dy in range(1, 4):
            cp.arrive(("q", i, dy), qkv_ref.at[(x + d) % 4, (y - dy) % 4], ydev(dy))
    cp.drain()


def front(h, gain, w, fine, coarse):
    vmem = pl.BlockSpec(memory_space=pltpu.VMEM)
    return pl.pallas_call(
        front_kernel,
        out_shape=(jax.ShapeDtypeStruct((4, TB, D), jnp.bfloat16), jax.ShapeDtypeStruct((4, 4, TB, 3 * DH), jnp.bfloat16)),
        in_specs=[vmem] * 5,
        out_specs=(vmem,) * 2,
        scratch_shapes=[
            pltpu.VMEM((4, WR, D), jnp.bfloat16),
            pltpu.VMEM((3 * TB, 6 * DH), jnp.float32),
            pltpu.VMEM((4, 3, TB, 3 * DH), jnp.bfloat16),
            pltpu.SemaphoreType.DMA((FRONT_SEMS,)),
            pltpu.SemaphoreType.DMA((FRONT_SEMS,)),
        ],
        compiler_params=pltpu.CompilerParams(vmem_limit_bytes=40 << 20, collective_id=0, has_side_effects=True),
        name="front",
    )(h, gain, w, fine, coarse)


TAIL_SEMS = 8 + 32 + 7


def tail_kernel(qkv_ref, g_ref, docs_row, docs_col, n_ref, fine_ref, coarse_ref, att_ref, gq_ref, gk_ref, gv_ref,
                kt, vt, s_scr, p_scr, acc, dk_acc, dv_acc, d_scr, dsend, drecv,
                rbuf, dt, own, cstage, cbuf, hstage, hbuf, fstage, fbuf, zstage, zbuf, ssem, rsem):
    c, z, x, y = place()
    ydev = lambda d: {"sp": x * 4 + (y + d) % 4}
    zdev = lambda d: {"fsdp": (z + d) % 8}
    other = {"bucket": 1 - c}
    greet([ydev(1), ydev(2), ydev(3), other] + [zdev(d) for d in range(1, 8)])()
    cp = Copies(ssem, rsem)
    q_ref, k_ref, v_ref = (qkv_ref.at[:, pl.ds(part * DH, DH)] for part in range(3))

    def exchange(i, dy):
        return pltpu.make_async_remote_copy(
            src_ref=d_scr.at[i, (y + dy) % 4], dst_ref=rbuf.at[dy - 1, i], send_sem=dsend.at[i, dy - 1],
            recv_sem=drecv.at[i, dy - 1], device_id=ydev(dy), device_id_type=MESH)

    @pl.loop(0, SEQ // KB)
    def _(j):
        rows = pl.ds(pl.multiple_of(j * KB, KB), KB)
        kt[j] = k_ref[rows, :].T
        vt[j] = v_ref[rows, :].T

    dk_acc[...] = jnp.zeros_like(dk_acc)
    dv_acc[...] = jnp.zeros_like(dv_acc)

    def finish_query(i, dqt):
        dq = dqt.T * SCALE
        for half in range(QB // 128):
            block = i * (QB // 128) + half
            cos, sin = rope_block(fine_ref, coarse_ref, block)
            x = dq[half * 128:(half + 1) * 128]
            rows = pl.ds(pl.multiple_of(block * 128, 128), 128)
            d_scr[i, half, :, 0:DH] = (x * cos - swap_pairs(x) * sin).astype(jnp.bfloat16)
            d_scr[i, half, :, DH:2 * DH] = (dk_acc[rows, :] * SCALE).astype(jnp.bfloat16)
            d_scr[i, half, :, 2 * DH:3 * DH] = dv_acc[rows, :].astype(jnp.bfloat16)
        for dy in (2, 1, 3):
            exchange(i, dy).start()

    @pl.when(c == 0)
    def _():
        @pl.loop(0, SEQ // QB)
        def _(step):
            i = SEQ // QB - 1 - step
            qrows = pl.ds(pl.multiple_of(i * QB, QB), QB)
            q = q_ref[qrows, :]
            g = g_ref[qrows, :]

            def scores(j):
                return nt(k_ref[pl.ds(pl.multiple_of(j * KB, KB), KB), :], q)

            def pass1(j, m):
                s = scores(j)
                s_scr[j] = s
                return jnp.maximum(m, jnp.max(s.reshape(KB // 8, 8, QB), axis=0))

            m8 = lax.fori_loop(0, i, pass1, jnp.full((8, QB), NEG, jnp.float32))
            s = scores(i)
            key = lax.broadcasted_iota(jnp.int32, (KB, QB), 0)
            qry = lax.broadcasted_iota(jnp.int32, (KB, QB), 1)
            s = jnp.where(key <= qry, s, NEG)
            s_scr[i] = s
            m8 = jnp.maximum(m8, jnp.max(s.reshape(KB // 8, 8, QB), axis=0))
            m = jnp.max(m8, axis=0, keepdims=True)
            acc[...] = jnp.zeros_like(acc)

            def pass2(j, l8):
                p = jnp.exp2((s_scr[j] - m) * EXP_C)
                pb = p.astype(jnp.bfloat16)
                p_scr[j] = pb
                acc[...] += nn(vt[j], pb)
                return l8 + jnp.sum(p.reshape(KB // 8, 8, QB), axis=0)

            l8 = lax.fori_loop(0, i + 1, pass2, jnp.zeros((8, QB), jnp.float32))
            rl = 1.0 / jnp.sum(l8, axis=0, keepdims=True)
            ot = acc[...] * rl
            att_ref[qrows, :] = ot.T.astype(jnp.bfloat16)
            gt = (g.astype(jnp.float32).T * rl).astype(jnp.bfloat16)
            gs = gt.T
            d = jnp.sum(ot * gt.astype(jnp.float32), axis=0, keepdims=True)
            acc[...] = jnp.zeros_like(acc)

            @pl.loop(0, i + 1)
            def _(j):
                krows = pl.ds(pl.multiple_of(j * KB, KB), KB)
                pb = p_scr[j]
                dp = nn(v_ref[krows, :], gt)
                ds = (pb.astype(jnp.float32) * (dp - d)).astype(jnp.bfloat16)
                acc[...] += nn(kt[j], ds)
                dk_acc[krows, :] += nn(ds, q)
                dv_acc[krows, :] += nn(pb, gs)

            finish_query(i, acc[...])

    @pl.when(c == 1)
    def _():
        span = QB + 128

        @pl.loop(0, SEQ // QB)
        def _(step):
            i = SEQ // QB - 1 - step
            qrows = pl.ds(pl.multiple_of(i * QB, QB), QB)
            first = pl.multiple_of(jnp.maximum(i * QB - 128, 0), 128)
            krows = pl.ds(first, span)
            q = q_ref[qrows, :]
            g = g_ref[qrows, :]
            k = k_ref[krows, :]
            v = v_ref[krows, :]
            key = lax.broadcasted_iota(jnp.int32, (span, QB), 0) + first
            qry = lax.broadcasted_iota(jnp.int32, (span, QB), 1) + i * QB
            same = docs_col[krows, :] == docs_row[i]
            s = jnp.where((key <= qry) & same, nt(k, q), NEG)
            m = jnp.max(s, axis=0, keepdims=True)
            p = jnp.exp2((s - m) * EXP_C)
            rl = 1.0 / jnp.sum(p, axis=0, keepdims=True)
            pb = p.astype(jnp.bfloat16)
            ot = nn(v.T, pb) * rl
            att_ref[qrows, :] = ot.T.astype(jnp.bfloat16)
            gt = (g.astype(jnp.float32).T * rl).astype(jnp.bfloat16)
            gs = gt.T
            d = jnp.sum(ot * gt.astype(jnp.float32), axis=0, keepdims=True)
            dp = nn(v, gt)
            ds = (pb.astype(jnp.float32) * (dp - d)).astype(jnp.bfloat16)
            dk_acc[krows, :] += nn(ds, q)
            dv_acc[krows, :] += nn(pb, gs)
            finish_query(i, nn(k.T, ds))

    for i in (3, 2, 1, 0):
        for dy in range(1, 4):
            exchange(i, dy).wait()

    for i in range(4):
        cols = pl.ds(i * TB, TB)
        part = [d_scr[i, y]] + [rbuf[dy - 1, i] for dy in range(1, 4)]
        for dy in range(4):
            dt[(y - dy) % 4, 0:DH, cols] = part[dy][:, 0:DH].T
        key, val = (sum(p[:, s * DH:(s + 1) * DH].astype(jnp.float32) for p in part) for s in (1, 2))
        cos, sin = rope_block(fine_ref, coarse_ref, 4 * i + y)
        key = (key * cos - swap_pairs(key) * sin).astype(jnp.bfloat16).T
        val = val.astype(jnp.bfloat16).T
        for yy in range(4):
            dt[yy, DH:DH + 32, cols] = key[yy * 32:(yy + 1) * 32]
            dt[yy, DH + 32:WR, cols] = val[yy * 32:(yy + 1) * 32]

    order = (4, 3, 5, 2, 6, 1, 7, 0)
    half = WR // 2

    def product(core, dz):
        col = pl.multiple_of((core * 8 + (z + dz) % 8) * WF, WF)
        rhs = n_ref[:, :, pl.ds(col, WF)].reshape(4 * TB, WF)
        return nn(dt[...].reshape(4 * WR, 4 * TB), rhs).reshape(4, WR, WF)

    def compute(t):
        cstage[t] = product(1 - c, order[t]).astype(jnp.bfloat16)
        cp.start(("c", t), cstage.at[t], cbuf.at[t], other)
        own[t] = product(c, order[t])

    def meet(t):
        cp.arrive(("c", t), cbuf.at[t], other)
        own[t] += cbuf[t].astype(jnp.float32)
        hstage[t, 0] = own[t, (y + 2) % 4, 0:half].astype(jnp.bfloat16)
        hstage[t, 1] = own[t, (y + 2) % 4, half:WR].astype(jnp.bfloat16)
        cp.start(("a", t), hstage.at[t, 0], hbuf.at[t, 0], ydev(1))
        cp.start(("b", t), hstage.at[t, 1], hbuf.at[t, 1], ydev(3))

    def pass_on(t):
        cp.arrive(("a", t), hbuf.at[t, 0], ydev(1))
        fstage[t, 0, 0:half] = (own[t, (y + 1) % 4, 0:half] + hbuf[t, 0].astype(jnp.float32)).astype(jnp.bfloat16)
        fstage[t, 0, half:WR] = own[t, (y + 1) % 4, half:WR].astype(jnp.bfloat16)
        cp.start(("r", t), fstage.at[t, 0], fbuf.at[t, 0], ydev(1))
        cp.arrive(("b", t), hbuf.at[t, 1], ydev(3))
        fstage[t, 1, 0:half] = own[t, (y + 3) % 4, 0:half].astype(jnp.bfloat16)
        fstage[t, 1, half:WR] = (own[t, (y + 3) % 4, half:WR] + hbuf[t, 1].astype(jnp.float32)).astype(jnp.bfloat16)
        cp.start(("l", t), fstage.at[t, 1], fbuf.at[t, 1], ydev(3))

    def home(t):
        cp.arrive(("r", t), fbuf.at[t, 0], ydev(1))
        cp.arrive(("l", t), fbuf.at[t, 1], ydev(3))
        total = own[t, y] + fbuf[t, 0].astype(jnp.float32) + fbuf[t, 1].astype(jnp.float32)
        if order[t] == 0:
            own[t, 0] = total
        else:
            zstage[t] = total.astype(jnp.bfloat16)
            cp.start(("z", t), zstage.at[t], zbuf.at[t], zdev(order[t]))

    for t in range(8 + 3):
        for delay, stage in ((0, compute), (1, meet), (2, pass_on), (3, home)):
            if 0 <= t - delay < 8:
                stage(t - delay)

    total = own[7, 0]
    for t in range(7):
        cp.arrive(("z", t), zbuf.at[t], zdev(order[t]))
        total = total + zbuf[t].astype(jnp.float32)
    gq_ref[...] = total[0:DH].T
    gk_ref[...] = total[DH:DH + 32].T
    gv_ref[...] = total[DH + 32:WR].T
    cp.drain()


def tail(qkv, g, docs, n, fine, coarse):
    vmem = pl.BlockSpec(memory_space=pltpu.VMEM)
    bf, f32, nb = jnp.bfloat16, jnp.float32, SEQ // KB
    return pl.pallas_call(
        tail_kernel,
        out_shape=(jax.ShapeDtypeStruct((SEQ, DH), bf),) + tuple(jax.ShapeDtypeStruct((WF, w), f32) for w in (DH, 32, 32)),
        in_specs=[vmem] * 7,
        out_specs=(vmem,) * 4,
        scratch_shapes=[
            pltpu.VMEM((nb, DH, KB), bf),
            pltpu.VMEM((nb, DH, KB), bf),
            pltpu.VMEM((nb, KB, QB), f32),
            pltpu.VMEM((nb, KB, QB), bf),
            pltpu.VMEM((DH, QB), f32),
            pltpu.VMEM((SEQ, DH), f32),
            pltpu.VMEM((SEQ, DH), f32),
            pltpu.VMEM((4, 4, TB, 3 * DH), bf),
            pltpu.SemaphoreType.DMA((4, 3)),
            pltpu.SemaphoreType.DMA((4, 3)),
            pltpu.VMEM((3, 4, TB, 3 * DH), bf),
            pltpu.VMEM((4, WR, 4 * TB), bf),
            pltpu.VMEM((8, 4, WR, WF), f32),
            pltpu.VMEM((8, 4, WR, WF), bf),
            pltpu.VMEM((8, 4, WR, WF), bf),
            pltpu.VMEM((8, 2, WR // 2, WF), bf),
            pltpu.VMEM((8, 2, WR // 2, WF), bf),
            pltpu.VMEM((8, 2, WR, WF), bf),
            pltpu.VMEM((8, 2, WR, WF), bf),
            pltpu.VMEM((7, WR, WF), bf),
            pltpu.VMEM((7, WR, WF), bf),
            pltpu.SemaphoreType.DMA((TAIL_SEMS,)),
            pltpu.SemaphoreType.DMA((TAIL_SEMS,)),
        ],
        compiler_params=pltpu.CompilerParams(vmem_limit_bytes=56 << 20, collective_id=1, has_side_effects=True),
        name="tail",
    )(qkv, g, docs.reshape(SEQ // QB, 1, QB), docs.reshape(SEQ, 1), n, fine, coarse)


def local(hidden_states, norm_gain, w_query, w_key, w_value, out_grad, short_docs):
    fine, coarse = (jnp.asarray(t) for t in rope_tables())
    w = jnp.concatenate([w_query.T, w_key.T, w_value.T], axis=0)
    n, qkv = front(hidden_states.reshape(TB, D), norm_gain.reshape(1, D), w, fine, coarse)
    docs = jnp.where(lax.axis_index("bucket") == 0, 0, short_docs[0])
    att, gq, gk, gv = tail(qkv.reshape(SEQ, 3 * DH), out_grad.reshape(SEQ, DH), docs, n, fine, coarse)
    return att.reshape(1, 1, SEQ, DH), gq, gk, gv


def solution(mesh):
    both = ("bucket", "fsdp")
    return jax.shard_map(
        local,
        mesh=mesh,
        in_specs=(P("bucket", "fsdp", "sp", None), P(), P(both, "sp"), P(both, "sp"), P(both, "sp"),
                  P("bucket", "fsdp", None, "sp"), P("fsdp", None)),
        out_specs=(P("bucket", "fsdp", None, "sp"), P(both, "sp"), P(both, "sp"), P(both, "sp")),
        check_vma=False,
    )
```

```python
import math
import functools
import numpy as np
import jax
import jax.numpy as jnp
from jax import lax
from jax.experimental import pallas as pl
from jax.experimental.pallas import tpu as pltpu
from jax.sharding import PartitionSpec as P

MESH = pl.DeviceIdType.MESH

DH = 128
SEQ = 2048
QB = 512
KB = 512
NEG = -1e30
SCALE = 1.0 / math.sqrt(DH)
EXP_C = SCALE * math.log2(math.e)


def rope_tables():
    freq = np.float32(500000.0) ** (-2.0 * np.arange(64, dtype=np.float32) / DH)
    freq = np.repeat(freq.astype(np.float64), 2)[None, :]
    sign = np.where(np.arange(DH) % 2 == 0, -1.0, 1.0)[None, :]
    fine = np.arange(128)[:, None] * freq
    coarse = 128 * np.arange(16)[:, None] * freq
    f = np.stack([np.cos(fine), np.sin(fine) * sign]).astype(np.float32)
    c = np.stack([np.cos(coarse), np.sin(coarse) * sign]).astype(np.float32)
    return f, c


def rope_block(fine_ref, coarse_ref, block):
    cf, sf = fine_ref[0], fine_ref[1]
    cc = coarse_ref[0, pl.ds(block, 1), :]
    sc = coarse_ref[1, pl.ds(block, 1), :]
    return cf * cc - sf * sc, sf * cc + cf * sc


def swap_pairs(x):
    lane = lax.broadcasted_iota(jnp.int32, x.shape, 1)
    return jnp.where(lane % 2 == 0, pltpu.roll(x, DH - 1, 1), pltpu.roll(x, 1, 1))


def nn(a, b):
    return jnp.dot(a, b, preferred_element_type=jnp.float32)


def nt(a, b):
    return lax.dot_general(a, b, (((1,), (1,)), ((), ())), preferred_element_type=jnp.float32)


D = 4096
TB = 128
WR = 192
WF = 256
EPS = 1e-5
RA, HA, HB = 112, 48, 32


class Copies:
    def __init__(self, send, recv):
        self.send, self.recv, self.ids, self.live = send, recv, {}, []

    def make(self, key, src, dst, dev):
        i = self.ids.setdefault(key, len(self.ids))
        return pltpu.make_async_remote_copy(src_ref=src, dst_ref=dst, send_sem=self.send.at[i], recv_sem=self.recv.at[i],
                                            device_id=dev, device_id_type=MESH)

    def start(self, key, src, dst, dev):
        copy = self.make(key, src, dst, dev)
        copy.start()
        self.live.append(copy)

    def arrive(self, key, dst, dev):
        self.make(key, dst, dst, dev).wait_recv()

    def drain(self):
        for copy in self.live:
            copy.wait_send()


def place():
    c, z, sp = lax.axis_index("bucket"), lax.axis_index("fsdp"), lax.axis_index("sp")
    return c, z, sp // 4, sp % 4


def greet(devs):
    barrier = pltpu.get_barrier_semaphore()
    for dev in devs:
        pl.semaphore_signal(barrier, inc=1, device_id=dev, device_id_type=MESH)
    return lambda: pl.semaphore_wait(barrier, len(devs))


SEMS = 7 + 32 + 4 + 28 + 16 + 12 + 12 + 8 + 32 + 7


class Part:
    def __init__(self, ref, part):
        self.ref, self.part = ref, part

    def __getitem__(self, index):
        return self.ref[index[0], self.part * DH:(self.part + 1) * DH]


def block_kernel(h_hbm, gain_hbm, wq_hbm, wk_hbm, wv_hbm, g_hbm, docs_hbm, fine_hbm, coarse_hbm, att_ref, grad_ref,
                 h_ref, gain_ref, wq_ref, wk_ref, wv_ref, g_ref, docs_ref, fine_ref, coarse_ref, w_ref,
                 n_ref, qkv4_ref, wbuf, pacc, stage,
                 kt, vt, s_scr, p_scr, acc, dk_acc, dv_acc, d_scr, dsend, drecv,
                 rbuf, dt, own, cstage, cbuf, hstage, hbuf, fstage, fbuf, zstage, zbuf, ssem, rsem, lsem):
    loads = {}
    for name, src, dst in (("wq", wq_hbm, wq_ref), ("wk", wk_hbm, wk_ref), ("wv", wv_hbm, wv_ref), ("h", h_hbm, h_ref),
                           ("gain", gain_hbm, gain_ref), ("fine", fine_hbm, fine_ref), ("coarse", coarse_hbm, coarse_ref),
                           ("g", g_hbm, g_ref), ("docs", docs_hbm, docs_ref)):
        loads[name] = pltpu.make_async_copy(src, dst, lsem.at[len(loads)])
        loads[name].start()
    c, z, x, y = place()
    xdev = lambda d: {"sp": (x + d) % 4 * 4 + y}
    ydev = lambda d: {"sp": x * 4 + (y + d) % 4}
    zdev = lambda d: {"fsdp": (z + d) % 8}
    other = {"bucket": 1 - c}
    wait_all = greet([xdev(1), xdev(3), ydev(1), ydev(2), ydev(3), other] + [zdev(d) for d in range(1, 8)])
    qkv_ref = qkv4_ref

    def wslot(core, zz, yy, lo=0, size=WR):
        col = pl.multiple_of((core * 8 + zz % 8) * WF, WF)
        return wbuf.at[yy % 4, pl.ds(lo, size), pl.ds(col, WF)]

    for name in ("wq", "wk", "wv"):
        loads[name].wait()
    w_ref[0:DH] = wq_ref[...].T
    w_ref[DH:DH + 32] = wk_ref[...].T
    w_ref[DH + 32:WR] = wv_ref[...].T
    wslot(c, z, y)[...] = w_ref[...]
    wait_all()
    loads["gain"].wait()
    cp = Copies(ssem, rsem)
    zoff = [0, -1, -2, -3, -4, 1, 2, 3]
    yoff = [0, 3, 1, 2]

    def spread(zi):
        src = w_ref.at[pl.ds(0, RA), :] if zi == 0 else wslot(c, z + zoff[zi], y, 0, RA)
        dst = wslot(c, z + zoff[zi], y, 0, RA)
        cp.start(("yr", zi), src, dst, ydev(1))
        cp.start(("yl", zi), src, dst, ydev(3))

    def serve(zi):
        zz = z + zoff[zi]
        cp.arrive(("yr", zi), wslot(c, zz, y + 3, 0, RA), ydev(1))
        part = wslot(c, zz, y + 3, 0, HA)
        cp.start(("ya", zi), part, part, ydev(1))
        cp.arrive(("yl", zi), wslot(c, zz, y + 1, 0, RA), ydev(3))
        part = wslot(c, zz, y + 1, HA, RA - HA)
        cp.start(("yb", zi), part, part, ydev(3))

    def wall(core, zz, lo, size):
        col = pl.multiple_of((core * 8 + zz % 8) * WF, WF)
        return wbuf.at[:, pl.ds(lo, size), pl.ds(col, WF)]

    def last(zi):
        zz = z + zoff[zi]
        cp.arrive(("ya", zi), wslot(c, zz, y + 2, 0, HA), ydev(1))
        cp.arrive(("yb", zi), wslot(c, zz, y + 2, HA, RA - HA), ydev(3))
        cp.start(("ca", zi), wall(c, zz, 0, RA), wall(c, zz, 0, RA), other)

    def chain(yk, step, right):
        n = 4 if right == (yk < 2) else 3
        if step > n:
            return
        zz = z - step if right else z + step
        name = "br" if right else "bl"
        part = wslot(c, zz, y + yoff[yk], RA, WR - RA)
        if step > 0:
            cp.arrive((name, yk, step), part, zdev(1 if right else 7))
        if step < n:
            src = w_ref.at[pl.ds(RA, WR - RA), :] if yk == 0 and step == 0 else part
            cp.start((name, yk, step + 1), src, part, zdev(1 if right else 7))

    def npiece(xx, p):
        return n_ref.at[xx % 4, pl.ds(p * 32, 32), :]

    own_a, own_b = w_ref.at[pl.ds(0, RA), :], w_ref.at[pl.ds(RA, WR - RA), :]
    cp.start(("zr", 1), own_a, wslot(c, z, y, 0, RA), zdev(1))
    cp.start(("zl", 1), own_a, wslot(c, z, y, 0, RA), zdev(7))
    cp.start(("er", 0), own_b, wslot(c, z, y, RA, WR - RA), ydev(1))
    cp.start(("el", 0), own_b, wslot(c, z, y, RA, WR - RA), ydev(3))
    spread(0)
    chain(0, 0, True)
    chain(0, 0, False)
    loads["h"].wait()
    for p in (0, 3, 1, 2):
        rows = h_ref[p * 32:(p + 1) * 32, :].astype(jnp.float32)
        inv = lax.rsqrt(jnp.mean(rows * rows, axis=1, keepdims=True) + EPS)
        n_ref[x, p * 32:(p + 1) * 32, :] = (rows * inv * gain_ref[...]).astype(jnp.bfloat16)
        if p in (0, 1):
            cp.start(("xr", p), npiece(x, p), npiece(x, p), xdev(1))
        else:
            cp.start(("xl", p), npiece(x, p), npiece(x, p), xdev(3))
    for p in (2, 3):
        cp.start(("xr", p), npiece(x, p), npiece(x, p), xdev(1))
        cp.start(("xl", 3 - p), npiece(x, 3 - p), npiece(x, 3 - p), xdev(3))
    cp.arrive(("er", 0), wslot(c, z, y + 3, RA, WR - RA), ydev(1))
    part = wslot(c, z, y + 3, RA, HB)
    cp.start(("ea", 0), part, part, ydev(1))
    chain(1, 0, True)
    chain(1, 0, False)
    cp.arrive(("el", 0), wslot(c, z, y + 1, RA, WR - RA), ydev(3))
    part = wslot(c, z, y + 1, RA + HB, WR - RA - HB)
    cp.start(("eb", 0), part, part, ydev(3))
    chain(2, 0, True)
    chain(2, 0, False)

    def relay_x(p):
        cp.arrive(("xr", p), npiece(x + 3, p), xdev(1))
        cp.start(("xa", p), npiece(x + 3, p), npiece(x + 3, p), xdev(1))
        cp.arrive(("xl", 3 - p), npiece(x + 1, 3 - p), xdev(3))
        cp.start(("xb", 3 - p), npiece(x + 1, 3 - p), npiece(x + 1, 3 - p), xdev(3))

    def core_b(zi):
        zz = z + zoff[zi]
        cp.start(("cb", zi), wall(c, zz, RA, WR - RA), wall(c, zz, RA, WR - RA), other)

    done, waiting = [0], []
    for step in range(1, 5):
        src = wslot(c, z - step, y, 0, RA)
        cp.arrive(("zr", step), src, zdev(1))
        if step < 4:
            cp.start(("zr", step + 1), src, src, zdev(1))
        spread(step)
        fresh = [step]
        if step < 4:
            src = wslot(c, z + step, y, 0, RA)
            cp.arrive(("zl", step), src, zdev(7))
            if step < 3:
                cp.start(("zl", step + 1), src, src, zdev(7))
            spread(4 + step)
            fresh.append(4 + step)
        if step == 1:
            cp.arrive(("ea", 0), wslot(c, z, y + 2, RA, HB), ydev(1))
            cp.arrive(("eb", 0), wslot(c, z, y + 2, RA + HB, WR - RA - HB), ydev(3))
            chain(3, 0, True)
            chain(3, 0, False)
            core_b(0)
        for zi in done:
            serve(zi)
        for yk in range(4):
            chain(yk, step, True)
            chain(yk, step, False)
        core_b(step)
        if step < 4:
            core_b(4 + step)
        for zi in waiting:
            last(zi)
        waiting, done = done, fresh
        if step == 3:
            relay_x(0)
            relay_x(1)
    for zi in done:
        serve(zi)
    for zi in waiting + done:
        last(zi)
    for zi in range(8):
        cp.arrive(("ca", zi), wall(1 - c, z + zoff[zi], 0, RA), other)
        cp.arrive(("cb", zi), wall(1 - c, z + zoff[zi], RA, WR - RA), other)

    lane = lax.broadcasted_iota(jnp.int32, (TB, DH), 1)

    def project(offsets, first):
        rows = len(offsets) * TB
        pacc[0:rows, :] = jnp.zeros((rows, 6 * DH), jnp.float32)

        @pl.loop(0, D // 512)
        def _(f):
            cols = pl.ds(pl.multiple_of(f * 512, 512), 512)
            lhs = jnp.concatenate([n_ref[(x + d) % 4, :, cols] for d in offsets], axis=0)
            rhs = jnp.concatenate([wbuf[yy, 0:DH, cols] for yy in range(4)] + [wbuf[yy, DH:WR, cols] for yy in range(4)], axis=0)
            pacc[0:rows, :] += nt(lhs, rhs)

        for n, d in enumerate(offsets):
            i = first + n
            xx = (x + d) % 4
            r = pl.ds(n * TB, TB)
            cos, sin = rope_block(fine_ref, coarse_ref, 4 * xx + y)
            turn = lambda t: (t * cos + swap_pairs(t) * sin).astype(jnp.bfloat16)
            a, b = pacc[r, 4 * DH:5 * DH], pacc[r, 5 * DH:6 * DH]
            pick = lambda p0, p1, p2, p3: jnp.where(lane < 32, p0, jnp.where(lane < 64, p1, jnp.where(lane < 96, p2, p3)))
            key = turn(pick(a, pltpu.roll(a, 96, 1), pltpu.roll(b, 64, 1), pltpu.roll(b, 32, 1)))
            val = pick(pltpu.roll(a, 96, 1), pltpu.roll(a, 64, 1), pltpu.roll(b, 32, 1), b).astype(jnp.bfloat16)
            for dy in range(4):
                q = turn(pacc[r, pl.ds(pl.multiple_of((y + dy) % 4 * DH, DH), DH)])
                dst = qkv_ref.at[xx, y] if dy == 0 else stage.at[i, dy - 1]
                dst[:, 0:DH] = q
                dst[:, DH:2 * DH] = key
                dst[:, 2 * DH:3 * DH] = val
            for dy in (2, 1, 3):
                cp.start(("q", i, dy), stage.at[i, dy - 1], qkv_ref.at[xx, y], ydev(dy))

    loads["fine"].wait()
    loads["coarse"].wait()
    project((0,), 0)
    for p in (2, 3):
        cp.arrive(("xr", p), npiece(x + 3, p), xdev(1))
        cp.arrive(("xl", 3 - p), npiece(x + 1, 3 - p), xdev(3))
    project((3, 1), 1)
    for p in (0, 1):
        cp.arrive(("xa", p), npiece(x + 2, p), xdev(1))
        cp.arrive(("xb", 3 - p), npiece(x + 2, 3 - p), xdev(3))
    project((2,), 3)
    for i, d in enumerate((0, 3, 1, 2)):
        for dy in range(1, 4):
            cp.arrive(("q", i, dy), qkv_ref.at[(x + d) % 4, (y - dy) % 4], ydev(dy))


    q_ref, k_ref, v_ref = (Part(qkv_ref.reshape(SEQ, 3 * DH), part) for part in range(3))
    loads["g"].wait()
    loads["docs"].wait()

    def exchange(i, dy):
        return pltpu.make_async_remote_copy(
            src_ref=d_scr.at[i, (y + dy) % 4], dst_ref=rbuf.at[dy - 1, i], send_sem=dsend.at[i, dy - 1],
            recv_sem=drecv.at[i, dy - 1], device_id=ydev(dy), device_id_type=MESH)

    @pl.loop(0, SEQ // KB)
    def _(j):
        rows = pl.ds(pl.multiple_of(j * KB, KB), KB)
        kt[j] = k_ref[rows, :].T
        vt[j] = v_ref[rows, :].T

    dk_acc[...] = jnp.zeros_like(dk_acc)
    dv_acc[...] = jnp.zeros_like(dv_acc)

    def finish_query(i, dqt):
        dq = dqt.T * SCALE
        for half in range(QB // 128):
            block = i * (QB // 128) + half
            cos, sin = rope_block(fine_ref, coarse_ref, block)
            x = dq[half * 128:(half + 1) * 128]
            rows = pl.ds(pl.multiple_of(block * 128, 128), 128)
            d_scr[i, half, :, 0:DH] = (x * cos - swap_pairs(x) * sin).astype(jnp.bfloat16)
            d_scr[i, half, :, DH:2 * DH] = (dk_acc[rows, :] * SCALE).astype(jnp.bfloat16)
            d_scr[i, half, :, 2 * DH:3 * DH] = dv_acc[rows, :].astype(jnp.bfloat16)
        for dy in (2, 1, 3):
            exchange(i, dy).start()

    @pl.when(c == 0)
    def _():
        @pl.loop(0, SEQ // QB)
        def _(step):
            i = SEQ // QB - 1 - step
            qrows = pl.ds(pl.multiple_of(i * QB, QB), QB)
            q = q_ref[qrows, :]
            g = g_ref[qrows, :]

            def scores(j):
                return nt(k_ref[pl.ds(pl.multiple_of(j * KB, KB), KB), :], q)

            def pass1(j, m):
                s = scores(j)
                s_scr[j] = s
                return jnp.maximum(m, jnp.max(s.reshape(KB // 8, 8, QB), axis=0))

            m8 = lax.fori_loop(0, i, pass1, jnp.full((8, QB), NEG, jnp.float32))
            s = scores(i)
            key = lax.broadcasted_iota(jnp.int32, (KB, QB), 0)
            qry = lax.broadcasted_iota(jnp.int32, (KB, QB), 1)
            s = jnp.where(key <= qry, s, NEG)
            s_scr[i] = s
            m8 = jnp.maximum(m8, jnp.max(s.reshape(KB // 8, 8, QB), axis=0))
            m = jnp.max(m8, axis=0, keepdims=True)
            acc[...] = jnp.zeros_like(acc)

            def pass2(j, l8):
                p = jnp.exp2((s_scr[j] - m) * EXP_C)
                pb = p.astype(jnp.bfloat16)
                p_scr[j] = pb
                acc[...] += nn(vt[j], pb)
                return l8 + jnp.sum(p.reshape(KB // 8, 8, QB), axis=0)

            l8 = lax.fori_loop(0, i + 1, pass2, jnp.zeros((8, QB), jnp.float32))
            rl = 1.0 / jnp.sum(l8, axis=0, keepdims=True)
            ot = acc[...] * rl
            att_ref[qrows, :] = ot.T.astype(jnp.bfloat16)
            gt = (g.astype(jnp.float32).T * rl).astype(jnp.bfloat16)
            gs = gt.T
            d = jnp.sum(ot * gt.astype(jnp.float32), axis=0, keepdims=True)
            acc[...] = jnp.zeros_like(acc)

            @pl.loop(0, i + 1)
            def _(j):
                krows = pl.ds(pl.multiple_of(j * KB, KB), KB)
                pb = p_scr[j]
                dp = nn(v_ref[krows, :], gt)
                ds = (pb.astype(jnp.float32) * (dp - d)).astype(jnp.bfloat16)
                acc[...] += nn(kt[j], ds)
                dk_acc[krows, :] += nn(ds, q)
                dv_acc[krows, :] += nn(pb, gs)

            finish_query(i, acc[...])

    @pl.when(c == 1)
    def _():
        span = QB + 128

        @pl.loop(0, SEQ // QB)
        def _(step):
            i = SEQ // QB - 1 - step
            qrows = pl.ds(pl.multiple_of(i * QB, QB), QB)
            first = pl.multiple_of(jnp.maximum(i * QB - 128, 0), 128)
            krows = pl.ds(first, span)
            q = q_ref[qrows, :]
            g = g_ref[qrows, :]
            k = k_ref[krows, :]
            v = v_ref[krows, :]
            key = lax.broadcasted_iota(jnp.int32, (span, QB), 0) + first
            qry = lax.broadcasted_iota(jnp.int32, (span, QB), 1) + i * QB
            def docs(start, size):
                rows = [docs_ref[:, pl.ds(pl.multiple_of(start + o, 128), 128)] for o in range(0, size, 128)]
                return jnp.concatenate(rows, axis=1).astype(jnp.float32)

            same = jnp.broadcast_to(docs(first, span), (128, span)).T[:, 0:1] == docs(i * QB, QB)
            s = jnp.where((key <= qry) & same, nt(k, q), NEG)
            m = jnp.max(s, axis=0, keepdims=True)
            p = jnp.exp2((s - m) * EXP_C)
            rl = 1.0 / jnp.sum(p, axis=0, keepdims=True)
            pb = p.astype(jnp.bfloat16)
            ot = nn(v.T, pb) * rl
            att_ref[qrows, :] = ot.T.astype(jnp.bfloat16)
            gt = (g.astype(jnp.float32).T * rl).astype(jnp.bfloat16)
            gs = gt.T
            d = jnp.sum(ot * gt.astype(jnp.float32), axis=0, keepdims=True)
            dp = nn(v, gt)
            ds = (pb.astype(jnp.float32) * (dp - d)).astype(jnp.bfloat16)
            dk_acc[krows, :] += nn(ds, q)
            dv_acc[krows, :] += nn(pb, gs)
            finish_query(i, nn(k.T, ds))

    for i in (3, 2, 1, 0):
        for dy in range(1, 4):
            exchange(i, dy).wait()

    for i in range(4):
        cols = pl.ds(i * TB, TB)
        part = [d_scr[i, y]] + [rbuf[dy - 1, i] for dy in range(1, 4)]
        for dy in range(4):
            dt[(y - dy) % 4, 0:DH, cols] = part[dy][:, 0:DH].T
        key, val = (sum(p[:, s * DH:(s + 1) * DH].astype(jnp.float32) for p in part) for s in (1, 2))
        cos, sin = rope_block(fine_ref, coarse_ref, 4 * i + y)
        key = (key * cos - swap_pairs(key) * sin).astype(jnp.bfloat16).T
        val = val.astype(jnp.bfloat16).T
        for yy in range(4):
            dt[yy, DH:DH + 32, cols] = key[yy * 32:(yy + 1) * 32]
            dt[yy, DH + 32:WR, cols] = val[yy * 32:(yy + 1) * 32]

    order = (4, 3, 5, 2, 6, 1, 7, 0)
    half = WR // 2

    def product(core, dz):
        col = pl.multiple_of((core * 8 + (z + dz) % 8) * WF, WF)
        rhs = n_ref[:, :, pl.ds(col, WF)].reshape(4 * TB, WF)
        return nn(dt[...].reshape(4 * WR, 4 * TB), rhs).reshape(4, WR, WF)

    def compute(t):
        cstage[t] = product(1 - c, order[t]).astype(jnp.bfloat16)
        cp.start(("c", t), cstage.at[t], cbuf.at[t], other)
        own[t] = product(c, order[t])

    def meet(t):
        cp.arrive(("c", t), cbuf.at[t], other)
        own[t] += cbuf[t].astype(jnp.float32)
        hstage[t, 0] = own[t, (y + 2) % 4, 0:half].astype(jnp.bfloat16)
        hstage[t, 1] = own[t, (y + 2) % 4, half:WR].astype(jnp.bfloat16)
        cp.start(("a", t), hstage.at[t, 0], hbuf.at[t, 0], ydev(1))
        cp.start(("b", t), hstage.at[t, 1], hbuf.at[t, 1], ydev(3))

    def pass_on(t):
        cp.arrive(("a", t), hbuf.at[t, 0], ydev(1))
        fstage[t, 0, 0:half] = (own[t, (y + 1) % 4, 0:half] + hbuf[t, 0].astype(jnp.float32)).astype(jnp.bfloat16)
        fstage[t, 0, half:WR] = own[t, (y + 1) % 4, half:WR].astype(jnp.bfloat16)
        cp.start(("r", t), fstage.at[t, 0], fbuf.at[t, 0], ydev(1))
        cp.arrive(("b", t), hbuf.at[t, 1], ydev(3))
        fstage[t, 1, 0:half] = own[t, (y + 3) % 4, 0:half].astype(jnp.bfloat16)
        fstage[t, 1, half:WR] = (own[t, (y + 3) % 4, half:WR] + hbuf[t, 1].astype(jnp.float32)).astype(jnp.bfloat16)
        cp.start(("l", t), fstage.at[t, 1], fbuf.at[t, 1], ydev(3))

    def home(t):
        cp.arrive(("r", t), fbuf.at[t, 0], ydev(1))
        cp.arrive(("l", t), fbuf.at[t, 1], ydev(3))
        total = own[t, y] + fbuf[t, 0].astype(jnp.float32) + fbuf[t, 1].astype(jnp.float32)
        if order[t] == 0:
            own[t, 0] = total
        else:
            zstage[t] = total.astype(jnp.bfloat16)
            cp.start(("z", t), zstage.at[t], zbuf.at[t], zdev(order[t]))

    for t in range(8 + 3):
        for delay, stage in ((0, compute), (1, meet), (2, pass_on), (3, home)):
            if 0 <= t - delay < 8:
                stage(t - delay)

    total = own[7, 0]
    for t in range(7):
        cp.arrive(("z", t), zbuf.at[t], zdev(order[t]))
        total = total + zbuf[t].astype(jnp.float32)
    grad_ref[...] = total
    cp.drain()


def finish_kernel(att_ref, grad_ref, out_ref, gq_ref, gk_ref, gv_ref):
    out_ref[...] = att_ref[...]
    gq_ref[...] = grad_ref[0:DH].T
    gk_ref[...] = grad_ref[DH:DH + 32].T
    gv_ref[...] = grad_ref[DH + 32:WR].T


def block(h, gain, wq, wk, wv, g, docs, fine, coarse):
    vmem, hbm = pl.BlockSpec(memory_space=pltpu.VMEM), pl.BlockSpec(memory_space=pl.ANY)
    bf, f32, nb = jnp.bfloat16, jnp.float32, SEQ // KB
    att, grad = pl.pallas_call(
        block_kernel,
        out_shape=(jax.ShapeDtypeStruct((SEQ, DH), bf), jax.ShapeDtypeStruct((WR, WF), f32)),
        in_specs=[hbm] * 9,
        out_specs=(vmem,) * 2,
        scratch_shapes=[
            pltpu.VMEM((TB, D), bf),
            pltpu.VMEM((1, D), f32),
            pltpu.VMEM((WF, DH), bf),
            pltpu.VMEM((WF, 32), bf),
            pltpu.VMEM((WF, 32), bf),
            pltpu.VMEM((SEQ, DH), bf),
            pltpu.VMEM((1, SEQ), jnp.int32),
            pltpu.VMEM((2, TB, DH), f32),
            pltpu.VMEM((2, 16, DH), f32),
            pltpu.VMEM((WR, WF), bf),
            pltpu.VMEM((4, TB, D), bf),
            pltpu.VMEM((4, 4, TB, 3 * DH), bf),
            pltpu.VMEM((4, WR, D), bf),
            pltpu.VMEM((2 * TB, 6 * DH), f32),
            pltpu.VMEM((4, 3, TB, 3 * DH), bf),
            pltpu.VMEM((nb, DH, KB), bf),
            pltpu.VMEM((nb, DH, KB), bf),
            pltpu.VMEM((nb, KB, QB), f32),
            pltpu.VMEM((nb, KB, QB), bf),
            pltpu.VMEM((DH, QB), f32),
            pltpu.VMEM((SEQ, DH), f32),
            pltpu.VMEM((SEQ, DH), f32),
            pltpu.VMEM((4, 4, TB, 3 * DH), bf),
            pltpu.SemaphoreType.DMA((4, 3)),
            pltpu.SemaphoreType.DMA((4, 3)),
            pltpu.VMEM((3, 4, TB, 3 * DH), bf),
            pltpu.VMEM((4, WR, 4 * TB), bf),
            pltpu.VMEM((8, 4, WR, WF), f32),
            pltpu.VMEM((8, 4, WR, WF), bf),
            pltpu.VMEM((8, 4, WR, WF), bf),
            pltpu.VMEM((8, 2, WR // 2, WF), bf),
            pltpu.VMEM((8, 2, WR // 2, WF), bf),
            pltpu.VMEM((8, 2, WR, WF), bf),
            pltpu.VMEM((8, 2, WR, WF), bf),
            pltpu.VMEM((7, WR, WF), bf),
            pltpu.VMEM((7, WR, WF), bf),
            pltpu.SemaphoreType.DMA((SEMS,)),
            pltpu.SemaphoreType.DMA((SEMS,)),
            pltpu.SemaphoreType.DMA((9,)),
        ],
        compiler_params=pltpu.CompilerParams(vmem_limit_bytes=62 << 20, collective_id=0, has_side_effects=True),
        name="block",
    )(h, gain, wq, wk, wv, g, docs, fine, coarse)
    return pl.pallas_call(
        finish_kernel,
        out_shape=(jax.ShapeDtypeStruct((SEQ, DH), bf),) + tuple(jax.ShapeDtypeStruct((WF, w), f32) for w in (DH, 32, 32)),
        in_specs=[vmem] * 2,
        out_specs=(vmem,) * 4,
        name="finish",
    )(att, grad)


def local(hidden_states, norm_gain, w_query, w_key, w_value, out_grad, short_docs):
    fine, coarse = (jnp.asarray(t) for t in rope_tables())
    att, gq, gk, gv = block(hidden_states.reshape(TB, D), norm_gain.reshape(1, D), w_query, w_key, w_value,
                            out_grad.reshape(SEQ, DH), short_docs, fine, coarse)
    return att.reshape(1, 1, SEQ, DH), gq, gk, gv


def solution(mesh):
    both = ("bucket", "fsdp")
    return jax.shard_map(
        local,
        mesh=mesh,
        in_specs=(P("bucket", "fsdp", "sp", None), P(), P(both, "sp"), P(both, "sp"), P(both, "sp"),
                  P("bucket", "fsdp", None, "sp"), P("fsdp", None)),
        out_specs=(P("bucket", "fsdp", None, "sp"), P(both, "sp"), P(both, "sp"), P(both, "sp")),
        check_vma=False,
    )
```

```python
import math
import functools
import numpy as np
import jax
import jax.numpy as jnp
from jax import lax
from jax.experimental import pallas as pl
from jax.experimental.pallas import tpu as pltpu
from jax.sharding import PartitionSpec as P

MESH = pl.DeviceIdType.MESH

DH = 128
SEQ = 2048
QB = 512
KB = 512
NEG = -1e30
SCALE = 1.0 / math.sqrt(DH)
EXP_C = SCALE * math.log2(math.e)


def rope_tables():
    freq = np.float32(500000.0) ** (-2.0 * np.arange(64, dtype=np.float32) / DH)
    freq = np.repeat(freq.astype(np.float64), 2)[None, :]
    sign = np.where(np.arange(DH) % 2 == 0, -1.0, 1.0)[None, :]
    fine = np.arange(128)[:, None] * freq
    coarse = 128 * np.arange(16)[:, None] * freq
    f = np.stack([np.cos(fine), np.sin(fine) * sign]).astype(np.float32)
    c = np.stack([np.cos(coarse), np.sin(coarse) * sign]).astype(np.float32)
    return f, c


def rope_block(fine_ref, coarse_ref, block):
    cf, sf = fine_ref[0], fine_ref[1]
    cc = coarse_ref[0, pl.ds(block, 1), :]
    sc = coarse_ref[1, pl.ds(block, 1), :]
    return cf * cc - sf * sc, sf * cc + cf * sc


def swap_pairs(x):
    lane = lax.broadcasted_iota(jnp.int32, x.shape, 1)
    return jnp.where(lane % 2 == 0, pltpu.roll(x, DH - 1, 1), pltpu.roll(x, 1, 1))


def nn(a, b):
    return jnp.dot(a, b, preferred_element_type=jnp.float32)


def nt(a, b):
    return lax.dot_general(a, b, (((1,), (1,)), ((), ())), preferred_element_type=jnp.float32)


D = 4096
TB = 128
WR = 192
WF = 256
EPS = 1e-5
RA, HA, HB = 112, 48, 32
R1, H1 = 144, 64


class Copies:
    def __init__(self, send, recv):
        self.send, self.recv, self.ids, self.live = send, recv, {}, []

    def make(self, key, src, dst, dev):
        i = self.ids.setdefault(key, len(self.ids))
        return pltpu.make_async_remote_copy(src_ref=src, dst_ref=dst, send_sem=self.send.at[i], recv_sem=self.recv.at[i],
                                            device_id=dev, device_id_type=MESH)

    def start(self, key, src, dst, dev):
        copy = self.make(key, src, dst, dev)
        copy.start()
        self.live.append(copy)

    def arrive(self, key, dst, dev):
        self.make(key, dst, dst, dev).wait_recv()

    def drain(self):
        for copy in self.live:
            copy.wait_send()


def place():
    c, z, sp = lax.axis_index("bucket"), lax.axis_index("fsdp"), lax.axis_index("sp")
    return c, z, sp // 4, sp % 4


def greet(devs):
    barrier = pltpu.get_barrier_semaphore()
    for dev in devs:
        pl.semaphore_signal(barrier, inc=1, device_id=dev, device_id_type=MESH)
    return lambda: pl.semaphore_wait(barrier, len(devs))


SEMS = 7 + 32 + 4 + 28 + 16 + 12 + 12 + 8 + 32 + 7 + 10


class Part:
    def __init__(self, ref, part):
        self.ref, self.part = ref, part

    def __getitem__(self, index):
        return self.ref[index[0], self.part * DH:(self.part + 1) * DH]


def block_kernel(h_hbm, gain_hbm, wq_hbm, wk_hbm, wv_hbm, g_hbm, docs_hbm, fine_hbm, coarse_hbm, att_ref, grad_ref,
                 h_ref, gain_ref, wq_ref, wk_ref, wv_ref, g_ref, docs_ref, fine_ref, coarse_ref, w_ref,
                 n_ref, qkv4_ref, wbuf, pacc, stage,
                 kt, vt, s_scr, p_scr, acc, dk_acc, dv_acc, d_scr, dsend, drecv,
                 rbuf, dt, own, cstage, cbuf, hstage, hbuf, fstage, fbuf, zstage, zbuf, rstage2, rbuf2, ystage, ybuf, ssem, rsem, lsem):
    loads = {}
    for name, src, dst in (("h", h_hbm, h_ref), ("gain", gain_hbm, gain_ref), ("wq", wq_hbm, wq_ref), ("wk", wk_hbm, wk_ref),
                           ("wv", wv_hbm, wv_ref), ("fine", fine_hbm, fine_ref), ("coarse", coarse_hbm, coarse_ref),
                           ("g", g_hbm, g_ref), ("docs", docs_hbm, docs_ref)):
        loads[name] = pltpu.make_async_copy(src, dst, lsem.at[len(loads)])
        loads[name].start()
    c, z, x, y = place()
    xdev = lambda d: {"sp": (x + d) % 4 * 4 + y}
    ydev = lambda d: {"sp": x * 4 + (y + d) % 4}
    zdev = lambda d: {"fsdp": (z + d) % 8}
    other = {"bucket": 1 - c}
    wait_all = greet([xdev(1), xdev(3), ydev(1), ydev(2), ydev(3), other] + [zdev(d) for d in range(1, 8)])
    qkv_ref = qkv4_ref

    def wslot(core, zz, yy, lo=0, size=WR):
        col = pl.multiple_of((core * 8 + zz % 8) * WF, WF)
        return wbuf.at[yy % 4, pl.ds(lo, size), pl.ds(col, WF)]

    for name in ("wq", "wk", "wv"):
        loads[name].wait()
    w_ref[0:DH] = wq_ref[...].T
    w_ref[DH:DH + 32] = wk_ref[...]
    w_ref[DH + 32:WR] = wv_ref[...]
    wslot(c, z, y)[...] = w_ref[...]
    loads["h"].wait()
    loads["gain"].wait()
    for r in range(0, TB, 32):
        rows = h_ref[r:r + 32, :].astype(jnp.float32)
        inv = lax.rsqrt(jnp.mean(rows * rows, axis=1, keepdims=True) + EPS)
        n_ref[x, r:r + 32, :] = (rows * inv * gain_ref[...]).astype(jnp.bfloat16)
    wait_all()
    cp = Copies(ssem, rsem)
    zoff = [0, -1, -2, -3, -4, 1, 2, 3]
    yoff = [0, 3, 1, 2]

    def spread(zi):
        src = w_ref.at[pl.ds(0, RA), :] if zi == 0 else wslot(c, z + zoff[zi], y, 0, RA)
        dst = wslot(c, z + zoff[zi], y, 0, RA)
        cp.start(("yr", zi), src, dst, ydev(1))
        cp.start(("yl", zi), src, dst, ydev(3))

    def serve(zi):
        zz = z + zoff[zi]
        cp.arrive(("yr", zi), wslot(c, zz, y + 3, 0, RA), ydev(1))
        part = wslot(c, zz, y + 3, 0, HA)
        cp.start(("ya", zi), part, part, ydev(1))
        cp.arrive(("yl", zi), wslot(c, zz, y + 1, 0, RA), ydev(3))
        part = wslot(c, zz, y + 1, HA, RA - HA)
        cp.start(("yb", zi), part, part, ydev(3))

    def wall(core, zz, lo, size):
        col = pl.multiple_of((core * 8 + zz % 8) * WF, WF)
        return wbuf.at[:, pl.ds(lo, size), pl.ds(col, WF)]

    def last(zi):
        zz = z + zoff[zi]
        cp.arrive(("ya", zi), wslot(c, zz, y + 2, 0, HA), ydev(1))
        cp.arrive(("yb", zi), wslot(c, zz, y + 2, HA, RA - HA), ydev(3))
        cp.start(("ca", zi), wall(c, zz, 0, RA), wall(c, zz, 0, RA), other)

    def chain(yk, step, right):
        n = 4 if right == (yk < 2) else 3
        if step > n:
            return
        zz = z - step if right else z + step
        name = "br" if right else "bl"
        part = wslot(c, zz, y + yoff[yk], RA, WR - RA)
        if step > 0:
            cp.arrive((name, yk, step), part, zdev(1 if right else 7))
        if step < n:
            src = w_ref.at[pl.ds(RA, WR - RA), :] if yk == 0 and step == 0 else part
            cp.start((name, yk, step + 1), src, part, zdev(1 if right else 7))

    def npiece(xx, p):
        return n_ref.at[xx % 4, pl.ds(p * 32, 32), :]

    for p in range(4):
        cp.start(("xr", p), npiece(x, p), npiece(x, p), xdev(1))
        cp.start(("xl", 3 - p), npiece(x, 3 - p), npiece(x, 3 - p), xdev(3))
    own_a, own_b = w_ref.at[pl.ds(0, RA), :], w_ref.at[pl.ds(RA, WR - RA), :]
    cp.start(("zr", 1), own_a, wslot(c, z, y, 0, RA), zdev(1))
    cp.start(("zl", 1), own_a, wslot(c, z, y, 0, RA), zdev(7))
    cp.start(("er", 0), own_b, wslot(c, z, y, RA, WR - RA), ydev(1))
    cp.start(("el", 0), own_b, wslot(c, z, y, RA, WR - RA), ydev(3))
    spread(0)
    chain(0, 0, True)
    chain(0, 0, False)
    cp.arrive(("er", 0), wslot(c, z, y + 3, RA, WR - RA), ydev(1))
    part = wslot(c, z, y + 3, RA, HB)
    cp.start(("ea", 0), part, part, ydev(1))
    chain(1, 0, True)
    chain(1, 0, False)
    cp.arrive(("el", 0), wslot(c, z, y + 1, RA, WR - RA), ydev(3))
    part = wslot(c, z, y + 1, RA + HB, WR - RA - HB)
    cp.start(("eb", 0), part, part, ydev(3))
    chain(2, 0, True)
    chain(2, 0, False)

    def relay_x(p):
        cp.arrive(("xr", p), npiece(x + 3, p), xdev(1))
        cp.start(("xa", p), npiece(x + 3, p), npiece(x + 3, p), xdev(1))
        cp.arrive(("xl", 3 - p), npiece(x + 1, 3 - p), xdev(3))
        cp.start(("xb", 3 - p), npiece(x + 1, 3 - p), npiece(x + 1, 3 - p), xdev(3))

    def core_b(zi):
        zz = z + zoff[zi]
        cp.start(("cb", zi), wall(c, zz, RA, WR - RA), wall(c, zz, RA, WR - RA), other)

    done, waiting = [0], []
    for step in range(1, 5):
        src = wslot(c, z - step, y, 0, RA)
        cp.arrive(("zr", step), src, zdev(1))
        if step < 4:
            cp.start(("zr", step + 1), src, src, zdev(1))
        spread(step)
        fresh = [step]
        if step < 4:
            src = wslot(c, z + step, y, 0, RA)
            cp.arrive(("zl", step), src, zdev(7))
            if step < 3:
                cp.start(("zl", step + 1), src, src, zdev(7))
            spread(4 + step)
            fresh.append(4 + step)
        if step == 1:
            cp.arrive(("ea", 0), wslot(c, z, y + 2, RA, HB), ydev(1))
            cp.arrive(("eb", 0), wslot(c, z, y + 2, RA + HB, WR - RA - HB), ydev(3))
            chain(3, 0, True)
            chain(3, 0, False)
            core_b(0)
        for zi in done:
            serve(zi)
        for yk in range(4):
            chain(yk, step, True)
            chain(yk, step, False)
        core_b(step)
        if step < 4:
            core_b(4 + step)
        for zi in waiting:
            last(zi)
        waiting, done = done, fresh
        if step == 3:
            relay_x(0)
            relay_x(1)
    for zi in done:
        serve(zi)
    for zi in waiting + done:
        last(zi)
    for zi in range(8):
        cp.arrive(("ca", zi), wall(1 - c, z + zoff[zi], 0, RA), other)
        cp.arrive(("cb", zi), wall(1 - c, z + zoff[zi], RA, WR - RA), other)

    lane = lax.broadcasted_iota(jnp.int32, (TB, DH), 1)

    def project(offsets, first):
        rows = len(offsets) * TB
        pacc[0:rows, :] = jnp.zeros((rows, 6 * DH), jnp.float32)

        @pl.loop(0, D // 512)
        def _(f):
            cols = pl.ds(pl.multiple_of(f * 512, 512), 512)
            lhs = jnp.concatenate([n_ref[(x + d) % 4, :, cols] for d in offsets], axis=0)
            rhs = jnp.concatenate([wbuf[yy, 0:DH, cols] for yy in range(4)] + [wbuf[yy, DH:WR, cols] for yy in range(4)], axis=0)
            pacc[0:rows, :] += nt(lhs, rhs)

        for n, d in enumerate(offsets):
            i = first + n
            xx = (x + d) % 4
            r = pl.ds(n * TB, TB)
            cos, sin = rope_block(fine_ref, coarse_ref, 4 * xx + y)
            turn = lambda t: (t * cos + swap_pairs(t) * sin).astype(jnp.bfloat16)
            a, b = pacc[r, 4 * DH:5 * DH], pacc[r, 5 * DH:6 * DH]
            pick = lambda p0, p1, p2, p3: jnp.where(lane < 32, p0, jnp.where(lane < 64, p1, jnp.where(lane < 96, p2, p3)))
            key = turn(pick(a, pltpu.roll(a, 96, 1), pltpu.roll(b, 64, 1), pltpu.roll(b, 32, 1)))
            val = pick(pltpu.roll(a, 96, 1), pltpu.roll(a, 64, 1), pltpu.roll(b, 32, 1), b).astype(jnp.bfloat16)
            for dy in range(4):
                q = turn(pacc[r, pl.ds(pl.multiple_of((y + dy) % 4 * DH, DH), DH)])
                dst = qkv_ref.at[xx, y] if dy == 0 else stage.at[i, dy - 1]
                dst[:, 0:DH] = q
                dst[:, DH:2 * DH] = key
                dst[:, 2 * DH:3 * DH] = val
            for dy in (2, 1, 3):
                cp.start(("q", i, dy), stage.at[i, dy - 1], qkv_ref.at[xx, y], ydev(dy))

    loads["fine"].wait()
    loads["coarse"].wait()
    project((0,), 0)
    for p in (2, 3):
        cp.arrive(("xr", p), npiece(x + 3, p), xdev(1))
        cp.arrive(("xl", 3 - p), npiece(x + 1, 3 - p), xdev(3))
    project((3, 1), 1)
    for p in (0, 1):
        cp.arrive(("xa", p), npiece(x + 2, p), xdev(1))
        cp.arrive(("xb", 3 - p), npiece(x + 2, 3 - p), xdev(3))
    project((2,), 3)
    for i, d in enumerate((0, 3, 1, 2)):
        for dy in range(1, 4):
            cp.arrive(("q", i, dy), qkv_ref.at[(x + d) % 4, (y - dy) % 4], ydev(dy))


    q_ref, k_ref, v_ref = (Part(qkv_ref.reshape(SEQ, 3 * DH), part) for part in range(3))
    loads["g"].wait()
    loads["docs"].wait()

    def exchange(i, dy):
        return pltpu.make_async_remote_copy(
            src_ref=d_scr.at[i, (y + dy) % 4], dst_ref=rbuf.at[dy - 1, i], send_sem=dsend.at[i, dy - 1],
            recv_sem=drecv.at[i, dy - 1], device_id=ydev(dy), device_id_type=MESH)

    @pl.loop(0, SEQ // KB)
    def _(j):
        rows = pl.ds(pl.multiple_of(j * KB, KB), KB)
        kt[j] = k_ref[rows, :].T
        vt[j] = v_ref[rows, :].T

    dk_acc[...] = jnp.zeros_like(dk_acc)
    dv_acc[...] = jnp.zeros_like(dv_acc)

    def finish_query(i, dqt):
        dq = dqt.T * SCALE
        for half in range(QB // 128):
            block = i * (QB // 128) + half
            cos, sin = rope_block(fine_ref, coarse_ref, block)
            x = dq[half * 128:(half + 1) * 128]
            rows = pl.ds(pl.multiple_of(block * 128, 128), 128)
            d_scr[i, half, :, 0:DH] = (x * cos - swap_pairs(x) * sin).astype(jnp.bfloat16)
            d_scr[i, half, :, DH:2 * DH] = (dk_acc[rows, :] * SCALE).astype(jnp.bfloat16)
            d_scr[i, half, :, 2 * DH:3 * DH] = dv_acc[rows, :].astype(jnp.bfloat16)
        for dy in (2, 1, 3):
            exchange(i, dy).start()

    @pl.when(c == 0)
    def _():
        @pl.loop(0, SEQ // QB)
        def _(step):
            i = SEQ // QB - 1 - step
            qrows = pl.ds(pl.multiple_of(i * QB, QB), QB)
            q = q_ref[qrows, :]
            g = g_ref[qrows, :]

            def scores(j):
                return nt(k_ref[pl.ds(pl.multiple_of(j * KB, KB), KB), :], q)

            def pass1(j, m):
                s = scores(j)
                s_scr[j] = s
                return jnp.maximum(m, jnp.max(s.reshape(KB // 8, 8, QB), axis=0))

            m8 = lax.fori_loop(0, i, pass1, jnp.full((8, QB), NEG, jnp.float32))
            s = scores(i)
            key = lax.broadcasted_iota(jnp.int32, (KB, QB), 0)
            qry = lax.broadcasted_iota(jnp.int32, (KB, QB), 1)
            s = jnp.where(key <= qry, s, NEG)
            s_scr[i] = s
            m8 = jnp.maximum(m8, jnp.max(s.reshape(KB // 8, 8, QB), axis=0))
            m = jnp.max(m8, axis=0, keepdims=True)
            acc[...] = jnp.zeros_like(acc)

            def pass2(j, l8):
                p = jnp.exp2((s_scr[j] - m) * EXP_C)
                pb = p.astype(jnp.bfloat16)
                p_scr[j] = pb
                acc[...] += nn(vt[j], pb)
                return l8 + jnp.sum(p.reshape(KB // 8, 8, QB), axis=0)

            l8 = lax.fori_loop(0, i + 1, pass2, jnp.zeros((8, QB), jnp.float32))
            rl = 1.0 / jnp.sum(l8, axis=0, keepdims=True)
            ot = acc[...] * rl
            att_ref[qrows, :] = ot.T.astype(jnp.bfloat16)
            gt = (g.astype(jnp.float32).T * rl).astype(jnp.bfloat16)
            gs = gt.T
            d = jnp.sum(ot * gt.astype(jnp.float32), axis=0, keepdims=True)
            acc[...] = jnp.zeros_like(acc)

            @pl.loop(0, i + 1)
            def _(j):
                krows = pl.ds(pl.multiple_of(j * KB, KB), KB)
                pb = p_scr[j]
                dp = nn(v_ref[krows, :], gt)
                ds = (pb.astype(jnp.float32) * (dp - d)).astype(jnp.bfloat16)
                acc[...] += nn(kt[j], ds)
                dk_acc[krows, :] += nn(ds, q)
                dv_acc[krows, :] += nn(pb, gs)

            finish_query(i, acc[...])

    @pl.when(c == 1)
    def _():
        span = QB + 128

        @pl.loop(0, SEQ // QB)
        def _(step):
            i = SEQ // QB - 1 - step
            qrows = pl.ds(pl.multiple_of(i * QB, QB), QB)
            first = pl.multiple_of(jnp.maximum(i * QB - 128, 0), 128)
            krows = pl.ds(first, span)
            q = q_ref[qrows, :]
            g = g_ref[qrows, :]
            k = k_ref[krows, :]
            v = v_ref[krows, :]
            key = lax.broadcasted_iota(jnp.int32, (span, QB), 0) + first
            qry = lax.broadcasted_iota(jnp.int32, (span, QB), 1) + i * QB
            def docs(start, size):
                rows = [docs_ref[:, pl.ds(pl.multiple_of(start + o, 128), 128)] for o in range(0, size, 128)]
                return jnp.concatenate(rows, axis=1).astype(jnp.float32)

            same = jnp.broadcast_to(docs(first, span), (128, span)).T[:, 0:1] == docs(i * QB, QB)
            s = jnp.where((key <= qry) & same, nt(k, q), NEG)
            m = jnp.max(s, axis=0, keepdims=True)
            p = jnp.exp2((s - m) * EXP_C)
            rl = 1.0 / jnp.sum(p, axis=0, keepdims=True)
            pb = p.astype(jnp.bfloat16)
            ot = nn(v.T, pb) * rl
            att_ref[qrows, :] = ot.T.astype(jnp.bfloat16)
            gt = (g.astype(jnp.float32).T * rl).astype(jnp.bfloat16)
            gs = gt.T
            d = jnp.sum(ot * gt.astype(jnp.float32), axis=0, keepdims=True)
            dp = nn(v, gt)
            ds = (pb.astype(jnp.float32) * (dp - d)).astype(jnp.bfloat16)
            dk_acc[krows, :] += nn(ds, q)
            dv_acc[krows, :] += nn(pb, gs)
            finish_query(i, nn(k.T, ds))

    for i in (3, 2, 1, 0):
        for dy in range(1, 4):
            exchange(i, dy).wait()

    for i in range(4):
        cols = pl.ds(i * TB, TB)
        part = [d_scr[i, y]] + [rbuf[dy - 1, i] for dy in range(1, 4)]
        for dy in range(4):
            dt[(y - dy) % 4, 0:DH, cols] = part[dy][:, 0:DH].T
        key, val = (sum(p[:, s * DH:(s + 1) * DH].astype(jnp.float32) for p in part) for s in (1, 2))
        cos, sin = rope_block(fine_ref, coarse_ref, 4 * i + y)
        key = (key * cos - swap_pairs(key) * sin).astype(jnp.bfloat16).T
        val = val.astype(jnp.bfloat16).T
        for yy in range(4):
            dt[yy, DH:DH + 32, cols] = key[yy * 32:(yy + 1) * 32]
            dt[yy, DH + 32:WR, cols] = val[yy * 32:(yy + 1) * 32]

    order = (4, 5, 3, 6, 2, 7, 1, 0)

    def product(core, dz):
        col = pl.multiple_of((core * 8 + (z + dz) % 8) * WF, WF)
        rhs = n_ref[:, :, pl.ds(col, WF)].reshape(4 * TB, WF)
        return nn(dt[...].reshape(4 * WR, 4 * TB), rhs).reshape(4, WR, WF)

    def compute(t):
        cstage[t] = product(1 - c, order[t]).astype(jnp.bfloat16)
        cp.start(("c", t), cstage.at[t], cbuf.at[t], other)
        own[t] = product(c, order[t])

    def meet(t):
        cp.arrive(("c", t), cbuf.at[t], other)
        own[t] += cbuf[t].astype(jnp.float32)
        hstage[t, 0, 0:H1] = own[t, (y + 2) % 4, 0:H1].astype(jnp.bfloat16)
        hstage[t, 1] = own[t, (y + 2) % 4, H1:R1].astype(jnp.bfloat16)
        cp.start(("a", t), hstage.at[t, 0, pl.ds(0, H1)], hbuf.at[t, 0, pl.ds(0, H1)], ydev(1))
        cp.start(("b", t), hstage.at[t, 1], hbuf.at[t, 1], ydev(3))
        if order[t] in (4, 5):
            ring(t, "n", own[t, :, R1:WR], rstage2, rbuf2)

    def ring(t, kind, value, sent, got):
        dz = order[t]
        right = dz <= 4
        step = 4 - dz if right else dz - 5
        name, peer, first = (kind + "r", zdev(1), 0) if right else (kind + "l", zdev(7), 4)
        if step > 0:
            cp.arrive((name, step - 1), got.at[first + step - 1], peer)
            value = value + got[first + step - 1].astype(jnp.float32)
        sent[first + step] = value.astype(jnp.bfloat16)
        cp.start((name, step), sent.at[first + step], got.at[first + step], peer)

    def ring_end(kind, got):
        cp.arrive((kind + "r", 3), got.at[3], zdev(1))
        cp.arrive((kind + "l", 2), got.at[6], zdev(7))
        return got[3].astype(jnp.float32) + got[6].astype(jnp.float32)

    def pass_on(t):
        cp.arrive(("a", t), hbuf.at[t, 0, pl.ds(0, H1)], ydev(1))
        fstage[t, 0, 0:H1] = (own[t, (y + 1) % 4, 0:H1] + hbuf[t, 0, 0:H1].astype(jnp.float32)).astype(jnp.bfloat16)
        fstage[t, 0, H1:R1] = own[t, (y + 1) % 4, H1:R1].astype(jnp.bfloat16)
        cp.start(("r", t), fstage.at[t, 0], fbuf.at[t, 0], ydev(1))
        cp.arrive(("b", t), hbuf.at[t, 1], ydev(3))
        fstage[t, 1, 0:H1] = own[t, (y + 3) % 4, 0:H1].astype(jnp.bfloat16)
        fstage[t, 1, H1:R1] = (own[t, (y + 3) % 4, H1:R1] + hbuf[t, 1].astype(jnp.float32)).astype(jnp.bfloat16)
        cp.start(("l", t), fstage.at[t, 1], fbuf.at[t, 1], ydev(3))
        if order[t] not in (0, 4, 5):
            ring(t, "n", own[t, :, R1:WR], rstage2, rbuf2)

    def home(t):
        cp.arrive(("r", t), fbuf.at[t, 0], ydev(1))
        cp.arrive(("l", t), fbuf.at[t, 1], ydev(3))
        total = own[t, y, 0:R1] + fbuf[t, 0].astype(jnp.float32) + fbuf[t, 1].astype(jnp.float32)
        if order[t] == 0:
            grad_ref[0:R1] = total
        else:
            ring(t, "m", total, zstage, zbuf)

    for t in range(8 + 6):
        for delay, part in ((0, compute), (2, meet), (4, pass_on), (6, home)):
            if 0 <= t - delay < 8:
                part(t - delay)

    own[7, :, R1:WR] += ring_end("n", rbuf2)
    for dy in (2, 1, 3):
        ystage[dy - 1] = own[7, (y + dy) % 4, R1:WR].astype(jnp.bfloat16)
        cp.start(("v", dy), ystage.at[dy - 1], ybuf.at[dy - 1], ydev(dy))
    grad_ref[0:R1] += ring_end("m", zbuf)
    total = own[7, y, R1:WR]
    for dy in (1, 3, 2):
        cp.arrive(("v", dy), ybuf.at[dy - 1], ydev(dy))
        total = total + ybuf[dy - 1].astype(jnp.float32)
    grad_ref[R1:WR] = total
    cp.drain()


def finish_kernel(att_ref, grad_ref, out_ref, gq_ref, gk_ref, gv_ref):
    out_ref[...] = att_ref[...]
    gq_ref[...] = grad_ref[0:DH].T
    gk_ref[...] = grad_ref[DH:DH + 32]
    gv_ref[...] = grad_ref[DH + 32:WR]


def block(h, gain, wq, wk, wv, g, docs, fine, coarse):
    vmem, hbm = pl.BlockSpec(memory_space=pltpu.VMEM), pl.BlockSpec(memory_space=pl.ANY)
    bf, f32, nb = jnp.bfloat16, jnp.float32, SEQ // KB
    att, grad = pl.pallas_call(
        block_kernel,
        out_shape=(jax.ShapeDtypeStruct((SEQ, DH), bf), jax.ShapeDtypeStruct((WR, WF), f32)),
        in_specs=[hbm] * 9,
        out_specs=(vmem,) * 2,
        scratch_shapes=[
            pltpu.VMEM((TB, D), bf),
            pltpu.VMEM((1, D), f32),
            pltpu.VMEM((WF, DH), bf),
            pltpu.VMEM((32, WF), bf),
            pltpu.VMEM((32, WF), bf),
            pltpu.VMEM((SEQ, DH), bf),
            pltpu.VMEM((1, SEQ), jnp.int32),
            pltpu.VMEM((2, TB, DH), f32),
            pltpu.VMEM((2, 16, DH), f32),
            pltpu.VMEM((WR, WF), bf),
            pltpu.VMEM((4, TB, D), bf),
            pltpu.VMEM((4, 4, TB, 3 * DH), bf),
            pltpu.VMEM((4, WR, D), bf),
            pltpu.VMEM((2 * TB, 6 * DH), f32),
            pltpu.VMEM((4, 3, TB, 3 * DH), bf),
            pltpu.VMEM((nb, DH, KB), bf),
            pltpu.VMEM((nb, DH, KB), bf),
            pltpu.VMEM((nb, KB, QB), f32),
            pltpu.VMEM((nb, KB, QB), bf),
            pltpu.VMEM((DH, QB), f32),
            pltpu.VMEM((SEQ, DH), f32),
            pltpu.VMEM((SEQ, DH), f32),
            pltpu.VMEM((4, 4, TB, 3 * DH), bf),
            pltpu.SemaphoreType.DMA((4, 3)),
            pltpu.SemaphoreType.DMA((4, 3)),
            pltpu.VMEM((3, 4, TB, 3 * DH), bf),
            pltpu.VMEM((4, WR, 4 * TB), bf),
            pltpu.VMEM((8, 4, WR, WF), f32),
            pltpu.VMEM((8, 4, WR, WF), bf),
            pltpu.VMEM((8, 4, WR, WF), bf),
            pltpu.VMEM((8, 2, R1 - H1, WF), bf),
            pltpu.VMEM((8, 2, R1 - H1, WF), bf),
            pltpu.VMEM((8, 2, R1, WF), bf),
            pltpu.VMEM((8, 2, R1, WF), bf),
            pltpu.VMEM((7, R1, WF), bf),
            pltpu.VMEM((7, R1, WF), bf),
            pltpu.VMEM((7, 4, WR - R1, WF), bf),
            pltpu.VMEM((7, 4, WR - R1, WF), bf),
            pltpu.VMEM((3, WR - R1, WF), bf),
            pltpu.VMEM((3, WR - R1, WF), bf),
            pltpu.SemaphoreType.DMA((SEMS,)),
            pltpu.SemaphoreType.DMA((SEMS,)),
            pltpu.SemaphoreType.DMA((9,)),
        ],
        compiler_params=pltpu.CompilerParams(vmem_limit_bytes=62 << 20, collective_id=0, has_side_effects=True),
        name="block",
    )(h, gain, wq, wk, wv, g, docs, fine, coarse)
    return pl.pallas_call(
        finish_kernel,
        out_shape=(jax.ShapeDtypeStruct((SEQ, DH), bf),) + tuple(jax.ShapeDtypeStruct(s, f32) for s in ((WF, DH), (32, WF), (32, WF))),
        in_specs=[vmem] * 2,
        out_specs=(vmem,) * 4,
        name="finish",
    )(att, grad)


def local(hidden_states, norm_gain, w_query, w_key, w_value, out_grad, short_docs):
    fine, coarse = (jnp.asarray(t) for t in rope_tables())
    att, gq, gk, gv = block(hidden_states.reshape(TB, D), norm_gain.reshape(1, D), w_query, w_key.T, w_value.T,
                            out_grad.reshape(SEQ, DH), short_docs, fine, coarse)
    return att.reshape(1, 1, SEQ, DH), gq, gk.T, gv.T


def solution(mesh):
    both = ("bucket", "fsdp")
    return jax.shard_map(
        local,
        mesh=mesh,
        in_specs=(P("bucket", "fsdp", "sp", None), P(), P(both, "sp"), P(both, "sp"), P(both, "sp"),
                  P("bucket", "fsdp", None, "sp"), P("fsdp", None)),
        out_specs=(P("bucket", "fsdp", None, "sp"), P(both, "sp"), P(both, "sp"), P(both, "sp")),
        check_vma=False,
    )
```

```python
import math
import functools
import numpy as np
import jax
import jax.numpy as jnp
from jax import lax
from jax.experimental import pallas as pl
from jax.experimental.pallas import tpu as pltpu
from jax.sharding import PartitionSpec as P

MESH = pl.DeviceIdType.MESH

DH = 128
SEQ = 2048
QB = 512
KB = 512
NEG = -1e30
SCALE = 1.0 / math.sqrt(DH)
EXP_C = SCALE * math.log2(math.e)


def rope_tables():
    freq = np.float32(500000.0) ** (-2.0 * np.arange(64, dtype=np.float32) / DH)
    freq = np.repeat(freq.astype(np.float64), 2)[None, :]
    sign = np.where(np.arange(DH) % 2 == 0, -1.0, 1.0)[None, :]
    fine = np.arange(128)[:, None] * freq
    coarse = 128 * np.arange(16)[:, None] * freq
    f = np.stack([np.cos(fine), np.sin(fine) * sign]).astype(np.float32)
    c = np.stack([np.cos(coarse), np.sin(coarse) * sign]).astype(np.float32)
    return f, c


def rope_block(fine_ref, coarse_ref, block):
    cf, sf = fine_ref[0], fine_ref[1]
    cc = coarse_ref[0, pl.ds(block, 1), :]
    sc = coarse_ref[1, pl.ds(block, 1), :]
    return cf * cc - sf * sc, sf * cc + cf * sc


def swap_pairs(x):
    lane = lax.broadcasted_iota(jnp.int32, x.shape, 1)
    return jnp.where(lane % 2 == 0, pltpu.roll(x, DH - 1, 1), pltpu.roll(x, 1, 1))


def nn(a, b):
    return jnp.dot(a, b, preferred_element_type=jnp.float32)


def nt(a, b):
    return lax.dot_general(a, b, (((1,), (1,)), ((), ())), preferred_element_type=jnp.float32)


D = 4096
TB = 128
WR = 192
WF = 256
EPS = 1e-5
RA, HA, HB = 112, 48, 32
R1, H1 = 144, 64


class Copies:
    def __init__(self, send, recv):
        self.send, self.recv, self.ids, self.live = send, recv, {}, []

    def make(self, key, src, dst, dev):
        i = self.ids.setdefault(key, len(self.ids))
        return pltpu.make_async_remote_copy(src_ref=src, dst_ref=dst, send_sem=self.send.at[i], recv_sem=self.recv.at[i],
                                            device_id=dev, device_id_type=MESH)

    def start(self, key, src, dst, dev):
        copy = self.make(key, src, dst, dev)
        copy.start()
        self.live.append(copy)

    def arrive(self, key, dst, dev):
        self.make(key, dst, dst, dev).wait_recv()

    def drain(self):
        for copy in self.live:
            copy.wait_send()


def place():
    c, z, sp = lax.axis_index("bucket"), lax.axis_index("fsdp"), lax.axis_index("sp")
    return c, z, sp // 4, sp % 4


def greet(devs):
    barrier = pltpu.get_barrier_semaphore()
    for dev in devs:
        pl.semaphore_signal(barrier, inc=1, device_id=dev, device_id_type=MESH)
    return lambda: pl.semaphore_wait(barrier, len(devs))


SEMS = 7 + 32 + 4 + 28 + 16 + 12 + 12 + 8 + 32 + 7 + 10


class Part:
    def __init__(self, ref, part):
        self.ref, self.part = ref, part

    def __getitem__(self, index):
        return self.ref[index[0], self.part * DH:(self.part + 1) * DH]


def block_kernel(h_hbm, gain_hbm, wq_hbm, wk_hbm, wv_hbm, g_hbm, docs_hbm, fine_hbm, coarse_hbm, att_ref, grad_ref,
                 h_ref, gain_ref, wq_ref, wk_ref, wv_ref, g_ref, docs_ref, fine_ref, coarse_ref, w_ref,
                 n_ref, qkv4_ref, wbuf, pacc, stage,
                 kt, vt, s_scr, p_scr, acc, dk_acc, dv_acc, d_scr, dsend, drecv,
                 rbuf, dt, own, cstage, cbuf, hstage, hbuf, fstage, fbuf, zstage, zbuf, rstage2, rbuf2, ystage, ybuf, ssem, rsem, lsem):
    loads = {}
    for name, src, dst in (("h", h_hbm, h_ref), ("gain", gain_hbm, gain_ref), ("wq", wq_hbm, wq_ref), ("wk", wk_hbm, wk_ref),
                           ("wv", wv_hbm, wv_ref), ("fine", fine_hbm, fine_ref), ("coarse", coarse_hbm, coarse_ref),
                           ("g", g_hbm, g_ref), ("docs", docs_hbm, docs_ref)):
        loads[name] = pltpu.make_async_copy(src, dst, lsem.at[len(loads)])
        loads[name].start()
    c, z, x, y = place()
    xdev = lambda d: {"sp": (x + d) % 4 * 4 + y}
    ydev = lambda d: {"sp": x * 4 + (y + d) % 4}
    zdev = lambda d: {"fsdp": (z + d) % 8}
    other = {"bucket": 1 - c}
    wait_all = greet([xdev(1), xdev(3), ydev(1), ydev(2), ydev(3), other] + [zdev(d) for d in range(1, 8)])
    qkv_ref = qkv4_ref

    def wslot(core, zz, yy, lo=0, size=WR):
        col = pl.multiple_of((core * 8 + zz % 8) * WF, WF)
        return wbuf.at[yy % 4, pl.ds(lo, size), pl.ds(col, WF)]

    for name in ("wq", "wk", "wv"):
        loads[name].wait()
    w_ref[0:DH] = wq_ref[...].T
    w_ref[DH:DH + 32] = wk_ref[...]
    w_ref[DH + 32:WR] = wv_ref[...]
    wslot(c, z, y)[...] = w_ref[...]
    loads["h"].wait()
    loads["gain"].wait()
    for r in range(0, TB, 32):
        rows = h_ref[r:r + 32, :].astype(jnp.float32)
        inv = lax.rsqrt(jnp.mean(rows * rows, axis=1, keepdims=True) + EPS)
        n_ref[x, r:r + 32, :] = (rows * inv * gain_ref[...]).astype(jnp.bfloat16)
    wait_all()
    cp = Copies(ssem, rsem)
    zoff = [0, -1, -2, -3, -4, 1, 2, 3]
    yoff = [0, 3, 1, 2]

    def spread(zi):
        src = w_ref.at[pl.ds(0, RA), :] if zi == 0 else wslot(c, z + zoff[zi], y, 0, RA)
        dst = wslot(c, z + zoff[zi], y, 0, RA)
        cp.start(("yr", zi), src, dst, ydev(1))
        cp.start(("yl", zi), src, dst, ydev(3))

    def serve(zi):
        zz = z + zoff[zi]
        cp.arrive(("yr", zi), wslot(c, zz, y + 3, 0, RA), ydev(1))
        part = wslot(c, zz, y + 3, 0, HA)
        cp.start(("ya", zi), part, part, ydev(1))
        cp.arrive(("yl", zi), wslot(c, zz, y + 1, 0, RA), ydev(3))
        part = wslot(c, zz, y + 1, HA, RA - HA)
        cp.start(("yb", zi), part, part, ydev(3))

    def wall(core, zz, lo, size):
        col = pl.multiple_of((core * 8 + zz % 8) * WF, WF)
        return wbuf.at[:, pl.ds(lo, size), pl.ds(col, WF)]

    def last(zi):
        zz = z + zoff[zi]
        cp.arrive(("ya", zi), wslot(c, zz, y + 2, 0, HA), ydev(1))
        cp.arrive(("yb", zi), wslot(c, zz, y + 2, HA, RA - HA), ydev(3))
        cp.start(("ca", zi), wall(c, zz, 0, RA), wall(c, zz, 0, RA), other)

    def chain(yk, step, right):
        n = 4 if right == (yk < 2) else 3
        if step > n:
            return
        zz = z - step if right else z + step
        name = "br" if right else "bl"
        part = wslot(c, zz, y + yoff[yk], RA, WR - RA)
        if step > 0:
            cp.arrive((name, yk, step), part, zdev(1 if right else 7))
        if step < n:
            src = w_ref.at[pl.ds(RA, WR - RA), :] if yk == 0 and step == 0 else part
            cp.start((name, yk, step + 1), src, part, zdev(1 if right else 7))

    def npiece(xx, p):
        return n_ref.at[xx % 4, pl.ds(p * 32, 32), :]

    for p in range(4):
        cp.start(("xr", p), npiece(x, p), npiece(x, p), xdev(1))
        cp.start(("xl", 3 - p), npiece(x, 3 - p), npiece(x, 3 - p), xdev(3))
    own_a, own_b = w_ref.at[pl.ds(0, RA), :], w_ref.at[pl.ds(RA, WR - RA), :]
    cp.start(("zr", 1), own_a, wslot(c, z, y, 0, RA), zdev(1))
    cp.start(("zl", 1), own_a, wslot(c, z, y, 0, RA), zdev(7))
    cp.start(("er", 0), own_b, wslot(c, z, y, RA, WR - RA), ydev(1))
    cp.start(("el", 0), own_b, wslot(c, z, y, RA, WR - RA), ydev(3))
    spread(0)
    chain(0, 0, True)
    chain(0, 0, False)
    cp.arrive(("er", 0), wslot(c, z, y + 3, RA, WR - RA), ydev(1))
    part = wslot(c, z, y + 3, RA, HB)
    cp.start(("ea", 0), part, part, ydev(1))
    chain(1, 0, True)
    chain(1, 0, False)
    cp.arrive(("el", 0), wslot(c, z, y + 1, RA, WR - RA), ydev(3))
    part = wslot(c, z, y + 1, RA + HB, WR - RA - HB)
    cp.start(("eb", 0), part, part, ydev(3))
    chain(2, 0, True)
    chain(2, 0, False)

    def relay_x(p):
        cp.arrive(("xr", p), npiece(x + 3, p), xdev(1))
        cp.start(("xa", p), npiece(x + 3, p), npiece(x + 3, p), xdev(1))
        cp.arrive(("xl", 3 - p), npiece(x + 1, 3 - p), xdev(3))
        cp.start(("xb", 3 - p), npiece(x + 1, 3 - p), npiece(x + 1, 3 - p), xdev(3))

    def core_b(zi):
        zz = z + zoff[zi]
        cp.start(("cb", zi), wall(c, zz, RA, WR - RA), wall(c, zz, RA, WR - RA), other)

    def a_step(step):
        src = wslot(c, z - step, y, 0, RA)
        cp.arrive(("zr", step), src, zdev(1))
        if step < 4:
            cp.start(("zr", step + 1), src, src, zdev(1))
        spread(step)
        if step < 4:
            src = wslot(c, z + step, y, 0, RA)
            cp.arrive(("zl", step), src, zdev(7))
            if step < 3:
                cp.start(("zl", step + 1), src, src, zdev(7))
            spread(4 + step)

    def b_step(step):
        for yk in range(4):
            chain(yk, step, True)
            chain(yk, step, False)
        core_b(step)
        if step < 4:
            core_b(4 + step)

    def each(act, *zis):
        for zi in zis:
            act(zi)

    a_step(1)
    cp.arrive(("ea", 0), wslot(c, z, y + 2, RA, HB), ydev(1))
    cp.arrive(("eb", 0), wslot(c, z, y + 2, RA + HB, WR - RA - HB), ydev(3))
    chain(3, 0, True)
    chain(3, 0, False)
    core_b(0)
    a_step(2)
    each(serve, 0)
    b_step(1)
    a_step(3)
    each(serve, 1, 5)
    each(last, 0)
    a_step(4)
    each(serve, 2, 6)
    b_step(2)
    each(relay_x, 0, 1)
    each(serve, 3, 7, 4)
    each(last, 1, 5, 2, 6)
    b_step(3)
    each(last, 3, 7, 4)
    b_step(4)
    for zi in range(8):
        cp.arrive(("ca", zi), wall(1 - c, z + zoff[zi], 0, RA), other)
        cp.arrive(("cb", zi), wall(1 - c, z + zoff[zi], RA, WR - RA), other)

    lane = lax.broadcasted_iota(jnp.int32, (TB, DH), 1)

    def project(offsets, first):
        rows = len(offsets) * TB
        pacc[0:rows, :] = jnp.zeros((rows, 6 * DH), jnp.float32)

        @pl.loop(0, D // 512)
        def _(f):
            cols = pl.ds(pl.multiple_of(f * 512, 512), 512)
            lhs = jnp.concatenate([n_ref[(x + d) % 4, :, cols] for d in offsets], axis=0)
            rhs = jnp.concatenate([wbuf[yy, 0:DH, cols] for yy in range(4)] + [wbuf[yy, DH:WR, cols] for yy in range(4)], axis=0)
            pacc[0:rows, :] += nt(lhs, rhs)

        for n, d in enumerate(offsets):
            i = first + n
            xx = (x + d) % 4
            r = pl.ds(n * TB, TB)
            cos, sin = rope_block(fine_ref, coarse_ref, 4 * xx + y)
            turn = lambda t: (t * cos + swap_pairs(t) * sin).astype(jnp.bfloat16)
            a, b = pacc[r, 4 * DH:5 * DH], pacc[r, 5 * DH:6 * DH]
            pick = lambda p0, p1, p2, p3: jnp.where(lane < 32, p0, jnp.where(lane < 64, p1, jnp.where(lane < 96, p2, p3)))
            key = turn(pick(a, pltpu.roll(a, 96, 1), pltpu.roll(b, 64, 1), pltpu.roll(b, 32, 1)))
            val = pick(pltpu.roll(a, 96, 1), pltpu.roll(a, 64, 1), pltpu.roll(b, 32, 1), b).astype(jnp.bfloat16)
            for dy in range(4):
                q = turn(pacc[r, pl.ds(pl.multiple_of((y + dy) % 4 * DH, DH), DH)])
                dst = qkv_ref.at[xx, y] if dy == 0 else stage.at[i, dy - 1]
                dst[:, 0:DH] = q
                dst[:, DH:2 * DH] = key
                dst[:, 2 * DH:3 * DH] = val
            for dy in (2, 1, 3):
                cp.start(("q", i, dy), stage.at[i, dy - 1], qkv_ref.at[xx, y], ydev(dy))

    loads["fine"].wait()
    loads["coarse"].wait()
    project((0,), 0)
    for p in (2, 3):
        cp.arrive(("xr", p), npiece(x + 3, p), xdev(1))
        cp.arrive(("xl", 3 - p), npiece(x + 1, 3 - p), xdev(3))
    project((3, 1), 1)
    for p in (0, 1):
        cp.arrive(("xa", p), npiece(x + 2, p), xdev(1))
        cp.arrive(("xb", 3 - p), npiece(x + 2, 3 - p), xdev(3))
    project((2,), 3)
    for i, d in enumerate((0, 3, 1, 2)):
        for dy in range(1, 4):
            cp.arrive(("q", i, dy), qkv_ref.at[(x + d) % 4, (y - dy) % 4], ydev(dy))


    q_ref, k_ref, v_ref = (Part(qkv_ref.reshape(SEQ, 3 * DH), part) for part in range(3))
    loads["g"].wait()
    loads["docs"].wait()

    def exchange(i, dy):
        return pltpu.make_async_remote_copy(
            src_ref=d_scr.at[i, (y + dy) % 4], dst_ref=rbuf.at[dy - 1, i], send_sem=dsend.at[i, dy - 1],
            recv_sem=drecv.at[i, dy - 1], device_id=ydev(dy), device_id_type=MESH)

    @pl.loop(0, SEQ // KB)
    def _(j):
        rows = pl.ds(pl.multiple_of(j * KB, KB), KB)
        kt[j] = k_ref[rows, :].T
        vt[j] = v_ref[rows, :].T

    dk_acc[...] = jnp.zeros_like(dk_acc)
    dv_acc[...] = jnp.zeros_like(dv_acc)

    def finish_query(i, dqt):
        dq = dqt.T * SCALE
        for half in range(QB // 128):
            block = i * (QB // 128) + half
            cos, sin = rope_block(fine_ref, coarse_ref, block)
            x = dq[half * 128:(half + 1) * 128]
            rows = pl.ds(pl.multiple_of(block * 128, 128), 128)
            d_scr[i, half, :, 0:DH] = (x * cos - swap_pairs(x) * sin).astype(jnp.bfloat16)
            d_scr[i, half, :, DH:2 * DH] = (dk_acc[rows, :] * SCALE).astype(jnp.bfloat16)
            d_scr[i, half, :, 2 * DH:3 * DH] = dv_acc[rows, :].astype(jnp.bfloat16)
        for dy in (2, 1, 3):
            exchange(i, dy).start()

    @pl.when(c == 0)
    def _():
        @pl.loop(0, SEQ // QB)
        def _(step):
            i = SEQ // QB - 1 - step
            qrows = pl.ds(pl.multiple_of(i * QB, QB), QB)
            q = q_ref[qrows, :]
            g = g_ref[qrows, :]

            def scores(j):
                return nt(k_ref[pl.ds(pl.multiple_of(j * KB, KB), KB), :], q)

            def pass1(j, m):
                s = scores(j)
                s_scr[j] = s
                return jnp.maximum(m, jnp.max(s.reshape(KB // 8, 8, QB), axis=0))

            m8 = lax.fori_loop(0, i, pass1, jnp.full((8, QB), NEG, jnp.float32))
            s = scores(i)
            key = lax.broadcasted_iota(jnp.int32, (KB, QB), 0)
            qry = lax.broadcasted_iota(jnp.int32, (KB, QB), 1)
            s = jnp.where(key <= qry, s, NEG)
            s_scr[i] = s
            m8 = jnp.maximum(m8, jnp.max(s.reshape(KB // 8, 8, QB), axis=0))
            m = jnp.max(m8, axis=0, keepdims=True)
            acc[...] = jnp.zeros_like(acc)

            def pass2(j, l8):
                p = jnp.exp2((s_scr[j] - m) * EXP_C)
                pb = p.astype(jnp.bfloat16)
                p_scr[j] = pb
                acc[...] += nn(vt[j], pb)
                return l8 + jnp.sum(p.reshape(KB // 8, 8, QB), axis=0)

            l8 = lax.fori_loop(0, i + 1, pass2, jnp.zeros((8, QB), jnp.float32))
            rl = 1.0 / jnp.sum(l8, axis=0, keepdims=True)
            ot = acc[...] * rl
            att_ref[qrows, :] = ot.T.astype(jnp.bfloat16)
            gt = (g.astype(jnp.float32).T * rl).astype(jnp.bfloat16)
            gs = gt.T
            d = jnp.sum(ot * gt.astype(jnp.float32), axis=0, keepdims=True)
            acc[...] = jnp.zeros_like(acc)

            @pl.loop(0, i + 1)
            def _(j):
                krows = pl.ds(pl.multiple_of(j * KB, KB), KB)
                pb = p_scr[j]
                dp = nn(v_ref[krows, :], gt)
                ds = (pb.astype(jnp.float32) * (dp - d)).astype(jnp.bfloat16)
                acc[...] += nn(kt[j], ds)
                dk_acc[krows, :] += nn(ds, q)
                dv_acc[krows, :] += nn(pb, gs)

            finish_query(i, acc[...])

    @pl.when(c == 1)
    def _():
        span = QB + 128

        @pl.loop(0, SEQ // QB)
        def _(step):
            i = SEQ // QB - 1 - step
            qrows = pl.ds(pl.multiple_of(i * QB, QB), QB)
            first = pl.multiple_of(jnp.maximum(i * QB - 128, 0), 128)
            krows = pl.ds(first, span)
            q = q_ref[qrows, :]
            g = g_ref[qrows, :]
            k = k_ref[krows, :]
            v = v_ref[krows, :]
            key = lax.broadcasted_iota(jnp.int32, (span, QB), 0) + first
            qry = lax.broadcasted_iota(jnp.int32, (span, QB), 1) + i * QB
            def docs(start, size):
                rows = [docs_ref[:, pl.ds(pl.multiple_of(start + o, 128), 128)] for o in range(0, size, 128)]
                return jnp.concatenate(rows, axis=1).astype(jnp.float32)

            same = jnp.broadcast_to(docs(first, span), (128, span)).T[:, 0:1] == docs(i * QB, QB)
            s = jnp.where((key <= qry) & same, nt(k, q), NEG)
            m = jnp.max(s, axis=0, keepdims=True)
            p = jnp.exp2((s - m) * EXP_C)
            rl = 1.0 / jnp.sum(p, axis=0, keepdims=True)
            pb = p.astype(jnp.bfloat16)
            ot = nn(v.T, pb) * rl
            att_ref[qrows, :] = ot.T.astype(jnp.bfloat16)
            gt = (g.astype(jnp.float32).T * rl).astype(jnp.bfloat16)
            gs = gt.T
            d = jnp.sum(ot * gt.astype(jnp.float32), axis=0, keepdims=True)
            dp = nn(v, gt)
            ds = (pb.astype(jnp.float32) * (dp - d)).astype(jnp.bfloat16)
            dk_acc[krows, :] += nn(ds, q)
            dv_acc[krows, :] += nn(pb, gs)
            finish_query(i, nn(k.T, ds))

    for i in (3, 2, 1, 0):
        for dy in range(1, 4):
            exchange(i, dy).wait()

    for i in range(4):
        cols = pl.ds(i * TB, TB)
        part = [d_scr[i, y]] + [rbuf[dy - 1, i] for dy in range(1, 4)]
        for dy in range(4):
            dt[(y - dy) % 4, 0:DH, cols] = part[dy][:, 0:DH].T
        key, val = (sum(p[:, s * DH:(s + 1) * DH].astype(jnp.float32) for p in part) for s in (1, 2))
        cos, sin = rope_block(fine_ref, coarse_ref, 4 * i + y)
        key = (key * cos - swap_pairs(key) * sin).astype(jnp.bfloat16).T
        val = val.astype(jnp.bfloat16).T
        for yy in range(4):
            dt[yy, DH:DH + 32, cols] = key[yy * 32:(yy + 1) * 32]
            dt[yy, DH + 32:WR, cols] = val[yy * 32:(yy + 1) * 32]

    order = (4, 5, 3, 6, 2, 7, 1, 0)

    def product(core, dz):
        col = pl.multiple_of((core * 8 + (z + dz) % 8) * WF, WF)
        rhs = n_ref[:, :, pl.ds(col, WF)].reshape(4 * TB, WF)
        return nn(dt[...].reshape(4 * WR, 4 * TB), rhs).reshape(4, WR, WF)

    def compute(t):
        cstage[t] = product(1 - c, order[t]).astype(jnp.bfloat16)
        cp.start(("c", t), cstage.at[t], cbuf.at[t], other)
        own[t] = product(c, order[t])

    def meet(t):
        cp.arrive(("c", t), cbuf.at[t], other)
        own[t] += cbuf[t].astype(jnp.float32)
        hstage[t, 0, 0:H1] = own[t, (y + 2) % 4, 0:H1].astype(jnp.bfloat16)
        hstage[t, 1] = own[t, (y + 2) % 4, H1:R1].astype(jnp.bfloat16)
        cp.start(("a", t), hstage.at[t, 0, pl.ds(0, H1)], hbuf.at[t, 0, pl.ds(0, H1)], ydev(1))
        cp.start(("b", t), hstage.at[t, 1], hbuf.at[t, 1], ydev(3))
        if order[t] in (4, 5):
            ring(t, "n", own[t, :, R1:WR], rstage2, rbuf2)

    def ring(t, kind, value, sent, got):
        dz = order[t]
        right = dz <= 4
        step = 4 - dz if right else dz - 5
        name, peer, first = (kind + "r", zdev(1), 0) if right else (kind + "l", zdev(7), 4)
        if step > 0:
            cp.arrive((name, step - 1), got.at[first + step - 1], peer)
            value = value + got[first + step - 1].astype(jnp.float32)
        sent[first + step] = value.astype(jnp.bfloat16)
        cp.start((name, step), sent.at[first + step], got.at[first + step], peer)

    def ring_end(kind, got):
        cp.arrive((kind + "r", 3), got.at[3], zdev(1))
        cp.arrive((kind + "l", 2), got.at[6], zdev(7))
        return got[3].astype(jnp.float32) + got[6].astype(jnp.float32)

    def pass_on(t):
        cp.arrive(("a", t), hbuf.at[t, 0, pl.ds(0, H1)], ydev(1))
        fstage[t, 0, 0:H1] = (own[t, (y + 1) % 4, 0:H1] + hbuf[t, 0, 0:H1].astype(jnp.float32)).astype(jnp.bfloat16)
        fstage[t, 0, H1:R1] = own[t, (y + 1) % 4, H1:R1].astype(jnp.bfloat16)
        cp.start(("r", t), fstage.at[t, 0], fbuf.at[t, 0], ydev(1))
        cp.arrive(("b", t), hbuf.at[t, 1], ydev(3))
        fstage[t, 1, 0:H1] = own[t, (y + 3) % 4, 0:H1].astype(jnp.bfloat16)
        fstage[t, 1, H1:R1] = (own[t, (y + 3) % 4, H1:R1] + hbuf[t, 1].astype(jnp.float32)).astype(jnp.bfloat16)
        cp.start(("l", t), fstage.at[t, 1], fbuf.at[t, 1], ydev(3))
        if order[t] not in (0, 4, 5):
            ring(t, "n", own[t, :, R1:WR], rstage2, rbuf2)

    def home(t):
        cp.arrive(("r", t), fbuf.at[t, 0], ydev(1))
        cp.arrive(("l", t), fbuf.at[t, 1], ydev(3))
        total = own[t, y, 0:R1] + fbuf[t, 0].astype(jnp.float32) + fbuf[t, 1].astype(jnp.float32)
        if order[t] == 0:
            grad_ref[0:R1] = total
        else:
            ring(t, "m", total, zstage, zbuf)

    for t in range(8 + 6):
        for delay, part in ((0, compute), (2, meet), (4, pass_on), (6, home)):
            if 0 <= t - delay < 8:
                part(t - delay)

    own[7, :, R1:WR] += ring_end("n", rbuf2)
    for dy in (2, 1, 3):
        ystage[dy - 1] = own[7, (y + dy) % 4, R1:WR].astype(jnp.bfloat16)
        cp.start(("v", dy), ystage.at[dy - 1], ybuf.at[dy - 1], ydev(dy))
    grad_ref[0:R1] += ring_end("m", zbuf)
    total = own[7, y, R1:WR]
    for dy in (1, 3, 2):
        cp.arrive(("v", dy), ybuf.at[dy - 1], ydev(dy))
        total = total + ybuf[dy - 1].astype(jnp.float32)
    grad_ref[R1:WR] = total
    cp.drain()


def finish_kernel(att_ref, grad_ref, out_ref, gq_ref, gk_ref, gv_ref):
    out_ref[...] = att_ref[...]
    gq_ref[...] = grad_ref[0:DH].T
    gk_ref[...] = grad_ref[DH:DH + 32]
    gv_ref[...] = grad_ref[DH + 32:WR]


def block(h, gain, wq, wk, wv, g, docs, fine, coarse):
    vmem, hbm = pl.BlockSpec(memory_space=pltpu.VMEM), pl.BlockSpec(memory_space=pl.ANY)
    bf, f32, nb = jnp.bfloat16, jnp.float32, SEQ // KB
    att, grad = pl.pallas_call(
        block_kernel,
        out_shape=(jax.ShapeDtypeStruct((SEQ, DH), bf), jax.ShapeDtypeStruct((WR, WF), f32)),
        in_specs=[hbm] * 9,
        out_specs=(vmem,) * 2,
        scratch_shapes=[
            pltpu.VMEM((TB, D), bf),
            pltpu.VMEM((1, D), f32),
            pltpu.VMEM((WF, DH), bf),
            pltpu.VMEM((32, WF), bf),
            pltpu.VMEM((32, WF), bf),
            pltpu.VMEM((SEQ, DH), bf),
            pltpu.VMEM((1, SEQ), jnp.int32),
            pltpu.VMEM((2, TB, DH), f32),
            pltpu.VMEM((2, 16, DH), f32),
            pltpu.VMEM((WR, WF), bf),
            pltpu.VMEM((4, TB, D), bf),
            pltpu.VMEM((4, 4, TB, 3 * DH), bf),
            pltpu.VMEM((4, WR, D), bf),
            pltpu.VMEM((2 * TB, 6 * DH), f32),
            pltpu.VMEM((4, 3, TB, 3 * DH), bf),
            pltpu.VMEM((nb, DH, KB), bf),
            pltpu.VMEM((nb, DH, KB), bf),
            pltpu.VMEM((nb, KB, QB), f32),
            pltpu.VMEM((nb, KB, QB), bf),
            pltpu.VMEM((DH, QB), f32),
            pltpu.VMEM((SEQ, DH), f32),
            pltpu.VMEM((SEQ, DH), f32),
            pltpu.VMEM((4, 4, TB, 3 * DH), bf),
            pltpu.SemaphoreType.DMA((4, 3)),
            pltpu.SemaphoreType.DMA((4, 3)),
            pltpu.VMEM((3, 4, TB, 3 * DH), bf),
            pltpu.VMEM((4, WR, 4 * TB), bf),
            pltpu.VMEM((8, 4, WR, WF), f32),
            pltpu.VMEM((8, 4, WR, WF), bf),
            pltpu.VMEM((8, 4, WR, WF), bf),
            pltpu.VMEM((8, 2, R1 - H1, WF), bf),
            pltpu.VMEM((8, 2, R1 - H1, WF), bf),
            pltpu.VMEM((8, 2, R1, WF), bf),
            pltpu.VMEM((8, 2, R1, WF), bf),
            pltpu.VMEM((7, R1, WF), bf),
            pltpu.VMEM((7, R1, WF), bf),
            pltpu.VMEM((7, 4, WR - R1, WF), bf),
            pltpu.VMEM((7, 4, WR - R1, WF), bf),
            pltpu.VMEM((3, WR - R1, WF), bf),
            pltpu.VMEM((3, WR - R1, WF), bf),
            pltpu.SemaphoreType.DMA((SEMS,)),
            pltpu.SemaphoreType.DMA((SEMS,)),
            pltpu.SemaphoreType.DMA((9,)),
        ],
        compiler_params=pltpu.CompilerParams(vmem_limit_bytes=62 << 20, collective_id=0, has_side_effects=True),
        name="block",
    )(h, gain, wq, wk, wv, g, docs, fine, coarse)
    return pl.pallas_call(
        finish_kernel,
        out_shape=(jax.ShapeDtypeStruct((SEQ, DH), bf),) + tuple(jax.ShapeDtypeStruct(s, f32) for s in ((WF, DH), (32, WF), (32, WF))),
        in_specs=[vmem] * 2,
        out_specs=(vmem,) * 4,
        name="finish",
    )(att, grad)


def local(hidden_states, norm_gain, w_query, w_key, w_value, out_grad, short_docs):
    fine, coarse = (jnp.asarray(t) for t in rope_tables())
    att, gq, gk, gv = block(hidden_states.reshape(TB, D), norm_gain.reshape(1, D), w_query, w_key.T, w_value.T,
                            out_grad.reshape(SEQ, DH), short_docs, fine, coarse)
    return att.reshape(1, 1, SEQ, DH), gq, gk.T, gv.T


def solution(mesh):
    both = ("bucket", "fsdp")
    return jax.shard_map(
        local,
        mesh=mesh,
        in_specs=(P("bucket", "fsdp", "sp", None), P(), P(both, "sp"), P(both, "sp"), P(both, "sp"),
                  P("bucket", "fsdp", None, "sp"), P("fsdp", None)),
        out_specs=(P("bucket", "fsdp", None, "sp"), P(both, "sp"), P(both, "sp"), P(both, "sp")),
        check_vma=False,
    )
```

```python
import math
import functools
import numpy as np
import jax
import jax.numpy as jnp
from jax import lax
from jax.experimental import pallas as pl
from jax.experimental.pallas import tpu as pltpu
from jax.sharding import PartitionSpec as P

MESH = pl.DeviceIdType.MESH

DH = 128
SEQ = 2048
QB = 512
KB = 512
NEG = -1e30
SCALE = 1.0 / math.sqrt(DH)
EXP_C = SCALE * math.log2(math.e)


def rope_tables():
    freq = np.float32(500000.0) ** (-2.0 * np.arange(64, dtype=np.float32) / DH)
    freq = np.repeat(freq.astype(np.float64), 2)[None, :]
    sign = np.where(np.arange(DH) % 2 == 0, -1.0, 1.0)[None, :]
    fine = np.arange(128)[:, None] * freq
    coarse = 128 * np.arange(16)[:, None] * freq
    f = np.stack([np.cos(fine), np.sin(fine) * sign]).astype(np.float32)
    c = np.stack([np.cos(coarse), np.sin(coarse) * sign]).astype(np.float32)
    return f, c


def rope_block(fine_ref, coarse_ref, block):
    cf, sf = fine_ref[0], fine_ref[1]
    cc = coarse_ref[0, pl.ds(block, 1), :]
    sc = coarse_ref[1, pl.ds(block, 1), :]
    return cf * cc - sf * sc, sf * cc + cf * sc


def swap_pairs(x):
    lane = lax.broadcasted_iota(jnp.int32, x.shape, 1)
    return jnp.where(lane % 2 == 0, pltpu.roll(x, DH - 1, 1), pltpu.roll(x, 1, 1))


def nn(a, b):
    return jnp.dot(a, b, preferred_element_type=jnp.float32)


def nt(a, b):
    return lax.dot_general(a, b, (((1,), (1,)), ((), ())), preferred_element_type=jnp.float32)


D = 4096
TB = 128
WR = 192
WF = 256
EPS = 1e-5
RA, HA, HB = 112, 48, 32
R1, H1 = 128, 64


class Copies:
    def __init__(self, send, recv):
        self.send, self.recv, self.ids, self.live = send, recv, {}, []

    def make(self, key, src, dst, dev):
        i = self.ids.setdefault(key, len(self.ids))
        return pltpu.make_async_remote_copy(src_ref=src, dst_ref=dst, send_sem=self.send.at[i], recv_sem=self.recv.at[i],
                                            device_id=dev, device_id_type=MESH)

    def start(self, key, src, dst, dev):
        copy = self.make(key, src, dst, dev)
        copy.start()
        self.live.append(copy)

    def arrive(self, key, dst, dev):
        self.make(key, dst, dst, dev).wait_recv()

    def drain(self):
        for copy in self.live:
            copy.wait_send()


def place():
    c, z, sp = lax.axis_index("bucket"), lax.axis_index("fsdp"), lax.axis_index("sp")
    return c, z, sp // 4, sp % 4


def greet(devs):
    barrier = pltpu.get_barrier_semaphore()
    for dev in devs:
        pl.semaphore_signal(barrier, inc=1, device_id=dev, device_id_type=MESH)
    return lambda: pl.semaphore_wait(barrier, len(devs))


SEMS = 7 + 32 + 4 + 28 + 16 + 12 + 12 + 8 + 32 + 7 + 10


class Part:
    def __init__(self, ref, part):
        self.ref, self.part = ref, part

    def __getitem__(self, index):
        return self.ref[index[0], self.part * DH:(self.part + 1) * DH]


def block_kernel(h_hbm, gain_hbm, wq_hbm, wk_hbm, wv_hbm, g_hbm, docs_hbm, fine_hbm, coarse_hbm, att_ref, grad_ref,
                 h_ref, gain_ref, wq_ref, wk_ref, wv_ref, g_ref, docs_ref, fine_ref, coarse_ref, w_ref,
                 n_ref, qkv4_ref, wbuf, pacc, stage,
                 kt, vt, s_scr, p_scr, acc, dk_acc, dv_acc, d_scr, dsend, drecv,
                 rbuf, dt, own, cstage, cbuf, hstage, hbuf, fstage, fbuf, zstage, zbuf, rstage2, rbuf2, ystage, ybuf, ssem, rsem, lsem):
    loads = {}
    for name, src, dst in (("h", h_hbm, h_ref), ("gain", gain_hbm, gain_ref), ("wq", wq_hbm, wq_ref), ("wk", wk_hbm, wk_ref),
                           ("wv", wv_hbm, wv_ref), ("fine", fine_hbm, fine_ref), ("coarse", coarse_hbm, coarse_ref),
                           ("g", g_hbm, g_ref), ("docs", docs_hbm, docs_ref)):
        loads[name] = pltpu.make_async_copy(src, dst, lsem.at[len(loads)])
        loads[name].start()
    c, z, x, y = place()
    xdev = lambda d: {"sp": (x + d) % 4 * 4 + y}
    ydev = lambda d: {"sp": x * 4 + (y + d) % 4}
    zdev = lambda d: {"fsdp": (z + d) % 8}
    other = {"bucket": 1 - c}
    wait_all = greet([xdev(1), xdev(3), ydev(1), ydev(2), ydev(3), other] + [zdev(d) for d in range(1, 8)])
    qkv_ref = qkv4_ref

    def wslot(core, zz, yy, lo=0, size=WR):
        col = pl.multiple_of((core * 8 + zz % 8) * WF, WF)
        return wbuf.at[yy % 4, pl.ds(lo, size), pl.ds(col, WF)]

    for name in ("wq", "wk", "wv"):
        loads[name].wait()
    w_ref[0:DH] = wq_ref[...].T
    w_ref[DH:DH + 32] = wk_ref[...]
    w_ref[DH + 32:WR] = wv_ref[...]
    wslot(c, z, y)[...] = w_ref[...]
    loads["h"].wait()
    loads["gain"].wait()
    for r in range(0, TB, 32):
        rows = h_ref[r:r + 32, :].astype(jnp.float32)
        inv = lax.rsqrt(jnp.mean(rows * rows, axis=1, keepdims=True) + EPS)
        n_ref[x, r:r + 32, :] = (rows * inv * gain_ref[...]).astype(jnp.bfloat16)
    wait_all()
    cp = Copies(ssem, rsem)
    zoff = [0, -1, -2, -3, -4, 1, 2, 3]
    yoff = [0, 3, 1, 2]

    def spread(zi):
        src = w_ref.at[pl.ds(0, RA), :] if zi == 0 else wslot(c, z + zoff[zi], y, 0, RA)
        dst = wslot(c, z + zoff[zi], y, 0, RA)
        cp.start(("yr", zi), src, dst, ydev(1))
        cp.start(("yl", zi), src, dst, ydev(3))

    def serve(zi):
        zz = z + zoff[zi]
        cp.arrive(("yr", zi), wslot(c, zz, y + 3, 0, RA), ydev(1))
        part = wslot(c, zz, y + 3, 0, HA)
        cp.start(("ya", zi), part, part, ydev(1))
        cp.arrive(("yl", zi), wslot(c, zz, y + 1, 0, RA), ydev(3))
        part = wslot(c, zz, y + 1, HA, RA - HA)
        cp.start(("yb", zi), part, part, ydev(3))

    def wall(core, zz, lo, size):
        col = pl.multiple_of((core * 8 + zz % 8) * WF, WF)
        return wbuf.at[:, pl.ds(lo, size), pl.ds(col, WF)]

    def last(zi):
        zz = z + zoff[zi]
        cp.arrive(("ya", zi), wslot(c, zz, y + 2, 0, HA), ydev(1))
        cp.arrive(("yb", zi), wslot(c, zz, y + 2, HA, RA - HA), ydev(3))
        cp.start(("ca", zi), wall(c, zz, 0, RA), wall(c, zz, 0, RA), other)

    def chain(yk, step, right):
        n = 4 if right == (yk < 2) else 3
        if step > n:
            return
        zz = z - step if right else z + step
        name = "br" if right else "bl"
        part = wslot(c, zz, y + yoff[yk], RA, WR - RA)
        if step > 0:
            cp.arrive((name, yk, step), part, zdev(1 if right else 7))
        if step < n:
            src = w_ref.at[pl.ds(RA, WR - RA), :] if yk == 0 and step == 0 else part
            cp.start((name, yk, step + 1), src, part, zdev(1 if right else 7))

    def npiece(xx, p):
        return n_ref.at[xx % 4, pl.ds(p * 32, 32), :]

    for p in range(4):
        cp.start(("xr", p), npiece(x, p), npiece(x, p), xdev(1))
        cp.start(("xl", 3 - p), npiece(x, 3 - p), npiece(x, 3 - p), xdev(3))
    own_a, own_b = w_ref.at[pl.ds(0, RA), :], w_ref.at[pl.ds(RA, WR - RA), :]
    cp.start(("zr", 1), own_a, wslot(c, z, y, 0, RA), zdev(1))
    cp.start(("zl", 1), own_a, wslot(c, z, y, 0, RA), zdev(7))
    cp.start(("er", 0), own_b, wslot(c, z, y, RA, WR - RA), ydev(1))
    cp.start(("el", 0), own_b, wslot(c, z, y, RA, WR - RA), ydev(3))
    spread(0)
    chain(0, 0, True)
    chain(0, 0, False)
    cp.arrive(("er", 0), wslot(c, z, y + 3, RA, WR - RA), ydev(1))
    part = wslot(c, z, y + 3, RA, HB)
    cp.start(("ea", 0), part, part, ydev(1))
    chain(1, 0, True)
    chain(1, 0, False)
    cp.arrive(("el", 0), wslot(c, z, y + 1, RA, WR - RA), ydev(3))
    part = wslot(c, z, y + 1, RA + HB, WR - RA - HB)
    cp.start(("eb", 0), part, part, ydev(3))
    chain(2, 0, True)
    chain(2, 0, False)

    def relay_x(p):
        cp.arrive(("xr", p), npiece(x + 3, p), xdev(1))
        cp.start(("xa", p), npiece(x + 3, p), npiece(x + 3, p), xdev(1))
        cp.arrive(("xl", 3 - p), npiece(x + 1, 3 - p), xdev(3))
        cp.start(("xb", 3 - p), npiece(x + 1, 3 - p), npiece(x + 1, 3 - p), xdev(3))

    def core_b(zi):
        zz = z + zoff[zi]
        cp.start(("cb", zi), wall(c, zz, RA, WR - RA), wall(c, zz, RA, WR - RA), other)

    def a_step(step):
        src = wslot(c, z - step, y, 0, RA)
        cp.arrive(("zr", step), src, zdev(1))
        if step < 4:
            cp.start(("zr", step + 1), src, src, zdev(1))
        spread(step)
        if step < 4:
            src = wslot(c, z + step, y, 0, RA)
            cp.arrive(("zl", step), src, zdev(7))
            if step < 3:
                cp.start(("zl", step + 1), src, src, zdev(7))
            spread(4 + step)

    def b_step(step):
        for yk in range(4):
            chain(yk, step, True)
            chain(yk, step, False)
        core_b(step)
        if step < 4:
            core_b(4 + step)

    def each(act, *zis):
        for zi in zis:
            act(zi)

    a_step(1)
    cp.arrive(("ea", 0), wslot(c, z, y + 2, RA, HB), ydev(1))
    cp.arrive(("eb", 0), wslot(c, z, y + 2, RA + HB, WR - RA - HB), ydev(3))
    chain(3, 0, True)
    chain(3, 0, False)
    core_b(0)
    a_step(2)
    each(serve, 0)
    b_step(1)
    a_step(3)
    each(serve, 1, 5)
    each(last, 0)
    a_step(4)
    each(serve, 2, 6)
    b_step(2)
    each(relay_x, 0, 1)
    each(serve, 3, 7, 4)
    each(last, 1, 5, 2, 6)
    b_step(3)
    each(last, 3, 7, 4)
    b_step(4)
    for zi in range(8):
        cp.arrive(("ca", zi), wall(1 - c, z + zoff[zi], 0, RA), other)
        cp.arrive(("cb", zi), wall(1 - c, z + zoff[zi], RA, WR - RA), other)

    lane = lax.broadcasted_iota(jnp.int32, (TB, DH), 1)

    def project(offsets, first):
        rows = len(offsets) * TB
        pacc[0:rows, :] = jnp.zeros((rows, 6 * DH), jnp.float32)

        @pl.loop(0, D // 512)
        def _(f):
            cols = pl.ds(pl.multiple_of(f * 512, 512), 512)
            lhs = jnp.concatenate([n_ref[(x + d) % 4, :, cols] for d in offsets], axis=0)
            rhs = jnp.concatenate([wbuf[yy, 0:DH, cols] for yy in range(4)] + [wbuf[yy, DH:WR, cols] for yy in range(4)], axis=0)
            pacc[0:rows, :] += nt(lhs, rhs)

        for n, d in enumerate(offsets):
            i = first + n
            xx = (x + d) % 4
            r = pl.ds(n * TB, TB)
            cos, sin = rope_block(fine_ref, coarse_ref, 4 * xx + y)
            turn = lambda t: (t * cos + swap_pairs(t) * sin).astype(jnp.bfloat16)
            a, b = pacc[r, 4 * DH:5 * DH], pacc[r, 5 * DH:6 * DH]
            pick = lambda p0, p1, p2, p3: jnp.where(lane < 32, p0, jnp.where(lane < 64, p1, jnp.where(lane < 96, p2, p3)))
            key = turn(pick(a, pltpu.roll(a, 96, 1), pltpu.roll(b, 64, 1), pltpu.roll(b, 32, 1)))
            val = pick(pltpu.roll(a, 96, 1), pltpu.roll(a, 64, 1), pltpu.roll(b, 32, 1), b).astype(jnp.bfloat16)
            for dy in range(4):
                q = turn(pacc[r, pl.ds(pl.multiple_of((y + dy) % 4 * DH, DH), DH)])
                dst = qkv_ref.at[xx, y] if dy == 0 else stage.at[i, dy - 1]
                dst[:, 0:DH] = q
                dst[:, DH:2 * DH] = key
                dst[:, 2 * DH:3 * DH] = val
            for dy in (2, 1, 3):
                cp.start(("q", i, dy), stage.at[i, dy - 1], qkv_ref.at[xx, y], ydev(dy))

    loads["fine"].wait()
    loads["coarse"].wait()
    project((0,), 0)
    for p in (2, 3):
        cp.arrive(("xr", p), npiece(x + 3, p), xdev(1))
        cp.arrive(("xl", 3 - p), npiece(x + 1, 3 - p), xdev(3))
    project((3, 1), 1)
    for p in (0, 1):
        cp.arrive(("xa", p), npiece(x + 2, p), xdev(1))
        cp.arrive(("xb", 3 - p), npiece(x + 2, 3 - p), xdev(3))
    project((2,), 3)
    for i, d in enumerate((0, 3, 1, 2)):
        for dy in range(1, 4):
            cp.arrive(("q", i, dy), qkv_ref.at[(x + d) % 4, (y - dy) % 4], ydev(dy))


    q_ref, k_ref, v_ref = (Part(qkv_ref.reshape(SEQ, 3 * DH), part) for part in range(3))
    loads["g"].wait()
    loads["docs"].wait()

    def exchange(i, dy):
        return pltpu.make_async_remote_copy(
            src_ref=d_scr.at[i, (y + dy) % 4], dst_ref=rbuf.at[dy - 1, i], send_sem=dsend.at[i, dy - 1],
            recv_sem=drecv.at[i, dy - 1], device_id=ydev(dy), device_id_type=MESH)

    @pl.loop(0, SEQ // KB)
    def _(j):
        rows = pl.ds(pl.multiple_of(j * KB, KB), KB)
        kt[j] = k_ref[rows, :].T
        vt[j] = v_ref[rows, :].T

    dk_acc[...] = jnp.zeros_like(dk_acc)
    dv_acc[...] = jnp.zeros_like(dv_acc)

    def finish_query(i, dqt):
        dq = dqt.T * SCALE
        for half in range(QB // 128):
            block = i * (QB // 128) + half
            cos, sin = rope_block(fine_ref, coarse_ref, block)
            x = dq[half * 128:(half + 1) * 128]
            rows = pl.ds(pl.multiple_of(block * 128, 128), 128)
            d_scr[i, half, :, 0:DH] = (x * cos - swap_pairs(x) * sin).astype(jnp.bfloat16)
            d_scr[i, half, :, DH:2 * DH] = (dk_acc[rows, :] * SCALE).astype(jnp.bfloat16)
            d_scr[i, half, :, 2 * DH:3 * DH] = dv_acc[rows, :].astype(jnp.bfloat16)
        for dy in (2, 1, 3):
            exchange(i, dy).start()

    @pl.when(c == 0)
    def _():
        @pl.loop(0, SEQ // QB)
        def _(step):
            i = SEQ // QB - 1 - step
            qrows = pl.ds(pl.multiple_of(i * QB, QB), QB)
            q = q_ref[qrows, :]
            g = g_ref[qrows, :]

            def scores(j):
                return nt(k_ref[pl.ds(pl.multiple_of(j * KB, KB), KB), :], q)

            def pass1(j, m):
                s = scores(j)
                s_scr[j] = s
                return jnp.maximum(m, jnp.max(s.reshape(KB // 8, 8, QB), axis=0))

            m8 = lax.fori_loop(0, i, pass1, jnp.full((8, QB), NEG, jnp.float32))
            s = scores(i)
            key = lax.broadcasted_iota(jnp.int32, (KB, QB), 0)
            qry = lax.broadcasted_iota(jnp.int32, (KB, QB), 1)
            s = jnp.where(key <= qry, s, NEG)
            s_scr[i] = s
            m8 = jnp.maximum(m8, jnp.max(s.reshape(KB // 8, 8, QB), axis=0))
            m = jnp.max(m8, axis=0, keepdims=True)
            acc[...] = jnp.zeros_like(acc)

            def pass2(j, l8):
                p = jnp.exp2((s_scr[j] - m) * EXP_C)
                pb = p.astype(jnp.bfloat16)
                p_scr[j] = pb
                acc[...] += nn(vt[j], pb)
                return l8 + jnp.sum(p.reshape(KB // 8, 8, QB), axis=0)

            l8 = lax.fori_loop(0, i + 1, pass2, jnp.zeros((8, QB), jnp.float32))
            rl = 1.0 / jnp.sum(l8, axis=0, keepdims=True)
            ot = acc[...] * rl
            att_ref[qrows, :] = ot.T.astype(jnp.bfloat16)
            gt = (g.astype(jnp.float32).T * rl).astype(jnp.bfloat16)
            gs = gt.T
            d = jnp.sum(ot * gt.astype(jnp.float32), axis=0, keepdims=True)
            acc[...] = jnp.zeros_like(acc)

            @pl.loop(0, i + 1)
            def _(j):
                krows = pl.ds(pl.multiple_of(j * KB, KB), KB)
                pb = p_scr[j]
                dp = nn(v_ref[krows, :], gt)
                ds = (pb.astype(jnp.float32) * (dp - d)).astype(jnp.bfloat16)
                acc[...] += nn(kt[j], ds)
                dk_acc[krows, :] += nn(ds, q)
                dv_acc[krows, :] += nn(pb, gs)

            finish_query(i, acc[...])

    @pl.when(c == 1)
    def _():
        span = QB + 128

        @pl.loop(0, SEQ // QB)
        def _(step):
            i = SEQ // QB - 1 - step
            qrows = pl.ds(pl.multiple_of(i * QB, QB), QB)
            first = pl.multiple_of(jnp.maximum(i * QB - 128, 0), 128)
            krows = pl.ds(first, span)
            q = q_ref[qrows, :]
            g = g_ref[qrows, :]
            k = k_ref[krows, :]
            v = v_ref[krows, :]
            key = lax.broadcasted_iota(jnp.int32, (span, QB), 0) + first
            qry = lax.broadcasted_iota(jnp.int32, (span, QB), 1) + i * QB
            def docs(start, size):
                rows = [docs_ref[:, pl.ds(pl.multiple_of(start + o, 128), 128)] for o in range(0, size, 128)]
                return jnp.concatenate(rows, axis=1).astype(jnp.float32)

            same = jnp.broadcast_to(docs(first, span), (128, span)).T[:, 0:1] == docs(i * QB, QB)
            s = jnp.where((key <= qry) & same, nt(k, q), NEG)
            m = jnp.max(s, axis=0, keepdims=True)
            p = jnp.exp2((s - m) * EXP_C)
            rl = 1.0 / jnp.sum(p, axis=0, keepdims=True)
            pb = p.astype(jnp.bfloat16)
            ot = nn(v.T, pb) * rl
            att_ref[qrows, :] = ot.T.astype(jnp.bfloat16)
            gt = (g.astype(jnp.float32).T * rl).astype(jnp.bfloat16)
            gs = gt.T
            d = jnp.sum(ot * gt.astype(jnp.float32), axis=0, keepdims=True)
            dp = nn(v, gt)
            ds = (pb.astype(jnp.float32) * (dp - d)).astype(jnp.bfloat16)
            dk_acc[krows, :] += nn(ds, q)
            dv_acc[krows, :] += nn(pb, gs)
            finish_query(i, nn(k.T, ds))

    for i in (3, 2, 1, 0):
        for dy in range(1, 4):
            exchange(i, dy).wait()

    for i in range(4):
        cols = pl.ds(i * TB, TB)
        part = [d_scr[i, y]] + [rbuf[dy - 1, i] for dy in range(1, 4)]
        for dy in range(4):
            dt[(y - dy) % 4, 0:DH, cols] = part[dy][:, 0:DH].T
        key, val = (sum(p[:, s * DH:(s + 1) * DH].astype(jnp.float32) for p in part) for s in (1, 2))
        cos, sin = rope_block(fine_ref, coarse_ref, 4 * i + y)
        key = (key * cos - swap_pairs(key) * sin).astype(jnp.bfloat16).T
        val = val.astype(jnp.bfloat16).T
        for yy in range(4):
            dt[yy, DH:DH + 32, cols] = key[yy * 32:(yy + 1) * 32]
            dt[yy, DH + 32:WR, cols] = val[yy * 32:(yy + 1) * 32]

    order = (4, 5, 3, 6, 2, 7, 1, 0)

    def product(core, dz):
        col = pl.multiple_of((core * 8 + (z + dz) % 8) * WF, WF)
        rhs = n_ref[:, :, pl.ds(col, WF)].reshape(4 * TB, WF)
        return nn(dt[...].reshape(4 * WR, 4 * TB), rhs).reshape(4, WR, WF)

    def compute(t):
        cstage[t] = product(1 - c, order[t]).astype(jnp.bfloat16)
        cp.start(("c", t), cstage.at[t], cbuf.at[t], other)
        own[t] = product(c, order[t])

    def meet(t):
        cp.arrive(("c", t), cbuf.at[t], other)
        own[t] += cbuf[t].astype(jnp.float32)
        hstage[t, 0, 0:H1] = own[t, (y + 2) % 4, 0:H1].astype(jnp.bfloat16)
        hstage[t, 1] = own[t, (y + 2) % 4, H1:R1].astype(jnp.bfloat16)
        cp.start(("a", t), hstage.at[t, 0, pl.ds(0, H1)], hbuf.at[t, 0, pl.ds(0, H1)], ydev(1))
        cp.start(("b", t), hstage.at[t, 1], hbuf.at[t, 1], ydev(3))
        if order[t] in (4, 5):
            ring(t, "n", own[t, :, R1:WR], rstage2, rbuf2)

    def ring(t, kind, value, sent, got):
        dz = order[t]
        right = dz <= 4
        step = 4 - dz if right else dz - 5
        name, peer, first = (kind + "r", zdev(1), 0) if right else (kind + "l", zdev(7), 4)
        if step > 0:
            cp.arrive((name, step - 1), got.at[first + step - 1], peer)
            value = value + got[first + step - 1].astype(jnp.float32)
        sent[first + step] = value.astype(jnp.bfloat16)
        cp.start((name, step), sent.at[first + step], got.at[first + step], peer)

    def ring_end(kind, got):
        cp.arrive((kind + "r", 3), got.at[3], zdev(1))
        cp.arrive((kind + "l", 2), got.at[6], zdev(7))
        return got[3].astype(jnp.float32) + got[6].astype(jnp.float32)

    def pass_on(t):
        cp.arrive(("a", t), hbuf.at[t, 0, pl.ds(0, H1)], ydev(1))
        fstage[t, 0, 0:H1] = (own[t, (y + 1) % 4, 0:H1] + hbuf[t, 0, 0:H1].astype(jnp.float32)).astype(jnp.bfloat16)
        fstage[t, 0, H1:R1] = own[t, (y + 1) % 4, H1:R1].astype(jnp.bfloat16)
        cp.start(("r", t), fstage.at[t, 0], fbuf.at[t, 0], ydev(1))
        cp.arrive(("b", t), hbuf.at[t, 1], ydev(3))
        fstage[t, 1, 0:H1] = own[t, (y + 3) % 4, 0:H1].astype(jnp.bfloat16)
        fstage[t, 1, H1:R1] = (own[t, (y + 3) % 4, H1:R1] + hbuf[t, 1].astype(jnp.float32)).astype(jnp.bfloat16)
        cp.start(("l", t), fstage.at[t, 1], fbuf.at[t, 1], ydev(3))
        if order[t] not in (0, 4, 5):
            ring(t, "n", own[t, :, R1:WR], rstage2, rbuf2)

    def home(t):
        cp.arrive(("r", t), fbuf.at[t, 0], ydev(1))
        cp.arrive(("l", t), fbuf.at[t, 1], ydev(3))
        total = own[t, y, 0:R1] + fbuf[t, 0].astype(jnp.float32) + fbuf[t, 1].astype(jnp.float32)
        if order[t] == 0:
            grad_ref[0:R1] = total
        else:
            ring(t, "m", total, zstage, zbuf)

    for t in range(8 + 6):
        for delay, part in ((0, compute), (2, meet), (4, pass_on), (6, home)):
            if 0 <= t - delay < 8:
                part(t - delay)

    own[7, :, R1:WR] += ring_end("n", rbuf2)
    for dy in (2, 1, 3):
        ystage[dy - 1] = own[7, (y + dy) % 4, R1:WR].astype(jnp.bfloat16)
        cp.start(("v", dy), ystage.at[dy - 1], ybuf.at[dy - 1], ydev(dy))
    grad_ref[0:R1] += ring_end("m", zbuf)
    total = own[7, y, R1:WR]
    for dy in (1, 3, 2):
        cp.arrive(("v", dy), ybuf.at[dy - 1], ydev(dy))
        total = total + ybuf[dy - 1].astype(jnp.float32)
    grad_ref[R1:WR] = total
    cp.drain()


def finish_kernel(att_ref, grad_ref, out_ref, gq_ref, gk_ref, gv_ref):
    out_ref[...] = att_ref[...]
    gq_ref[...] = grad_ref[0:DH].T
    gk_ref[...] = grad_ref[DH:DH + 32]
    gv_ref[...] = grad_ref[DH + 32:WR]


def block(h, gain, wq, wk, wv, g, docs, fine, coarse):
    vmem, hbm = pl.BlockSpec(memory_space=pltpu.VMEM), pl.BlockSpec(memory_space=pl.ANY)
    bf, f32, nb = jnp.bfloat16, jnp.float32, SEQ // KB
    att, grad = pl.pallas_call(
        block_kernel,
        out_shape=(jax.ShapeDtypeStruct((SEQ, DH), bf), jax.ShapeDtypeStruct((WR, WF), f32)),
        in_specs=[hbm] * 9,
        out_specs=(vmem,) * 2,
        scratch_shapes=[
            pltpu.VMEM((TB, D), bf),
            pltpu.VMEM((1, D), f32),
            pltpu.VMEM((WF, DH), bf),
            pltpu.VMEM((32, WF), bf),
            pltpu.VMEM((32, WF), bf),
            pltpu.VMEM((SEQ, DH), bf),
            pltpu.VMEM((1, SEQ), jnp.int32),
            pltpu.VMEM((2, TB, DH), f32),
            pltpu.VMEM((2, 16, DH), f32),
            pltpu.VMEM((WR, WF), bf),
            pltpu.VMEM((4, TB, D), bf),
            pltpu.VMEM((4, 4, TB, 3 * DH), bf),
            pltpu.VMEM((4, WR, D), bf),
            pltpu.VMEM((2 * TB, 6 * DH), f32),
            pltpu.VMEM((4, 3, TB, 3 * DH), bf),
            pltpu.VMEM((nb, DH, KB), bf),
            pltpu.VMEM((nb, DH, KB), bf),
            pltpu.VMEM((nb, KB, QB), f32),
            pltpu.VMEM((nb, KB, QB), bf),
            pltpu.VMEM((DH, QB), f32),
            pltpu.VMEM((SEQ, DH), f32),
            pltpu.VMEM((SEQ, DH), f32),
            pltpu.VMEM((4, 4, TB, 3 * DH), bf),
            pltpu.SemaphoreType.DMA((4, 3)),
            pltpu.SemaphoreType.DMA((4, 3)),
            pltpu.VMEM((3, 4, TB, 3 * DH), bf),
            pltpu.VMEM((4, WR, 4 * TB), bf),
            pltpu.VMEM((8, 4, WR, WF), f32),
            pltpu.VMEM((8, 4, WR, WF), bf),
            pltpu.VMEM((8, 4, WR, WF), bf),
            pltpu.VMEM((8, 2, R1 - H1, WF), bf),
            pltpu.VMEM((8, 2, R1 - H1, WF), bf),
            pltpu.VMEM((8, 2, R1, WF), bf),
            pltpu.VMEM((8, 2, R1, WF), bf),
            pltpu.VMEM((7, R1, WF), bf),
            pltpu.VMEM((7, R1, WF), bf),
            pltpu.VMEM((7, 4, WR - R1, WF), bf),
            pltpu.VMEM((7, 4, WR - R1, WF), bf),
            pltpu.VMEM((3, WR - R1, WF), bf),
            pltpu.VMEM((3, WR - R1, WF), bf),
            pltpu.SemaphoreType.DMA((SEMS,)),
            pltpu.SemaphoreType.DMA((SEMS,)),
            pltpu.SemaphoreType.DMA((9,)),
        ],
        compiler_params=pltpu.CompilerParams(vmem_limit_bytes=62 << 20, collective_id=0, has_side_effects=True),
        name="block",
    )(h, gain, wq, wk, wv, g, docs, fine, coarse)
    return pl.pallas_call(
        finish_kernel,
        out_shape=(jax.ShapeDtypeStruct((SEQ, DH), bf),) + tuple(jax.ShapeDtypeStruct(s, f32) for s in ((WF, DH), (32, WF), (32, WF))),
        in_specs=[vmem] * 2,
        out_specs=(vmem,) * 4,
        name="finish",
    )(att, grad)


def local(hidden_states, norm_gain, w_query, w_key, w_value, out_grad, short_docs):
    fine, coarse = (jnp.asarray(t) for t in rope_tables())
    att, gq, gk, gv = block(hidden_states.reshape(TB, D), norm_gain.reshape(1, D), w_query, w_key.T, w_value.T,
                            out_grad.reshape(SEQ, DH), short_docs, fine, coarse)
    return att.reshape(1, 1, SEQ, DH), gq, gk.T, gv.T


def solution(mesh):
    both = ("bucket", "fsdp")
    return jax.shard_map(
        local,
        mesh=mesh,
        in_specs=(P("bucket", "fsdp", "sp", None), P(), P(both, "sp"), P(both, "sp"), P(both, "sp"),
                  P("bucket", "fsdp", None, "sp"), P("fsdp", None)),
        out_specs=(P("bucket", "fsdp", None, "sp"), P(both, "sp"), P(both, "sp"), P(both, "sp")),
        check_vma=False,
    )
```
